32 devices in a mesh: dp: 8 (over z, y), tensor: 4 (over x, core).
Axes of the slice: x: 2, y: 2, z: 4, core: 2. Of those that a mesh axis runs over, the one named last changes fastest.
Arguments:
- layer_input: bfloat16 [16, 1024, 768], P('dp', 'tensor'), may hold values from -6 to 6
- cotangent: bfloat16 [16, 1024, 768], P('dp', 'tensor'), may hold values from -6 to 6
- segment_ids: int32 [16, 1024], P('dp'), may hold values from 0 to 15, never falling along the last dimension, each value on 1 to 512 neighbouring positions
- query_weight: bfloat16 [768, 768], P('dp', 'tensor'), may hold values from -0.21875 to 0.21875
- key_weight: bfloat16 [768, 768], P('dp', 'tensor'), may hold values from -0.21875 to 0.21875
- value_weight: bfloat16 [768, 768], P('dp', 'tensor'), may hold values from -0.21875 to 0.21875
- output_weight: bfloat16 [768, 768], P('tensor', 'dp'), may hold values from -0.875 to 0.875
- gate_weight: bfloat16 [768, 3072], P('dp', 'tensor'), may hold values from -0.21875 to 0.21875
- up_weight: bfloat16 [768, 3072], P('dp', 'tensor'), may hold values from -0.21875 to 0.21875
- down_weight: bfloat16 [3072, 768], P('tensor', 'dp'), may hold values from -0.109375 to 0.109375
- first_gain: float32 [768], replicated, may hold values from 0.5 to 1.5
- first_bias: float32 [768], replicated, may hold values from -1 to 1
- second_gain: float32 [768], replicated, may hold values from 0.5 to 1.5
- second_bias: float32 [768], replicated, may hold values from -1 to 1
Outputs:
- output: bfloat16 [16, 1024, 768], P('dp', 'tensor')
- grad_input: bfloat16 [16, 1024, 768], P('dp', 'tensor')
- grad_query_weight: float32 [768, 768], P('dp', 'tensor')
- grad_key_weight: float32 [768, 768], P('dp', 'tensor')
- grad_value_weight: float32 [768, 768], P('dp', 'tensor')
- grad_output_weight: float32 [768, 768], P('tensor', 'dp')
- grad_gate_weight: float32 [768, 3072], P('dp', 'tensor')
- grad_up_weight: float32 [768, 3072], P('dp', 'tensor')
- grad_down_weight: float32 [3072, 768], P('tensor', 'dp')
- grad_first_gain: float32 [768], replicated
- grad_first_bias: float32 [768], replicated
- grad_second_gain: float32 [768], replicated
- grad_second_bias: float32 [768], replicated
The draws below stay inside these ranges and needn't reach their ends.
Inputs may be any that keep to these rules, and one draw needn't show every extreme that they name: `segment_ids`: ids never fall along a packed row and attention only joins tokens of equal id within one row; a document has 1 to 512 tokens, and some document has exactly that many.
All inputs are finite; a program needn't handle non-finite values.
Results may differ from the reference program's by a relative error of at most 0.023.
Values may be sent and summed in bfloat16 or wider, within the bound.
A program may use at most 128 MiB of HBM per device.

```python
import math
import jax
import jax.numpy as jnp
import numpy as np
from jax import lax

D = 768
HEADS = 12
HD = 64
FF = 3072
SEQ = 1024
ROWS = 16


def spiked(drawn, rng, source, target, parts, factor):
    owner, partner = [(jnp.arange(drawn.shape[axis_at]) // (drawn.shape[axis_at] // parts)).reshape([-1 if axis == axis_at else 1 for axis in range(drawn.ndim)]) for axis_at in (source, target)]
    chosen = jax.random.permutation(rng, parts)[partner]
    strong = (owner == chosen) | (owner == (partner + parts // 2) % parts)
    return jnp.where(strong, factor * drawn, drawn)


def levels(own_key, shape, shards, smallest, top_value):
    factor_of = 1.0
    for dim, parts in shards:
        heights = jax.random.uniform(jax.random.fold_in(jax.random.fold_in(own_key, 6), dim), (parts,), jnp.float32, smallest / len(shards), top_value / len(shards))
        factor_of = factor_of * jnp.repeat(jnp.exp(heights), shape[dim] // parts).reshape((-1,) + (1,) * (len(shape) - 1 - dim))
    return factor_of


def split_up(count, total, most, skew):
    portions = [(1 << 20) // math.isqrt(rank ** skew) + 1 for rank in range(2, count + 1)]
    rest, counts = total - most - (count - 1), [1] * (count - 1)
    while rest > 0:
        movable = [i for i in range(count - 1) if counts[i] < most]
        mass, budget = sum([portions[i] for i in movable]), rest
        for i in movable:
            addition = min(most - counts[i], max(1, budget * portions[i] // mass), rest)
            counts[i] = counts[i] + addition
            rest = rest - addition
    return np.array([most] + counts)


def ragged_sizes(stream_key, count, total, bound, lean):
    if count == 2:
        one = jax.random.randint(stream_key, (), max(1, total - bound), min(bound, total - 1) + 1)
        return jnp.stack([one, total - one])
    sizes = jnp.asarray(split_up(count, total, bound, lean), jnp.int32)
    couples = (count - 1) // 2
    donor, taker = sizes[1:1 + 2 * couples:2], sizes[2:2 + 2 * couples:2]
    margin = jnp.minimum(donor - 1, bound - taker)
    shifted = jax.random.randint(jax.random.fold_in(stream_key, 1), (couples,), 0, 1 << 20) % (margin + 1)
    sizes = sizes.at[1:1 + 2 * couples:2].set(donor - shifted).at[2:2 + 2 * couples:2].set(taker + shifted)
    return sizes[jax.random.permutation(jax.random.fold_in(stream_key, 2), count)]


def bell_draw(rng, extent, deviation, reach, split=(), kind=jnp.bfloat16):
    values = jax.random.normal(rng, extent, jnp.float32) * deviation
    if len(split) > 0:
        values = levels(rng, extent, split, -0.22, 0.18) * values
    return jnp.clip(values, min=-reach, max=reach).astype(kind)


def heavy_noise(key, shape, deviation, most, cuts, heavy, kind=jnp.bfloat16):
    drawn = deviation * jax.random.normal(key, shape, jnp.float32)
    if cuts:
        drawn = drawn * levels(key, shape, cuts, -0.22, 0.18)
    return jnp.clip(spiked(drawn, jax.random.fold_in(key, 3), *heavy), -most, most).astype(kind)


def setup_inputs(seed: int = 0) -> dict:
    seeds = jax.random.split(jax.random.key(seed), 15)
    layer_input = heavy_noise(seeds[0], (ROWS, SEQ, D), 1.0, 6.0, ((0, 8), (1, 4)), (0, 2, 8, 2.0))
    cotangent = heavy_noise(seeds[1], (ROWS, SEQ, D), 1.0, 6.0, ((0, 8), (1, 4)), (0, 2, 8, 2.0))
    segment_ids = jax.vmap(lambda own: jnp.searchsorted(jnp.cumsum(ragged_sizes(own, max(4, SEQ // 64), SEQ, SEQ // 2, 2)), jnp.arange(SEQ), side="right"))(jax.random.split(seeds[2], ROWS)).reshape((ROWS, SEQ)).astype(jnp.int32)
    query_weight = bell_draw(seeds[3], (D, D), D ** -0.5, 0.21875, ((0, 8), (1, 4)))
    key_weight = bell_draw(seeds[4], (D, D), D ** -0.5, 0.21875, ((0, 8), (1, 4)))
    value_weight = bell_draw(seeds[5], (D, D), D ** -0.5, 0.21875, ((0, 8), (1, 4)))
    output_weight = bell_draw(seeds[6], (D, D), (D // 16) ** -0.5, 0.875, ((0, 4), (1, 8)))
    gate_weight = bell_draw(seeds[7], (D, FF), D ** -0.5, 0.21875, ((0, 8), (1, 4)))
    up_weight = bell_draw(seeds[8], (D, FF), D ** -0.5, 0.21875, ((0, 8), (1, 4)))
    down_weight = bell_draw(seeds[9], (FF, D), FF ** -0.5, 0.109375, ((0, 4), (1, 8)))
    first_gain = jnp.clip(1.0 + 0.1 * jax.random.normal(seeds[10], (D,), jnp.float32), 0.5, 1.5)
    first_bias = bell_draw(seeds[11], (D,), 0.2, 1.0, (), jnp.float32)
    second_gain = jnp.clip(1.0 + 0.1 * jax.random.normal(seeds[12], (D,), jnp.float32), 0.5, 1.5)
    second_bias = bell_draw(seeds[13], (D,), 0.2, 1.0, (), jnp.float32)
    return {"layer_input": layer_input, "cotangent": cotangent, "segment_ids": segment_ids, "query_weight": query_weight, "key_weight": key_weight, "value_weight": value_weight, "output_weight": output_weight, "gate_weight": gate_weight, "up_weight": up_weight, "down_weight": down_weight, "first_gain": first_gain, "first_bias": first_bias, "second_gain": second_gain, "second_bias": second_bias}


exact_mode = lax.Precision.HIGHEST
eps_norm = 1e-06
rope_base = 1000.0
mask_fill = -1e+30

@jax.custom_vjp
def low(v):
    return lax.optimization_barrier(v.astype(jnp.bfloat16)).astype(jnp.float32)

@jax.custom_vjp
def low_back(v):
    return v

def low_keep(v):
    return (low(v), None)

def low_pass(kept, grad):
    return (grad,)

def back_keep(v):
    return (v, None)

def back_low(kept, grad):
    return (low(grad),)
low.defvjp(low_keep, low_pass)
low_back.defvjp(back_keep, back_low)

def layer_norm(field_rows, gain_vec, bias_vec):
    row_mean = lax.optimization_barrier(jnp.mean(field_rows, axis=-1, keepdims=True))
    centred = field_rows - row_mean
    variance = lax.optimization_barrier(jnp.mean(centred * centred, axis=-1, keepdims=True))
    return centred * lax.rsqrt(variance + eps_norm) * gain_vec + bias_vec

def rotary_tables(length, head_dim):
    half_dim = head_dim // 2
    frequency = rope_base ** (-(2.0 * jnp.arange(half_dim, dtype=jnp.float32)) / head_dim)
    angles = jnp.arange(length, dtype=jnp.float32)[:, None] * frequency[None, :]
    return (jnp.cos(angles), jnp.sin(angles))

def rotate(heads_data, cos_table, sine_table):
    half_dim = heads_data.shape[-1] // 2
    first_half = heads_data[..., :half_dim]
    second_half = heads_data[..., half_dim:]
    cos_part = cos_table[:, None, :]
    sine_part = sine_table[:, None, :]
    return jnp.concatenate([first_half * cos_part - second_half * sine_part, second_half * cos_part + first_half * sine_part], axis=-1)

def matmul(left, right):
    return jnp.dot(left, right, precision=exact_mode)

def attend_block(query_block, segment_block, key_rows, value_rows, segment_row):
    scores = jnp.einsum('qhd,khd->hqk', query_block, key_rows, precision=exact_mode) * (1.0 / math.sqrt(HD))
    scores = low_back(scores)
    allowed = segment_block[:, None] == segment_row[None, :]
    scores = jnp.where(allowed[None, :, :], scores, mask_fill)
    probabilities = low(jax.nn.softmax(scores, axis=-1))
    return jnp.einsum('hqk,khd->qhd', probabilities, value_rows, precision=exact_mode)

def layer_row(weights, row_input, segment_row):
    query_weight, key_weight, value_weight, output_weight, gate_weight, up_weight, down_weight, first_gain, first_bias, second_gain, second_bias = weights
    length = row_input.shape[0]
    block_rows = min(512, length)
    cos_table, sine_table = rotary_tables(length, HD)
    query_pre = low_back(matmul(row_input, query_weight)).reshape(length, HEADS, HD)
    key_pre = low_back(matmul(row_input, key_weight)).reshape(length, HEADS, HD)
    value_rows = low(low_back(matmul(row_input, value_weight))).reshape(length, HEADS, HD)
    query_rows = low(rotate(query_pre, cos_table, sine_table))
    key_rows = low(rotate(key_pre, cos_table, sine_table))

    def attend_one(block_inputs):
        return attend_block(block_inputs[0], block_inputs[1], key_rows, value_rows, segment_row)
    mixed_rows = lax.map(jax.checkpoint(attend_one), (query_rows.reshape(length // block_rows, block_rows, HEADS, HD), segment_row.reshape(length // block_rows, block_rows)))
    attended = low(low_back(mixed_rows.reshape(length, HEADS * HD)))
    attention_branch = low_back(matmul(attended, output_weight))
    hidden_state = layer_norm(row_input + attention_branch, first_gain, first_bias)
    hidden_low = low(hidden_state)
    gate_pre = low_back(matmul(hidden_low, gate_weight))
    up_pre = low_back(matmul(hidden_low, up_weight))
    activated = low(jax.nn.silu(gate_pre) * up_pre)
    feed_branch = low_back(matmul(activated, down_weight))
    return layer_norm(hidden_state + feed_branch, second_gain, second_bias)

def reference(layer_input, cotangent, segment_ids, query_weight, key_weight, value_weight, output_weight, gate_weight, up_weight, down_weight, first_gain, first_bias, second_gain, second_bias):
    weights = tuple((weight_part.astype(jnp.float32) for weight_part in (query_weight, key_weight, value_weight, output_weight, gate_weight, up_weight, down_weight, first_gain, first_bias, second_gain, second_bias)))
    inputs = layer_input.astype(jnp.float32)

    def forward(weight_set, input_rows):

        def one_row(row_inputs):
            return layer_row(weight_set, row_inputs[0], row_inputs[1])
        return lax.map(jax.checkpoint(one_row), (input_rows, segment_ids))
    result, pullback = jax.vjp(forward, weights, inputs)
    grad_weights, grad_rows = pullback(cotangent.astype(jnp.float32))
    grad_query, grad_key, grad_value, grad_output, grad_gate, grad_up, grad_down, grad_gain_one, grad_bias_one, grad_gain_two, grad_bias_two = grad_weights
    return (result.astype(jnp.bfloat16), grad_rows.astype(jnp.bfloat16), grad_query, grad_key, grad_value, grad_output, grad_gate, grad_up, grad_down, grad_gain_one, grad_bias_one, grad_gain_two, grad_bias_two)
```

```python
import functools

import jax
import jax.numpy as jnp
import numpy as np
from jax import lax
from jax.experimental import pallas as pl
from jax.experimental.pallas import tpu as pltpu
from jax.sharding import PartitionSpec as P

HD = 64


eps_norm = 1e-06
rope_base = 1000.0
mask_fill = -1e30


def layer_norm(field_rows, gain_vec, bias_vec):
    row_mean = jnp.mean(field_rows, axis=-1, keepdims=True)
    centred = field_rows - row_mean
    variance = jnp.mean(centred * centred, axis=-1, keepdims=True)
    return centred * lax.rsqrt(variance + eps_norm) * gain_vec + bias_vec


def rotary_tables(length, head_dim):
    half_dim = head_dim // 2
    frequency = rope_base ** (-(2.0 * jnp.arange(half_dim, dtype=jnp.float32)) / head_dim)
    angles = jnp.arange(length, dtype=jnp.float32)[:, None] * frequency[None, :]
    return (jnp.cos(angles), jnp.sin(angles))


def rotate(heads_data, cos_table, sine_table):
    half_dim = heads_data.shape[-1] // 2
    first_half = heads_data[..., :half_dim]
    second_half = heads_data[..., half_dim:]
    cos_part = cos_table[:, None, :]
    sine_part = sine_table[:, None, :]
    return jnp.concatenate(
        [
            first_half * cos_part - second_half * sine_part,
            second_half * cos_part + first_half * sine_part,
        ],
        axis=-1,
    )


def swiglu(gate_pre, up_pre):
    return jax.nn.silu(gate_pre) * up_pre


def contract_rows(left, right):
    return lax.dot_general(
        left, right, (((0,), (0,)), ((), ())), preferred_element_type=jnp.float32
    )


def times_transpose(left, right):
    return lax.dot_general(
        left, right, (((1,), (1,)), ((), ())), preferred_element_type=jnp.float32
    )


def per_device(
    layer_input,
    cotangent,
    segment_ids,
    query_weight,
    key_weight,
    value_weight,
    output_weight,
    gate_weight,
    up_weight,
    down_weight,
    first_gain,
    first_bias,
    second_gain,
    second_bias,
):
    model_width = layer_input.shape[2]
    length = segment_ids.shape[1]
    block_rows = min(512, length)
    block_count = length // block_rows
    local_heads = query_weight.shape[1] // HD
    local_width = local_heads * HD
    score_scale = HD ** (-0.5)
    cos_table, sine_table = rotary_tables(length, HD)

    def fetch_weights():
        row_parts = (
            lax.all_gather(query_weight, "dp", axis=0, tiled=True),
            lax.all_gather(key_weight, "dp", axis=0, tiled=True),
            lax.all_gather(value_weight, "dp", axis=0, tiled=True),
            lax.all_gather(gate_weight, "dp", axis=0, tiled=True),
            lax.all_gather(up_weight, "dp", axis=0, tiled=True),
        )
        col_parts = (
            lax.all_gather(output_weight, "dp", axis=1, tiled=True),
            lax.all_gather(down_weight, "dp", axis=1, tiled=True),
        )
        return tuple(row_parts) + tuple(col_parts)

    def micro_step(weights, row_input, row_cotangent, segment_row):
        query_full, key_full, value_full, gate_full, up_full, output_full, down_full = weights
        full_input = lax.all_gather(row_input, "tensor", axis=0, tiled=True)
        query_pre = jnp.dot(full_input, query_full, preferred_element_type=jnp.float32).reshape(
            length, local_heads, HD
        )
        key_pre = jnp.dot(full_input, key_full, preferred_element_type=jnp.float32).reshape(
            length, local_heads, HD
        )
        value_rows = (
            jnp.dot(full_input, value_full, preferred_element_type=jnp.float32)
            .astype(jnp.bfloat16)
            .reshape(length, local_heads, HD)
        )
        query_rows = rotate(query_pre, cos_table, sine_table).astype(jnp.bfloat16)
        key_rows = rotate(key_pre, cos_table, sine_table).astype(jnp.bfloat16)
        query_blocks = query_rows.reshape(block_count, block_rows, local_heads, HD)
        segment_blocks = segment_row.reshape(block_count, block_rows)

        def block_scores(query_block, segment_block):
            scores = (
                jnp.einsum(
                    "qhd,khd->hqk", query_block, key_rows, preferred_element_type=jnp.float32
                )
                * score_scale
            )
            allowed = segment_block[:, None] == segment_row[None, :]
            return jnp.where(allowed[None, :, :], scores, mask_fill)

        def attend_forward(block_inputs):
            scores = block_scores(block_inputs[0], block_inputs[1])
            row_max = jnp.max(scores, axis=-1, keepdims=True)
            exponent_terms = jnp.exp(scores - row_max)
            row_total = jnp.sum(exponent_terms, axis=-1, keepdims=True)
            probabilities = (exponent_terms / row_total).astype(jnp.bfloat16)
            mixed_rows = jnp.einsum(
                "hqk,khd->qhd", probabilities, value_rows, preferred_element_type=jnp.float32
            )
            return (mixed_rows, (row_max + jnp.log(row_total))[..., 0])

        mixed_blocks, log_totals = lax.map(attend_forward, (query_blocks, segment_blocks))
        attended = mixed_blocks.reshape(length, local_width).astype(jnp.bfloat16)
        attention_branch = lax.psum_scatter(
            jnp.dot(attended, output_full, preferred_element_type=jnp.float32).astype(jnp.bfloat16),
            "tensor",
            scatter_dimension=0,
            tiled=True,
        ).astype(jnp.float32)
        first_sum = row_input.astype(jnp.float32) + attention_branch
        hidden_state, first_back = jax.vjp(layer_norm, first_sum, first_gain, first_bias)
        full_hidden = lax.all_gather(
            hidden_state.astype(jnp.bfloat16), "tensor", axis=0, tiled=True
        )
        gate_pre = jnp.dot(full_hidden, gate_full, preferred_element_type=jnp.float32)
        up_pre = jnp.dot(full_hidden, up_full, preferred_element_type=jnp.float32)
        activated_exact, swiglu_back = jax.vjp(swiglu, gate_pre, up_pre)
        activated = activated_exact.astype(jnp.bfloat16)
        feed_branch = lax.psum_scatter(
            jnp.dot(activated, down_full, preferred_element_type=jnp.float32).astype(jnp.bfloat16),
            "tensor",
            scatter_dimension=0,
            tiled=True,
        ).astype(jnp.float32)
        layer_output, second_back = jax.vjp(
            layer_norm, hidden_state + feed_branch, second_gain, second_bias
        )
        grad_second_sum, grad_second_gain, grad_second_bias = second_back(
            row_cotangent.astype(jnp.float32)
        )
        grad_second_full = lax.all_gather(
            grad_second_sum.astype(jnp.bfloat16), "tensor", axis=0, tiled=True
        )
        grad_activated = times_transpose(grad_second_full, down_full)
        grad_down = contract_rows(activated, grad_second_full)
        grad_gate_pre, grad_up_pre = swiglu_back(grad_activated)
        gate_low = grad_gate_pre.astype(jnp.bfloat16)
        up_low = grad_up_pre.astype(jnp.bfloat16)
        grad_hidden = grad_second_sum + lax.psum_scatter(
            (times_transpose(gate_low, gate_full) + times_transpose(up_low, up_full)).astype(
                jnp.bfloat16
            ),
            "tensor",
            scatter_dimension=0,
            tiled=True,
        ).astype(jnp.float32)
        grad_gate = contract_rows(full_hidden, gate_low)
        grad_up = contract_rows(full_hidden, up_low)
        grad_first_sum, grad_first_gain, grad_first_bias = first_back(grad_hidden)
        grad_first_full = lax.all_gather(
            grad_first_sum.astype(jnp.bfloat16), "tensor", axis=0, tiled=True
        )
        grad_attended = (
            times_transpose(grad_first_full, output_full)
            .astype(jnp.bfloat16)
            .reshape(block_count, block_rows, local_heads, HD)
        )
        grad_output = contract_rows(attended, grad_first_full)

        def attend_backward(sums_carry, block_inputs):
            key_sum, value_sum = sums_carry
            query_block, segment_block, log_block, grad_block = block_inputs
            scores = block_scores(query_block, segment_block)
            probabilities = jnp.exp(scores - log_block[..., None])
            grad_softmax = jnp.einsum(
                "qhd,khd->hqk", grad_block, value_rows, preferred_element_type=jnp.float32
            )
            value_sum = value_sum + jnp.einsum(
                "hqk,qhd->khd",
                probabilities.astype(jnp.bfloat16),
                grad_block,
                preferred_element_type=jnp.float32,
            )
            row_inner = jnp.sum(probabilities * grad_softmax, axis=-1, keepdims=True)
            grad_scores = (probabilities * (grad_softmax - row_inner)).astype(jnp.bfloat16)
            grad_query_block = (
                jnp.einsum(
                    "hqk,khd->qhd", grad_scores, key_rows, preferred_element_type=jnp.float32
                )
                * score_scale
            )
            key_sum = (
                key_sum
                + jnp.einsum(
                    "hqk,qhd->khd", grad_scores, query_block, preferred_element_type=jnp.float32
                )
                * score_scale
            )
            return ((key_sum, value_sum), grad_query_block)

        zero_heads = jnp.zeros((length, local_heads, HD), jnp.float32)
        (grad_key_rot, grad_value_rows), grad_query_blocks = lax.scan(
            attend_backward,
            (zero_heads, zero_heads),
            (query_blocks, segment_blocks, log_totals, grad_attended),
        )
        grad_query_low = (
            rotate(grad_query_blocks.reshape(length, local_heads, HD), cos_table, -sine_table)
            .astype(jnp.bfloat16)
            .reshape(length, local_width)
        )
        grad_key_low = (
            rotate(grad_key_rot, cos_table, -sine_table)
            .astype(jnp.bfloat16)
            .reshape(length, local_width)
        )
        grad_value_low = grad_value_rows.astype(jnp.bfloat16).reshape(length, local_width)
        query_part = times_transpose(grad_query_low, query_full)
        key_part = times_transpose(grad_key_low, key_full)
        value_part = times_transpose(grad_value_low, value_full)
        grad_input = grad_first_sum + lax.psum_scatter(
            (query_part + key_part + value_part).astype(jnp.bfloat16),
            "tensor",
            scatter_dimension=0,
            tiled=True,
        ).astype(jnp.float32)
        row_grads = (
            contract_rows(full_input, grad_query_low),
            contract_rows(full_input, grad_key_low),
            contract_rows(full_input, grad_value_low),
            grad_gate,
            grad_up,
        )
        col_grads = (grad_output, grad_down)
        norm_parts = (grad_first_gain, grad_first_bias, grad_second_gain, grad_second_bias)
        return (
            layer_output.astype(jnp.bfloat16),
            grad_input.astype(jnp.bfloat16),
            (row_grads, col_grads, norm_parts),
        )

    norm_zero = tuple(
        (
            jnp.zeros(gain_like.shape, jnp.float32)
            for gain_like in (first_gain, first_bias, second_gain, second_bias)
        )
    )
    row_zero = tuple(
        (
            jnp.zeros((model_width, weight_part.shape[1]), jnp.float32)
            for weight_part in (query_weight, key_weight, value_weight, gate_weight, up_weight)
        )
    )
    col_zero = (
        jnp.zeros((output_weight.shape[0], model_width), jnp.float32),
        jnp.zeros((down_weight.shape[0], model_width), jnp.float32),
    )

    def scan_step(totals, batch_rows):
        weights = fetch_weights()
        layer_output, grad_input, grad_terms = micro_step(
            weights, batch_rows[0], batch_rows[1], batch_rows[2]
        )
        return (jax.tree.map(jnp.add, totals, grad_terms), (layer_output, grad_input))

    totals, (outputs, grad_inputs) = lax.scan(
        scan_step, (row_zero, col_zero, norm_zero), (layer_input, cotangent, segment_ids)
    )
    row_grads, col_grads, norm_parts = totals
    row_done = lax.psum_scatter(row_grads, "dp", scatter_dimension=0, tiled=True)
    col_done = (
        lax.psum_scatter(col_grads[0], "dp", scatter_dimension=1, tiled=True),
        lax.psum_scatter(col_grads[1], "dp", scatter_dimension=1, tiled=True),
    )
    norm_done = lax.psum(norm_parts, ("dp", "tensor"))
    totals = (tuple(row_done), tuple(col_done), tuple(norm_done))
    row_done, col_done, norm_done = totals
    return (
        outputs,
        grad_inputs,
        row_done[0],
        row_done[1],
        row_done[2],
        col_done[0],
        row_done[3],
        row_done[4],
        col_done[1],
        norm_done[0],
        norm_done[1],
        norm_done[2],
        norm_done[3],
    )


F32 = jnp.float32
BF16 = jnp.bfloat16
NY = 2
LANES = 128
MESH = pl.DeviceIdType.MESH


def mm(left, right):
    return lax.dot_general(left, right, (((1,), (0,)), ((), ())), preferred_element_type=F32)


def mt(left, right):
    return lax.dot_general(left, right, (((1,), (1,)), ((), ())), preferred_element_type=F32)


def lane_tables(length):
    half = HD // 2
    steps = np.arange(half, dtype=np.float32)
    frequency = np.float32(rope_base) ** (-(np.float32(2.0) * steps) / np.float32(HD))
    angles = np.arange(length, dtype=np.float32)[:, None] * frequency[None, :]
    angles = angles.astype(np.float32)
    cos, sin = np.cos(angles).astype(np.float32), np.sin(angles).astype(np.float32)
    cos_lane = np.concatenate([cos] * 4, axis=1)
    sin_lane = np.concatenate([-sin, sin, -sin, sin], axis=1)
    return cos_lane, sin_lane, np.ascontiguousarray(cos.T), np.ascontiguousarray(sin.T)


def norm_of(v):
    mu = jnp.mean(v, axis=-1, keepdims=True)
    cen = v - mu
    rstd = lax.rsqrt(jnp.mean(cen * cen, axis=-1, keepdims=True) + eps_norm)
    return cen * rstd, rstd


def grad_of_norm(dn, n, rstd):
    m0 = jnp.mean(dn, axis=-1, keepdims=True)
    m1 = jnp.mean(dn * n, axis=-1, keepdims=True)
    return (dn - m0 - n * m1) * rstd


def colsum(v):
    return jnp.sum(v, axis=0, keepdims=True)


def layer_kernel(
    nz,
    xin,
    cot,
    seg,
    wpk,
    g1_ref,
    b1_ref,
    g2_ref,
    b2_ref,
    cosl_h,
    sinl_h,
    cosf_h,
    sinf_h,
    out_h,
    gin_h,
    gw_h,
    ng_out,
    W,
    G,
    S1X,
    S1Y,
    S2X,
    S2Y,
    ZR,
    X,
    XT,
    TT,
    DT,
    CT,
    SC,
    COSL,
    SINL,
    COSF,
    SINF,
    PK,
    QZ,
    KT,
    VT,
    LSE,
    DEL,
    ATT,
    ATTT,
    N1,
    R1,
    F4,
    GP,
    UP,
    RR,
    DZ,
    CXS,
    CXR,
    ACC,
    OB,
    DKA,
    DVA,
    NG,
    NR,
    NS,
    NZR,
    loc,
    ssem,
    rsem,
):
    quarter, width = X.shape[1], X.shape[2]
    length = 4 * quarter
    rows = W.shape[4]
    dp = lax.axis_index("dp")
    tt = lax.axis_index("tensor")
    c = lax.rem(tt, 2)
    xi = lax.div(tt, 2)
    z = lax.div(dp, NY)
    y = lax.rem(dp, NY)
    oy = 1 - y
    t_x = lax.rem(tt + 2, 4)
    dev_x = (dp, t_x)
    dev_c = (dp, tt + 1 - 2 * c)
    dev_y = (dp + 1 - 2 * y, tt)
    zs = [lax.rem(z + j, nz) for j in range(nz)]
    zfrom = [lax.rem(z + nz - j, nz) for j in range(nz)]
    dev_z = [(zs[j] * NY + y, tt) for j in range(nz)]
    hz = nz // 2
    count = [0]
    lcount = [0]
    sends = {}

    def rc(src, dst, dev):
        i = count[0]
        count[0] += 1
        copy = pltpu.make_async_remote_copy(
            src_ref=src,
            dst_ref=dst,
            send_sem=ssem.at[i],
            recv_sem=rsem.at[i],
            device_id=dev,
            device_id_type=MESH,
        )
        copy.start()
        sends[id(copy)] = copy
        return copy

    def sent(copy):
        copy.wait_send()
        del sends[id(copy)]

    def lc(src, dst):
        i = lcount[0]
        lcount[0] += 1
        copy = pltpu.make_async_copy(src, dst, loc.at[i])
        copy.start()
        return copy

    l_w = lc(wpk, W.at[:, 0, z, y])
    l_x = lc(xin.at[xi], X.at[tt])
    l_ct = lc(cot.at[xi], CT.at[xi])
    l_tab = [lc(cosl_h, COSL), lc(sinl_h, SINL), lc(cosf_h, COSF), lc(sinf_h, SINF)]

    barrier = pltpu.get_barrier_semaphore()
    peers = [dev_x, dev_c, dev_y] + dev_z[1:]
    for dev in peers:
        pl.semaphore_signal(barrier, inc=1, device_id=dev, device_id_type=MESH)
    pl.semaphore_wait(barrier, len(peers))

    ag = {}

    def e1(k):
        own = wpk.at[k]
        ag[k, "z"] = [rc(own, W.at[k, 0, z, y], dev_z[j]) for j in range(1, nz)]
        ag[k, "x"] = [rc(own, W.at[k, 1, z, y], dev_x)]
        ag[k, "y"] = [rc(own, W.at[k, 0, z, y], dev_y)]

    def e2(k):
        for j in range(1, nz):
            ag[k, "z"][j - 1].wait_recv()
            part = W.at[k, 0, zfrom[j], y]
            ag[k, "x"].append(rc(part, W.at[k, 1, zfrom[j], y], dev_x))
            ag[k, "y"].append(rc(part, part, dev_y))

    def e3(k):
        ag[k, "d"] = []
        for j in range(nz):
            ag[k, "x"][j].wait_recv()
            if j < hz:
                part = W.at[k, 1, zfrom[j], y]
                ag[k, "d"].append(rc(part, part, dev_y))
            ag[k, "y"][j].wait_recv()
            if j >= hz:
                ag[k, "d"].append(rc(W.at[k, 0, zfrom[j], oy], W.at[k, 1, zfrom[j], oy], dev_x))

    def e4(k):
        for copy in ag[k, "d"]:
            copy.wait_recv()

    def e_sent(k):
        for copy in ag[k, "z"] + ag[k, "x"] + ag[k, "y"] + ag[k, "d"]:
            sent(copy)

    x_far = rc(xin.at[1 - xi], X.at[tt], dev_x)
    x_core = rc(xin.at[xi], X.at[tt], dev_c)
    e1(0)

    SC[...] = jnp.broadcast_to(seg[pl.ds(xi, 1), :].astype(F32), (LANES, length)).T
    NG[...] = jnp.zeros_like(NG)
    lane = lax.broadcasted_iota(jnp.int32, (1, LANES), 1)
    low_half = lane < HD
    swap_low = lax.rem(lane, HD) < (HD // 2)

    def swap(v):
        return jnp.where(swap_low, pltpu.roll(v, LANES - HD // 2, 1), pltpu.roll(v, HD // 2, 1))

    def at_quarter(i):
        return pl.ds(pl.multiple_of(i * quarter, quarter), quarter)

    def wmat(k, s, lo=0, hi=None):
        hi = width if hi is None else hi
        return W[k, s, :, :, :, lo:hi].reshape(width, hi - lo)

    def turn_rows(src, dst):
        def step(i, _):
            dst[:, at_quarter(i)] = src[i].T
            return 0

        lax.fori_loop(0, 4, step, 0)

    x_far.wait_recv()
    x_core2 = rc(X.at[t_x], X.at[t_x], dev_c)
    x_core.wait_recv()
    l_x.wait()
    l_w.wait()
    l_ct.wait()
    for copy in l_tab:
        copy.wait()
    x_core2.wait_recv()
    turn_rows(X, XT)
    e2(0)
    e1(1)
    ct_far = rc(cot.at[1 - xi], CT.at[xi], dev_x)
    e3(0)
    e4(0)

    def project(s):
        def step(i, _):
            at = at_quarter(i)
            y5 = mm(X[i], wmat(0, s, 0, 5 * LANES))
            cos, sin = COSL[at, :], SINL[at, :]
            turned = []
            for b in range(5):
                v = y5[:, b * LANES : (b + 1) * LANES]
                if b in (0, 1, 3):
                    v = v * cos + swap(v) * sin
                v = v.astype(BF16)
                PK[s, b, at, :] = v
                turned.append(v.T)
            zero = jnp.zeros((HD, quarter), BF16)
            q0 = turned[0] * BF16(0.125)
            q2 = turned[3] * BF16(0.125)
            QZ[3 * s, :HD, at] = q0[:HD]
            QZ[3 * s, HD:, at] = zero
            QZ[3 * s + 1, :HD, at] = zero
            QZ[3 * s + 1, HD:, at] = q0[HD:]
            QZ[3 * s + 2, :HD, at] = zero
            QZ[3 * s + 2, HD:, at] = q2[:HD]
            KT[3 * s, :, at] = turned[1][:HD]
            KT[3 * s + 1, :, at] = turned[1][HD:]
            KT[3 * s + 2, :, at] = turned[3][HD:]
            VT[3 * s, :, at] = turned[2][:HD]
            VT[3 * s + 1, :, at] = turned[2][HD:]
            VT[3 * s + 2, :, at] = turned[4][:HD]
            return 0

        lax.fori_loop(0, 4, step, 0)

    def scores_of(s, hh, h, at):
        st = mm(PK[s, 1 + 2 * lax.div(hh, 2)], QZ[h, :, at])
        key_seg = jnp.concatenate([SC[...]] * (quarter // LANES), axis=1)
        query_seg = seg[pl.ds(xi, 1), at].astype(F32)
        return jnp.where(key_seg == query_seg, st, mask_fill)

    def attend(s):
        def step(n, _):
            hh = lax.div(n, 4)
            h = 3 * s + hh
            at = at_quarter(lax.rem(n, 4))
            st = scores_of(s, hh, h, at)
            top = jnp.max(st, axis=0, keepdims=True)
            p = jnp.exp(st - top)
            total = jnp.sum(p, axis=0, keepdims=True)
            ot = mm(VT[h], p.astype(BF16)) * (1.0 / total)
            LSE[h, :, at] = top + jnp.log(total)
            ATTT[h, :, at] = ot.astype(BF16)
            return 0

        lax.fori_loop(0, 12, step, 0)

        def turn(i, _):
            at = at_quarter(i)
            pair = jnp.concatenate([ATTT[3 * s, :, at], ATTT[3 * s + 1, :, at]], axis=0)
            lone = jnp.concatenate([jnp.zeros((HD, quarter), BF16), ATTT[3 * s + 2, :, at]], axis=0)
            ATT[s, at, :LANES] = lone.T
            ATT[s, at, LANES:] = pair.T
            return 0

        lax.fori_loop(0, 4, turn, 0)

    project(0)
    project(1)
    e2(1)
    e1(2)
    attend(0)
    e3(1)
    e2(2)
    e1(3)
    attend(1)

    last_exchange = []

    def exchange(n, part):
        if last_exchange:
            sent(last_exchange.pop())

        def other(k, _):
            CXS[k] = part(1 - c + 2 * k).astype(BF16)
            return 0

        lax.fori_loop(0, 2, other, 0)
        copy = rc(CXS, CXR.at[n % 2], dev_c)
        last_exchange.append(copy)

        def own(k, _):
            ACC[k] = part(c + 2 * k)
            return 0

        lax.fori_loop(0, 2, own, 0)
        copy.wait_recv()

    def spread():
        return [rc(F4.at[c + 2 * k], F4.at[c + 2 * k], dev_c) for k in range(2)]

    def out_part(i):
        at = at_quarter(i)
        return mt(ATT[0, at, :], wmat(0, 0, 4 * LANES)) + mt(ATT[1, at, :], wmat(0, 1, 4 * LANES))

    exchange(0, out_part)
    tile = quarter // 2

    def over_tiles(fn):
        def step(n, _):
            k = lax.div(n, 2)
            fn(k, c + 2 * k, pl.ds(pl.multiple_of(lax.rem(n, 2) * tile, tile), tile))
            return 0

        lax.fori_loop(0, 4, step, 0)

    def first_norm(k, i, at):
        z1 = X[i, at, :].astype(F32) + ACC[k, at, :] + CXR[0, k, at, :].astype(F32)
        n1, rstd = norm_of(z1)
        N1[k, at, :] = n1
        R1[k, at, :] = jnp.broadcast_to(rstd, (tile, LANES))
        F4[i, at, :] = (n1 * g1_ref[...] + b1_ref[...]).astype(BF16)

    over_tiles(first_norm)
    h_copies = spread()
    e4(1)
    for copy in h_copies:
        copy.wait_recv()
    turn_rows(F4, TT)
    e3(2)
    e2(3)
    e4(2)

    def ff_up(n, _):
        s = lax.div(n, 4)
        i = lax.rem(n, 4)
        at = at_quarter(i)
        g = mm(F4[i], wmat(1, s))
        u = mm(F4[i], wmat(2, s))
        GP[s, at, :] = g.astype(BF16)
        UP[s, at, :] = u.astype(BF16)
        RR[s, at, :] = (g * jax.nn.sigmoid(g) * u).astype(BF16)
        return 0

    lax.fori_loop(0, 8, ff_up, 0)
    e3(3)
    e4(3)

    def down_part(i):
        at = at_quarter(i)
        return mt(RR[0, at, :], wmat(3, 0)) + mt(RR[1, at, :], wmat(3, 1))

    for copy in h_copies:
        sent(copy)
    exchange(1, down_part)
    ct_far.wait_recv()

    def second_norm(k, i, at):
        h = N1[k, at, :] * g1_ref[...] + b1_ref[...]
        z2 = h + ACC[k, at, :] + CXR[1, k, at, :].astype(F32)
        n2, rstd = norm_of(z2)
        OB[0, k, at, :] = (n2 * g2_ref[...] + b2_ref[...]).astype(BF16)
        dy = CT[k, at, :].astype(F32)
        NG[2:3, :] += colsum(dy * n2)
        NG[3:4, :] += colsum(dy)
        dz = grad_of_norm(dy * g2_ref[...], n2, rstd)
        DZ[k, at, :] = dz
        F4[i, at, :] = dz.astype(BF16)

    over_tiles(second_norm)
    d_copies = spread()
    o_far = rc(OB.at[0, 1 - xi], out_h.at[xi], dev_x)
    o_own = lc(OB.at[0, xi], out_h.at[xi])

    slots = {3: G, 1: W.at[3], 2: W.at[1], 0: W.at[2]}
    rs = {}
    lo_z, hi_z = pl.ds(0, hz), pl.ds(hz, nz - hz)

    def r1(k):
        g = slots[k]
        rs[k, "dx"] = rc(g.at[1, lo_z, oy], S1X.at[k], dev_x)
        rs[k, "dy"] = rc(g.at[1, hi_z, oy], S1Y.at[k], dev_y)
        rs[k, "x0"] = rc(g.at[1, lo_z, y], S2X.at[k, lo_z], dev_x)
        rs[k, "y0"] = rc(g.at[0, hi_z, oy], S2Y.at[k, hi_z], dev_y)

    def r2(k):
        g = slots[k]
        rs[k, "dx"].wait_recv()
        for j in range(hz):
            g[0, j, oy] = (g[0, j, oy].astype(F32) + S1X[k, j].astype(F32)).astype(BF16)
        rs[k, "y1"] = rc(g.at[0, lo_z, oy], S2Y.at[k, lo_z], dev_y)
        rs[k, "dy"].wait_recv()
        for j in range(hz, nz):
            g[1, j, y] = (g[1, j, y].astype(F32) + S1Y[k, j - hz].astype(F32)).astype(BF16)
        rs[k, "x1"] = rc(g.at[1, hi_z, y], S2X.at[k, hi_z], dev_x)

    def r3(k):
        g = slots[k]
        for name in ("x0", "y0", "y1", "x1"):
            rs[k, name].wait_recv()
        for j in range(nz):
            g[0, j, y] = (
                g[0, j, y].astype(F32) + S2X[k, j].astype(F32) + S2Y[k, j].astype(F32)
            ).astype(BF16)
        rs[k, "z"] = [rc(g.at[0, zs[j], y], ZR.at[k, z], dev_z[j]) for j in range(1, nz)]

    def r4(k):
        g = slots[k]
        for copy in rs[k, "z"]:
            copy.wait_recv()
        total = g[0, z, y].astype(F32)
        for j in range(1, nz):
            total = total + ZR[k, zfrom[j]].astype(F32)
        place = N1.at[k // 2, pl.ds((k % 2) * rows, rows)]
        place[...] = total
        rs[k, "out"] = lc(place, gw_h.at[k])

    def weight_grad(k, left, right):
        g = slots[k]
        block = NY * rows

        def step(n, _):
            s = lax.div(n, nz)
            j = lax.rem(n, nz)
            at = pl.ds(pl.multiple_of(j * block, block), block)
            g[s, j] = mm(left[at, :], right[s]).astype(BF16).reshape(NY, rows, width)
            return 0

        lax.fori_loop(0, 2 * nz, step, 0)

    for copy in d_copies:
        copy.wait_recv()
    turn_rows(F4, DT)
    weight_grad(3, DT, RR)
    r1(3)

    def ff_back(n, _):
        s = lax.div(n, 4)
        i = lax.rem(n, 4)
        at = at_quarter(i)
        dr = mm(F4[i], wmat(3, s))
        g = GP[s, at, :].astype(F32)
        u = UP[s, at, :].astype(F32)
        sg = jax.nn.sigmoid(g)
        GP[s, at, :] = (dr * u * sg * (1.0 + g * (1.0 - sg))).astype(BF16)
        UP[s, at, :] = (dr * g * sg).astype(BF16)
        return 0

    lax.fori_loop(0, 8, ff_back, 0)
    e_sent(3)
    weight_grad(1, TT, GP)
    r1(1)
    r2(3)

    def hidden_part(i):
        at = at_quarter(i)
        return (
            mt(GP[0, at, :], wmat(1, 0))
            + mt(UP[0, at, :], wmat(2, 0))
            + mt(GP[1, at, :], wmat(1, 1))
            + mt(UP[1, at, :], wmat(2, 1))
        )

    for copy in d_copies:
        sent(copy)
    exchange(2, hidden_part)

    def first_norm_back(k, i, at):
        dh = DZ[k, at, :] + ACC[k, at, :] + CXR[0, k, at, :].astype(F32)
        n1 = N1[k, at, :]
        NG[0:1, :] += colsum(dh * n1)
        NG[1:2, :] += colsum(dh)
        dz = grad_of_norm(dh * g1_ref[...], n1, R1[k, at, :1])
        DZ[k, at, :] = dz
        F4[i, at, :] = dz.astype(BF16)

    over_tiles(first_norm_back)
    b_copies = spread()
    n_core = rc(NG, NR.at[0], dev_c)
    e_sent(1)
    e_sent(2)
    weight_grad(2, TT, UP)
    r3(3)
    r1(2)
    r2(1)
    for copy in b_copies:
        copy.wait_recv()
    n_core.wait_recv()
    NS[0] = NG[...] + NR[0]
    n_x = rc(NS.at[0], NR.at[1], dev_x)
    turn_rows(F4, DT)

    def out_grad(n, _):
        s = lax.div(n, nz)
        j = lax.rem(n, nz)
        block = NY * rows
        at = pl.ds(pl.multiple_of(j * block, block), block)
        part = mm(DT[at, :], ATT[s]).astype(BF16)
        slots[0][s, j, :, :, 4 * LANES :] = part.reshape(NY, rows, 2 * LANES)
        return 0

    lax.fori_loop(0, 2 * nz, out_grad, 0)

    def head_lanes(h):
        return pl.ds(pl.multiple_of(h * LANES, LANES), LANES)

    def att_grad(i, _):
        at = at_quarter(i)
        for s in range(2):
            da = mm(F4[i], wmat(0, s, 4 * LANES))
            pair = da[:, LANES:]
            lone = pltpu.roll(da[:, :LANES], HD, 1)
            zero = jnp.zeros_like(pair)
            views = (
                jnp.where(low_half, pair, zero),
                jnp.where(low_half, zero, pair),
                jnp.where(low_half, lone, zero),
            )
            for hh in range(3):
                h = 3 * s + hh
                v = views[hh].astype(BF16)
                GP[0, at, h * LANES : (h + 1) * LANES] = v
                vt = v.T
                TT[h * LANES : (h + 1) * LANES, at] = vt
                part = vt[HD:] if hh == 1 else vt[:HD]
                DEL[h, :, at] = colsum(part.astype(F32) * ATTT[h, :, at].astype(F32))
        return 0

    lax.fori_loop(0, 4, att_grad, 0)
    n_x.wait_recv()
    NS[1] = NS[0] + NR[1]
    n_y = rc(NS.at[1], NR.at[2], dev_y)
    r2(2)
    r3(1)

    def attend_back(s):
        def head(hh, _):
            h = 3 * s + hh
            DKA[...] = jnp.zeros_like(DKA)
            DVA[...] = jnp.zeros_like(DVA)
            hl = head_lanes(h)

            def step(qb, _):
                at = at_quarter(qb)
                p = jnp.exp(scores_of(s, hh, h, at) - LSE[h, :, at])
                dpt = mm(PK[s, 2 + 2 * lax.div(hh, 2)], TT[hl, at])
                ds = (p * (dpt - DEL[h, :, at])).astype(BF16)
                DVA[...] += mm(p.astype(BF16), GP[0, at, hl])
                DKA[...] += mm(ds, PK[s, 3 * lax.div(hh, 2), at, :])
                dq = mm(KT[h], ds) * 0.125
                a, b = dq[: HD // 2], dq[HD // 2 :]
                cos, sin = COSF[:, at], SINF[:, at]
                VT[h, : HD // 2, at] = (a * cos + b * sin).astype(BF16)
                VT[h, HD // 2 :, at] = (b * cos - a * sin).astype(BF16)
                return 0

            lax.fori_loop(0, 4, step, 0)

            def finish(i, _):
                at = at_quarter(i)
                dk = DKA[at, :] * 0.125
                UP[0, at, hl] = (dk * COSL[at, :] - swap(dk) * SINL[at, :]).astype(BF16)
                GP[0, at, hl] = DVA[at, :].astype(BF16)
                return 0

            lax.fori_loop(0, 4, finish, 0)
            return 0

        lax.fori_loop(0, 3, head, 0)

        def gather(i, _):
            at = at_quarter(i)

            def part(ref, hh):
                h = 3 * s + hh
                return ref[0, at, h * LANES : (h + 1) * LANES].astype(F32)

            dq0 = jnp.concatenate([VT[3 * s, :, at], VT[3 * s + 1, :, at]], axis=0).T
            dq2 = jnp.concatenate([VT[3 * s + 2, :, at]] * 2, axis=0).T
            dk2 = pltpu.roll(part(UP, 2), HD, 1)
            dv2 = part(GP, 2)
            RR[s, at, 0:LANES] = dq0
            RR[s, at, LANES : 2 * LANES] = jnp.where(low_half, part(UP, 0), part(UP, 1)).astype(BF16)
            RR[s, at, 2 * LANES : 3 * LANES] = jnp.where(
                low_half, part(GP, 0), part(GP, 1)
            ).astype(BF16)
            RR[s, at, 3 * LANES : 4 * LANES] = jnp.where(low_half, dq2.astype(F32), dk2).astype(BF16)
            RR[s, at, 4 * LANES : 5 * LANES] = jnp.where(
                low_half, dv2, jnp.zeros_like(dv2)
            ).astype(BF16)
            return 0

        lax.fori_loop(0, 4, gather, 0)

    attend_back(0)
    r4(3)
    r3(2)
    n_y.wait_recv()
    NS[2] = NS[1] + NR[2]
    NZR[z] = NS[2]
    n_z = [rc(NS.at[2], NZR.at[z], dev_z[j]) for j in range(1, nz)]
    attend_back(1)

    def in_grad(n, _):
        s = lax.div(n, nz)
        j = lax.rem(n, nz)
        block = NY * rows
        at = pl.ds(pl.multiple_of(j * block, block), block)
        part = mm(XT[at, :], RR[s, :, : 5 * LANES])
        mixed = slots[0][s, j, :, :, 4 * LANES : 5 * LANES].reshape(block, LANES)
        mixed = (part[:, 4 * LANES :] + mixed.astype(F32)).astype(BF16)
        slots[0][s, j, :, :, : 4 * LANES] = (
            part[:, : 4 * LANES].astype(BF16).reshape(NY, rows, 4 * LANES)
        )
        slots[0][s, j, :, :, 4 * LANES : 5 * LANES] = mixed.reshape(NY, rows, LANES)
        return 0

    lax.fori_loop(0, 2 * nz, in_grad, 0)
    r1(0)
    r4(1)

    def input_part(i):
        at = at_quarter(i)
        return mt(RR[0, at, : 5 * LANES], wmat(0, 0, 0, 5 * LANES)) + mt(
            RR[1, at, : 5 * LANES], wmat(0, 1, 0, 5 * LANES)
        )

    exchange(3, input_part)

    def input_grad(k, i, at):
        g = DZ[k, at, :] + ACC[k, at, :] + CXR[1, k, at, :].astype(F32)
        OB[1, k, at, :] = g.astype(BF16)

    over_tiles(input_grad)
    i_far = rc(OB.at[1, 1 - xi], gin_h.at[xi], dev_x)
    i_own = lc(OB.at[1, xi], gin_h.at[xi])
    r2(0)
    r4(2)
    for copy in n_z:
        copy.wait_recv()
    total = NZR[0]
    for j in range(1, nz):
        total = total + NZR[j]
    ng_out[...] = total
    r3(0)
    r4(0)
    o_far.wait_recv()
    i_far.wait_recv()
    o_own.wait()
    i_own.wait()
    for k in range(4):
        rs[k, "out"].wait()
    for copy in list(sends.values()):
        sent(copy)


def layer_per_device(
    dp_size,
    layer_input,
    cotangent,
    segment_ids,
    query_weight,
    key_weight,
    value_weight,
    output_weight,
    gate_weight,
    up_weight,
    down_weight,
    first_gain,
    first_bias,
    second_gain,
    second_bias,
):
    _, quarter, width = layer_input.shape
    length = 4 * quarter
    rows = query_weight.shape[0]
    nz = dp_size // NY
    out_turned = output_weight.T
    two = 2 * HD
    attention_pack = jnp.concatenate(
        [
            query_weight[:, :two],
            key_weight[:, :two],
            value_weight[:, :two],
            query_weight[:, two:],
            key_weight[:, two:],
            value_weight[:, two:],
            out_turned[:, two:],
            out_turned[:, :two],
        ],
        axis=1,
    )
    packed = jnp.stack([attention_pack, gate_weight, up_weight, down_weight.T])
    tables = [jnp.asarray(t) for t in lane_tables(length)]
    vectors = [v.reshape(1, width) for v in (first_gain, first_bias, second_gain, second_bias)]
    anywhere = pl.BlockSpec(memory_space=pl.ANY)
    vmem = pl.BlockSpec(memory_space=pltpu.VMEM)
    half = HD // 2
    copies = 256
    scratch = [
        ((4, 2, nz, NY, rows, width), BF16),
        ((2, nz, NY, rows, width), BF16),
        ((4, nz // 2, rows, width), BF16),
        ((4, nz - nz // 2, rows, width), BF16),
        ((4, nz, rows, width), BF16),
        ((4, nz, rows, width), BF16),
        ((4, nz, rows, width), BF16),
        ((4, quarter, width), BF16),
        ((width, length), BF16),
        ((width, length), BF16),
        ((width, length), BF16),
        ((2, quarter, width), BF16),
        ((length, LANES), F32),
        ((length, LANES), F32),
        ((length, LANES), F32),
        ((half, length), F32),
        ((half, length), F32),
        ((2, 5, length, LANES), BF16),
        ((6, LANES, length), BF16),
        ((6, HD, length), BF16),
        ((6, HD, length), BF16),
        ((6, 1, length), F32),
        ((6, 1, length), F32),
        ((2, length, 2 * LANES), BF16),
        ((6, HD, length), BF16),
        ((2, quarter, width), F32),
        ((2, quarter, LANES), F32),
        ((4, quarter, width), BF16),
        ((2, length, width), BF16),
        ((2, length, width), BF16),
        ((2, length, width), BF16),
        ((2, quarter, width), F32),
        ((2, quarter, width), BF16),
        ((2, 2, quarter, width), BF16),
        ((2, quarter, width), F32),
        ((2, 2, quarter, width), BF16),
        ((length, LANES), F32),
        ((length, LANES), F32),
        ((8, width), F32),
        ((3, 8, width), F32),
        ((3, 8, width), F32),
        ((nz, 8, width), F32),
    ]
    outputs, grad_input, grads, norms = pl.pallas_call(
        functools.partial(layer_kernel, nz),
        out_shape=(
            jax.ShapeDtypeStruct(layer_input.shape, BF16),
            jax.ShapeDtypeStruct(layer_input.shape, BF16),
            jax.ShapeDtypeStruct((4, rows, width), F32),
            jax.ShapeDtypeStruct((8, width), F32),
        ),
        in_specs=[anywhere, anywhere, vmem, anywhere] + [vmem] * 4 + [anywhere] * 4,
        out_specs=(anywhere, anywhere, anywhere, vmem),
        scratch_shapes=[pltpu.VMEM(shape, kind) for shape, kind in scratch]
        + [
            pltpu.SemaphoreType.DMA((16,)),
            pltpu.SemaphoreType.DMA((copies,)),
            pltpu.SemaphoreType.DMA((copies,)),
        ],
        compiler_params=pltpu.CompilerParams(
            collective_id=0, has_side_effects=True, vmem_limit_bytes=VMEM_BYTES
        ),
    )(layer_input, cotangent, segment_ids, packed, *vectors, *tables)
    attention, gate, up, down = grads
    b = [attention[:, i * LANES : (i + 1) * LANES] for i in range(6)]
    grad_query = jnp.concatenate([b[0], b[3][:, :HD]], axis=1)
    grad_key = jnp.concatenate([b[1], b[3][:, HD:]], axis=1)
    grad_value = jnp.concatenate([b[2], b[4][:, :HD]], axis=1)
    grad_output = jnp.concatenate([b[5], b[4][:, HD:]], axis=1).T
    return (
        outputs,
        grad_input,
        grad_query,
        grad_key,
        grad_value,
        grad_output,
        gate,
        up,
        down.T,
        norms[0],
        norms[1],
        norms[2],
        norms[3],
    )


VMEM_BYTES = 64 << 20


def solution(mesh):
    in_specs = (
        P("dp", "tensor", None),
        P("dp", "tensor", None),
        P("dp", None),
        P("dp", "tensor"),
        P("dp", "tensor"),
        P("dp", "tensor"),
        P("tensor", "dp"),
        P("dp", "tensor"),
        P("dp", "tensor"),
        P("tensor", "dp"),
        P(),
        P(),
        P(),
        P(),
    )
    out_specs = (
        P("dp", "tensor", None),
        P("dp", "tensor", None),
        P("dp", "tensor"),
        P("dp", "tensor"),
        P("dp", "tensor"),
        P("tensor", "dp"),
        P("dp", "tensor"),
        P("dp", "tensor"),
        P("tensor", "dp"),
        P(),
        P(),
        P(),
        P(),
    )
    dp_size, tensor_size = mesh.shape["dp"], mesh.shape["tensor"]

    def whole(*arrays):
        layer_input, query_weight, gate_weight = arrays[0], arrays[3], arrays[7]
        batch, length, width = layer_input.shape
        fits = (
            tensor_size == 4
            and dp_size % (2 * NY) == 0
            and batch == 2 * dp_size
            and width % (16 * dp_size) == 0
            and query_weight.shape[1] == 12 * HD
            and query_weight.shape[1] == width
            and gate_weight.shape[1] == 4 * width
            and length % 1024 == 0
        )
        program = functools.partial(layer_per_device, dp_size) if fits else per_device
        return jax.shard_map(
            program, mesh=mesh, in_specs=in_specs, out_specs=out_specs, check_vma=False
        )(*arrays)

    return whole
```

```python
import functools

import jax
import jax.numpy as jnp
import numpy as np
from jax import lax
from jax.experimental import pallas as pl
from jax.experimental.pallas import tpu as pltpu
from jax.sharding import PartitionSpec as P

HD = 64


eps_norm = 1e-06
rope_base = 1000.0
mask_fill = -1e30


def layer_norm(field_rows, gain_vec, bias_vec):
    row_mean = jnp.mean(field_rows, axis=-1, keepdims=True)
    centred = field_rows - row_mean
    variance = jnp.mean(centred * centred, axis=-1, keepdims=True)
    return centred * lax.rsqrt(variance + eps_norm) * gain_vec + bias_vec


def rotary_tables(length, head_dim):
    half_dim = head_dim // 2
    frequency = rope_base ** (-(2.0 * jnp.arange(half_dim, dtype=jnp.float32)) / head_dim)
    angles = jnp.arange(length, dtype=jnp.float32)[:, None] * frequency[None, :]
    return (jnp.cos(angles), jnp.sin(angles))


def rotate(heads_data, cos_table, sine_table):
    half_dim = heads_data.shape[-1] // 2
    first_half = heads_data[..., :half_dim]
    second_half = heads_data[..., half_dim:]
    cos_part = cos_table[:, None, :]
    sine_part = sine_table[:, None, :]
    return jnp.concatenate(
        [
            first_half * cos_part - second_half * sine_part,
            second_half * cos_part + first_half * sine_part,
        ],
        axis=-1,
    )


def swiglu(gate_pre, up_pre):
    return jax.nn.silu(gate_pre) * up_pre


def contract_rows(left, right):
    return lax.dot_general(
        left, right, (((0,), (0,)), ((), ())), preferred_element_type=jnp.float32
    )


def times_transpose(left, right):
    return lax.dot_general(
        left, right, (((1,), (1,)), ((), ())), preferred_element_type=jnp.float32
    )


def per_device(
    layer_input,
    cotangent,
    segment_ids,
    query_weight,
    key_weight,
    value_weight,
    output_weight,
    gate_weight,
    up_weight,
    down_weight,
    first_gain,
    first_bias,
    second_gain,
    second_bias,
):
    model_width = layer_input.shape[2]
    length = segment_ids.shape[1]
    block_rows = min(512, length)
    block_count = length // block_rows
    local_heads = query_weight.shape[1] // HD
    local_width = local_heads * HD
    score_scale = HD ** (-0.5)
    cos_table, sine_table = rotary_tables(length, HD)

    def fetch_weights():
        row_parts = (
            lax.all_gather(query_weight, "dp", axis=0, tiled=True),
            lax.all_gather(key_weight, "dp", axis=0, tiled=True),
            lax.all_gather(value_weight, "dp", axis=0, tiled=True),
            lax.all_gather(gate_weight, "dp", axis=0, tiled=True),
            lax.all_gather(up_weight, "dp", axis=0, tiled=True),
        )
        col_parts = (
            lax.all_gather(output_weight, "dp", axis=1, tiled=True),
            lax.all_gather(down_weight, "dp", axis=1, tiled=True),
        )
        return tuple(row_parts) + tuple(col_parts)

    def micro_step(weights, row_input, row_cotangent, segment_row):
        query_full, key_full, value_full, gate_full, up_full, output_full, down_full = weights
        full_input = lax.all_gather(row_input, "tensor", axis=0, tiled=True)
        query_pre = jnp.dot(full_input, query_full, preferred_element_type=jnp.float32).reshape(
            length, local_heads, HD
        )
        key_pre = jnp.dot(full_input, key_full, preferred_element_type=jnp.float32).reshape(
            length, local_heads, HD
        )
        value_rows = (
            jnp.dot(full_input, value_full, preferred_element_type=jnp.float32)
            .astype(jnp.bfloat16)
            .reshape(length, local_heads, HD)
        )
        query_rows = rotate(query_pre, cos_table, sine_table).astype(jnp.bfloat16)
        key_rows = rotate(key_pre, cos_table, sine_table).astype(jnp.bfloat16)
        query_blocks = query_rows.reshape(block_count, block_rows, local_heads, HD)
        segment_blocks = segment_row.reshape(block_count, block_rows)

        def block_scores(query_block, segment_block):
            scores = (
                jnp.einsum(
                    "qhd,khd->hqk", query_block, key_rows, preferred_element_type=jnp.float32
                )
                * score_scale
            )
            allowed = segment_block[:, None] == segment_row[None, :]
            return jnp.where(allowed[None, :, :], scores, mask_fill)

        def attend_forward(block_inputs):
            scores = block_scores(block_inputs[0], block_inputs[1])
            row_max = jnp.max(scores, axis=-1, keepdims=True)
            exponent_terms = jnp.exp(scores - row_max)
            row_total = jnp.sum(exponent_terms, axis=-1, keepdims=True)
            probabilities = (exponent_terms / row_total).astype(jnp.bfloat16)
            mixed_rows = jnp.einsum(
                "hqk,khd->qhd", probabilities, value_rows, preferred_element_type=jnp.float32
            )
            return (mixed_rows, (row_max + jnp.log(row_total))[..., 0])

        mixed_blocks, log_totals = lax.map(attend_forward, (query_blocks, segment_blocks))
        attended = mixed_blocks.reshape(length, local_width).astype(jnp.bfloat16)
        attention_branch = lax.psum_scatter(
            jnp.dot(attended, output_full, preferred_element_type=jnp.float32).astype(jnp.bfloat16),
            "tensor",
            scatter_dimension=0,
            tiled=True,
        ).astype(jnp.float32)
        first_sum = row_input.astype(jnp.float32) + attention_branch
        hidden_state, first_back = jax.vjp(layer_norm, first_sum, first_gain, first_bias)
        full_hidden = lax.all_gather(
            hidden_state.astype(jnp.bfloat16), "tensor", axis=0, tiled=True
        )
        gate_pre = jnp.dot(full_hidden, gate_full, preferred_element_type=jnp.float32)
        up_pre = jnp.dot(full_hidden, up_full, preferred_element_type=jnp.float32)
        activated_exact, swiglu_back = jax.vjp(swiglu, gate_pre, up_pre)
        activated = activated_exact.astype(jnp.bfloat16)
        feed_branch = lax.psum_scatter(
            jnp.dot(activated, down_full, preferred_element_type=jnp.float32).astype(jnp.bfloat16),
            "tensor",
            scatter_dimension=0,
            tiled=True,
        ).astype(jnp.float32)
        layer_output, second_back = jax.vjp(
            layer_norm, hidden_state + feed_branch, second_gain, second_bias
        )
        grad_second_sum, grad_second_gain, grad_second_bias = second_back(
            row_cotangent.astype(jnp.float32)
        )
        grad_second_full = lax.all_gather(
            grad_second_sum.astype(jnp.bfloat16), "tensor", axis=0, tiled=True
        )
        grad_activated = times_transpose(grad_second_full, down_full)
        grad_down = contract_rows(activated, grad_second_full)
        grad_gate_pre, grad_up_pre = swiglu_back(grad_activated)
        gate_low = grad_gate_pre.astype(jnp.bfloat16)
        up_low = grad_up_pre.astype(jnp.bfloat16)
        grad_hidden = grad_second_sum + lax.psum_scatter(
            (times_transpose(gate_low, gate_full) + times_transpose(up_low, up_full)).astype(
                jnp.bfloat16
            ),
            "tensor",
            scatter_dimension=0,
            tiled=True,
        ).astype(jnp.float32)
        grad_gate = contract_rows(full_hidden, gate_low)
        grad_up = contract_rows(full_hidden, up_low)
        grad_first_sum, grad_first_gain, grad_first_bias = first_back(grad_hidden)
        grad_first_full = lax.all_gather(
            grad_first_sum.astype(jnp.bfloat16), "tensor", axis=0, tiled=True
        )
        grad_attended = (
            times_transpose(grad_first_full, output_full)
            .astype(jnp.bfloat16)
            .reshape(block_count, block_rows, local_heads, HD)
        )
        grad_output = contract_rows(attended, grad_first_full)

        def attend_backward(sums_carry, block_inputs):
            key_sum, value_sum = sums_carry
            query_block, segment_block, log_block, grad_block = block_inputs
            scores = block_scores(query_block, segment_block)
            probabilities = jnp.exp(scores - log_block[..., None])
            grad_softmax = jnp.einsum(
                "qhd,khd->hqk", grad_block, value_rows, preferred_element_type=jnp.float32
            )
            value_sum = value_sum + jnp.einsum(
                "hqk,qhd->khd",
                probabilities.astype(jnp.bfloat16),
                grad_block,
                preferred_element_type=jnp.float32,
            )
            row_inner = jnp.sum(probabilities * grad_softmax, axis=-1, keepdims=True)
            grad_scores = (probabilities * (grad_softmax - row_inner)).astype(jnp.bfloat16)
            grad_query_block = (
                jnp.einsum(
                    "hqk,khd->qhd", grad_scores, key_rows, preferred_element_type=jnp.float32
                )
                * score_scale
            )
            key_sum = (
                key_sum
                + jnp.einsum(
                    "hqk,qhd->khd", grad_scores, query_block, preferred_element_type=jnp.float32
                )
                * score_scale
            )
            return ((key_sum, value_sum), grad_query_block)

        zero_heads = jnp.zeros((length, local_heads, HD), jnp.float32)
        (grad_key_rot, grad_value_rows), grad_query_blocks = lax.scan(
            attend_backward,
            (zero_heads, zero_heads),
            (query_blocks, segment_blocks, log_totals, grad_attended),
        )
        grad_query_low = (
            rotate(grad_query_blocks.reshape(length, local_heads, HD), cos_table, -sine_table)
            .astype(jnp.bfloat16)
            .reshape(length, local_width)
        )
        grad_key_low = (
            rotate(grad_key_rot, cos_table, -sine_table)
            .astype(jnp.bfloat16)
            .reshape(length, local_width)
        )
        grad_value_low = grad_value_rows.astype(jnp.bfloat16).reshape(length, local_width)
        query_part = times_transpose(grad_query_low, query_full)
        key_part = times_transpose(grad_key_low, key_full)
        value_part = times_transpose(grad_value_low, value_full)
        grad_input = grad_first_sum + lax.psum_scatter(
            (query_part + key_part + value_part).astype(jnp.bfloat16),
            "tensor",
            scatter_dimension=0,
            tiled=True,
        ).astype(jnp.float32)
        row_grads = (
            contract_rows(full_input, grad_query_low),
            contract_rows(full_input, grad_key_low),
            contract_rows(full_input, grad_value_low),
            grad_gate,
            grad_up,
        )
        col_grads = (grad_output, grad_down)
        norm_parts = (grad_first_gain, grad_first_bias, grad_second_gain, grad_second_bias)
        return (
            layer_output.astype(jnp.bfloat16),
            grad_input.astype(jnp.bfloat16),
            (row_grads, col_grads, norm_parts),
        )

    norm_zero = tuple(
        (
            jnp.zeros(gain_like.shape, jnp.float32)
            for gain_like in (first_gain, first_bias, second_gain, second_bias)
        )
    )
    row_zero = tuple(
        (
            jnp.zeros((model_width, weight_part.shape[1]), jnp.float32)
            for weight_part in (query_weight, key_weight, value_weight, gate_weight, up_weight)
        )
    )
    col_zero = (
        jnp.zeros((output_weight.shape[0], model_width), jnp.float32),
        jnp.zeros((down_weight.shape[0], model_width), jnp.float32),
    )

    def scan_step(totals, batch_rows):
        weights = fetch_weights()
        layer_output, grad_input, grad_terms = micro_step(
            weights, batch_rows[0], batch_rows[1], batch_rows[2]
        )
        return (jax.tree.map(jnp.add, totals, grad_terms), (layer_output, grad_input))

    totals, (outputs, grad_inputs) = lax.scan(
        scan_step, (row_zero, col_zero, norm_zero), (layer_input, cotangent, segment_ids)
    )
    row_grads, col_grads, norm_parts = totals
    row_done = lax.psum_scatter(row_grads, "dp", scatter_dimension=0, tiled=True)
    col_done = (
        lax.psum_scatter(col_grads[0], "dp", scatter_dimension=1, tiled=True),
        lax.psum_scatter(col_grads[1], "dp", scatter_dimension=1, tiled=True),
    )
    norm_done = lax.psum(norm_parts, ("dp", "tensor"))
    totals = (tuple(row_done), tuple(col_done), tuple(norm_done))
    row_done, col_done, norm_done = totals
    return (
        outputs,
        grad_inputs,
        row_done[0],
        row_done[1],
        row_done[2],
        col_done[0],
        row_done[3],
        row_done[4],
        col_done[1],
        norm_done[0],
        norm_done[1],
        norm_done[2],
        norm_done[3],
    )


F32 = jnp.float32
BF16 = jnp.bfloat16
NY = 2
LANES = 128
MESH = pl.DeviceIdType.MESH


def mm(left, right):
    return lax.dot_general(left, right, (((1,), (0,)), ((), ())), preferred_element_type=F32)


def mt(left, right):
    return lax.dot_general(left, right, (((1,), (1,)), ((), ())), preferred_element_type=F32)


def lane_tables(length):
    half = HD // 2
    steps = np.arange(half, dtype=np.float32)
    frequency = np.float32(rope_base) ** (-(np.float32(2.0) * steps) / np.float32(HD))
    angles = np.arange(length, dtype=np.float32)[:, None] * frequency[None, :]
    angles = angles.astype(np.float32)
    cos, sin = np.cos(angles).astype(np.float32), np.sin(angles).astype(np.float32)
    cos_lane = np.concatenate([cos] * 4, axis=1)
    sin_lane = np.concatenate([-sin, sin, -sin, sin], axis=1)
    return cos_lane, sin_lane, np.ascontiguousarray(cos.T), np.ascontiguousarray(sin.T)


def norm_of(v):
    mu = jnp.mean(v, axis=-1, keepdims=True)
    cen = v - mu
    rstd = lax.rsqrt(jnp.mean(cen * cen, axis=-1, keepdims=True) + eps_norm)
    return cen * rstd, rstd


def grad_of_norm(dn, n, rstd):
    m0 = jnp.mean(dn, axis=-1, keepdims=True)
    m1 = jnp.mean(dn * n, axis=-1, keepdims=True)
    return (dn - m0 - n * m1) * rstd


def colsum(v):
    return jnp.sum(v, axis=0, keepdims=True)


def layer_kernel(
    nz,
    xin,
    cot,
    seg_h,
    wq_h,
    wk_h,
    wv_h,
    wo_h,
    wg_h,
    wu_h,
    wd_h,
    g1_h,
    b1_h,
    g2_h,
    b2_h,
    cosl_h,
    sinl_h,
    cosf_h,
    sinf_h,
    out_h,
    gin_h,
    gw_h,
    ng_out,
    W,
    G,
    S1X,
    S1Y,
    S2X,
    S2Y,
    ZR,
    X,
    XT,
    TT,
    DT,
    CT,
    SC,
    COSL,
    SINL,
    COSF,
    SINF,
    PK,
    QZ,
    KT,
    VT,
    LSE,
    DEL,
    ATT,
    ATTT,
    N1,
    R1,
    F4,
    GP,
    UP,
    RR,
    DZ,
    CXS,
    CXR,
    ACC,
    OB,
    DKA,
    DVA,
    SEG,
    WQ,
    WK,
    WV,
    WO,
    VEC,
    NG,
    NR,
    NS,
    NZR,
    ZB,
    loc,
    ssem,
    rsem,
):
    quarter, width = X.shape[1], X.shape[2]
    length = 4 * quarter
    rows = W.shape[4]
    dp = lax.axis_index("dp")
    tt = lax.axis_index("tensor")
    c = lax.rem(tt, 2)
    xi = lax.div(tt, 2)
    z = lax.div(dp, NY)
    y = lax.rem(dp, NY)
    oy = 1 - y
    t_x = lax.rem(tt + 2, 4)
    dev_x = (dp, t_x)
    dev_c = (dp, tt + 1 - 2 * c)
    dev_y = (dp + 1 - 2 * y, tt)
    zs = [lax.rem(z + j, nz) for j in range(nz)]
    zfrom = [lax.rem(z + nz - j, nz) for j in range(nz)]
    dev_z = [(zs[j] * NY + y, tt) for j in range(nz)]
    hz = nz // 2
    count = [0]
    lcount = [0]
    sends = {}

    def rc(src, dst, dev):
        i = count[0]
        count[0] += 1
        copy = pltpu.make_async_remote_copy(
            src_ref=src,
            dst_ref=dst,
            send_sem=ssem.at[i],
            recv_sem=rsem.at[i],
            device_id=dev,
            device_id_type=MESH,
        )
        copy.start()
        sends[id(copy)] = copy
        return copy

    def sent(copy):
        copy.wait_send()
        del sends[id(copy)]

    def lc(src, dst):
        i = lcount[0]
        lcount[0] += 1
        copy = pltpu.make_async_copy(src, dst, loc.at[i])
        copy.start()
        return copy

    l_out, l_att = lc(wo_h, WO), [lc(wq_h, WQ), lc(wk_h, WK), lc(wv_h, WV)]
    l_w = [lc(wg_h, W.at[1, 0, z, y]), lc(wu_h, W.at[2, 0, z, y]), lc(wd_h, W.at[3, 0, z, y])]
    l_seg = lc(seg_h, SEG)
    l_vec = [lc(h, VEC.at[i, 0]) for i, h in enumerate((g1_h, b1_h, g2_h, b2_h))]
    l_x = lc(xin.at[xi], X.at[tt])
    l_ct = lc(cot.at[xi], CT.at[xi])
    l_tab = [lc(cosl_h, COSL), lc(sinl_h, SINL), lc(cosf_h, COSF), lc(sinf_h, SINF)]

    barrier = pltpu.get_barrier_semaphore()
    peers = [dev_x, dev_c, dev_y] + dev_z[1:]
    for dev in peers:
        pl.semaphore_signal(barrier, inc=1, device_id=dev, device_id_type=MESH)
    l_out.wait()
    for copy in l_att:
        copy.wait()
    shards = [W.at[0, 0, z, y], wg_h, wu_h, wd_h]
    two = 2 * HD
    turned_out = WO[...].T
    shards[0][:, :two] = WQ[:, :two]
    shards[0][:, two : 2 * two] = WK[:, :two]
    shards[0][:, 2 * two : 3 * two] = WV[:, :two]
    shards[0][:, 3 * two : 4 * two] = jnp.concatenate([WQ[:, two:], WK[:, two:]], axis=1)
    shards[0][:, 4 * two : 5 * two] = jnp.concatenate([WV[:, two:], turned_out[:, two:]], axis=1)
    shards[0][:, 5 * two :] = turned_out[:, :two]
    pl.semaphore_wait(barrier, len(peers))

    ag = {}
    half_cols = width // 2
    pieces = [(0, 0, width), (1, 0, width), (2, 0, width), (3, 0, half_cols), (3, half_cols, half_cols)]
    LAST = 4

    def cut(view, p):
        _, lo, n = pieces[p]
        return view if n == width else view.at[..., pl.ds(lo, n)]

    def w_at(p, s, zz, yy):
        return cut(W.at[pieces[p][0], s, zz, yy], p)

    def own_shard(p):
        return cut(shards[pieces[p][0]], p)

    def e1_plane(p):
        own = own_shard(p)
        ag[p, "x"] = [rc(own, w_at(p, 1, z, y), dev_x)]
        ag[p, "y"] = [rc(own, w_at(p, 0, z, y), dev_y)]

    def e1(p):
        own = own_shard(p)
        ag[p, "z"] = [rc(own, w_at(p, 0, z, y), dev_z[j]) for j in range(1, nz)]
        e1_plane(p)

    def e2(p):
        for j in range(1, nz):
            ag[p, "z"][j - 1].wait_recv()
            part = w_at(p, 0, zfrom[j], y)
            ag[p, "x"].append(rc(part, w_at(p, 1, zfrom[j], y), dev_x))
            ag[p, "y"].append(rc(part, part, dev_y))

    def e3(p, by_x):
        ag[p, "d"] = []
        for j in range(nz):
            ag[p, "x"][j].wait_recv()
            if j < nz - by_x:
                part = w_at(p, 1, zfrom[j], y)
                ag[p, "d"].append(rc(part, part, dev_y))
            ag[p, "y"][j].wait_recv()
            if j >= nz - by_x:
                ag[p, "d"].append(rc(w_at(p, 0, zfrom[j], oy), w_at(p, 1, zfrom[j], oy), dev_x))

    def e4(p):
        for copy in ag[p, "d"]:
            copy.wait_recv()

    top_rows, low_rows = pl.ds(0, rows // 2), pl.ds(rows // 2, rows // 2)

    def f2(p):
        ag[p, "x"][0].wait_recv()
        part = w_at(p, 1, z, y).at[top_rows]
        ag[p, "d"] = [rc(part, part, dev_y)]
        ag[p, "y"][0].wait_recv()
        ag[p, "d"].append(
            rc(w_at(p, 0, z, oy).at[low_rows], w_at(p, 1, z, oy).at[low_rows], dev_x)
        )

    def f3(p):
        for copy in ag[p, "d"]:
            copy.wait_recv()
        plane = cut(W.at[3, :, z], p)
        ag[p, "z"] = [rc(plane, plane, dev_z[j]) for j in range(1, nz)]

    def f4(p):
        for copy in ag[p, "z"]:
            copy.wait_recv()

    def e_sent(p):
        for copy in ag[p, "z"] + ag[p, "x"] + ag[p, "y"] + ag[p, "d"]:
            sent(copy)

    x_far = rc(xin.at[1 - xi], X.at[tt], dev_x)
    x_core = rc(xin.at[xi], X.at[tt], dev_c)
    e1(0)
    e1_plane(LAST)

    l_seg.wait()
    seg = SEG
    g1_ref, b1_ref, g2_ref, b2_ref = (VEC.at[i] for i in range(4))
    SC[...] = jnp.broadcast_to(seg[pl.ds(xi, 1), :].astype(F32), (LANES, length)).T
    NG[...] = jnp.zeros_like(NG)
    lane = lax.broadcasted_iota(jnp.int32, (1, LANES), 1)
    low_half = lane < HD
    swap_low = lax.rem(lane, HD) < (HD // 2)

    def swap(v):
        return jnp.where(swap_low, pltpu.roll(v, LANES - HD // 2, 1), pltpu.roll(v, HD // 2, 1))

    def at_quarter(i):
        return pl.ds(pl.multiple_of(i * quarter, quarter), quarter)

    def wmat(k, s, lo=0, hi=None):
        hi = width if hi is None else hi
        return W[k, s, :, :, :, lo:hi].reshape(width, hi - lo)

    def turn_rows(src, dst):
        def step(i, _):
            dst[:, at_quarter(i)] = src[i].T
            return 0

        lax.fori_loop(0, 4, step, 0)

    x_far.wait_recv()
    x_core2 = rc(X.at[t_x], X.at[t_x], dev_c)
    x_core.wait_recv()
    l_x.wait()
    l_ct.wait()
    for copy in l_w + l_vec + l_tab:
        copy.wait()
    x_core2.wait_recv()
    turn_rows(X, XT)
    e2(0)
    e1(1)
    f2(LAST)
    e3(0, 1)

    def project(s):
        def step(i, _):
            at = at_quarter(i)
            y5 = mm(X[i], wmat(0, s, 0, 5 * LANES))
            cos, sin = COSL[at, :], SINL[at, :]
            turned = []
            for b in range(5):
                v = y5[:, b * LANES : (b + 1) * LANES]
                if b in (0, 1, 3):
                    v = v * cos + swap(v) * sin
                v = v.astype(BF16)
                PK[s, b, at, :] = v
                turned.append(v.T)
            zero = jnp.zeros((HD, quarter), BF16)
            q0 = turned[0] * BF16(0.125)
            q2 = turned[3] * BF16(0.125)
            QZ[3 * s, :HD, at] = q0[:HD]
            QZ[3 * s, HD:, at] = zero
            QZ[3 * s + 1, :HD, at] = zero
            QZ[3 * s + 1, HD:, at] = q0[HD:]
            QZ[3 * s + 2, :HD, at] = zero
            QZ[3 * s + 2, HD:, at] = q2[:HD]
            KT[3 * s, :, at] = turned[1][:HD]
            KT[3 * s + 1, :, at] = turned[1][HD:]
            KT[3 * s + 2, :, at] = turned[3][HD:]
            VT[3 * s, :, at] = turned[2][:HD]
            VT[3 * s + 1, :, at] = turned[2][HD:]
            VT[3 * s + 2, :, at] = turned[4][:HD]
            return 0

        lax.fori_loop(0, 4, step, 0)

    def scores_of(s, hh, h, at):
        st = mm(PK[s, 1 + 2 * lax.div(hh, 2)], QZ[h, :, at])
        key_seg = jnp.concatenate([SC[...]] * (quarter // LANES), axis=1)
        query_seg = seg[pl.ds(xi, 1), at].astype(F32)
        return jnp.where(key_seg == query_seg, st, mask_fill)

    def attend(first, heads):
        def step(n, _):
            h = first + lax.div(n, 4)
            s, hh = lax.div(h, 3), lax.rem(h, 3)
            at = at_quarter(lax.rem(n, 4))
            st = scores_of(s, hh, h, at)
            top = jnp.max(st, axis=0, keepdims=True)
            p = jnp.exp(st - top)
            total = jnp.sum(p, axis=0, keepdims=True)
            ot = mm(VT[h], p.astype(BF16)) * (1.0 / total)
            LSE[h, :, at] = top + jnp.log(total)
            ATTT[h, :, at] = ot.astype(BF16)
            return 0

        lax.fori_loop(0, 4 * heads, step, 0)

    def turn_heads(s):
        def turn(i, _):
            at = at_quarter(i)
            pair = jnp.concatenate([ATTT[3 * s, :, at], ATTT[3 * s + 1, :, at]], axis=0)
            lone = jnp.concatenate([jnp.zeros((HD, quarter), BF16), ATTT[3 * s + 2, :, at]], axis=0)
            ATT[s, at, :LANES] = lone.T
            ATT[s, at, LANES:] = pair.T
            return 0

        lax.fori_loop(0, 4, turn, 0)

    project(0)
    e2(1)
    e1(2)
    e4(0)
    project(1)
    attend(0, 2)
    e3(1, 2)
    e2(2)
    e1(3)
    attend(2, 2)
    ct_far = rc(cot.at[1 - xi], CT.at[xi], dev_x)
    f3(LAST)
    attend(4, 2)
    e4(1)
    turn_heads(0)
    turn_heads(1)
    last_exchange = []

    def exchange(n, part):
        if last_exchange:
            sent(last_exchange.pop())

        def other(k, _):
            CXS[k] = part(1 - c + 2 * k).astype(BF16)
            return 0

        lax.fori_loop(0, 2, other, 0)
        copy = rc(CXS, CXR.at[n % 2], dev_c)
        last_exchange.append(copy)

        def own(k, _):
            ACC[k] = part(c + 2 * k)
            return 0

        lax.fori_loop(0, 2, own, 0)
        copy.wait_recv()

    def spread():
        return [rc(F4.at[c + 2 * k], F4.at[c + 2 * k], dev_c) for k in range(2)]

    def out_part(i):
        at = at_quarter(i)
        return mt(ATT[0, at, :], wmat(0, 0, 4 * LANES)) + mt(ATT[1, at, :], wmat(0, 1, 4 * LANES))

    exchange(0, out_part)
    tile = quarter // 2

    def over_tiles(fn):
        def step(n, _):
            k = lax.div(n, 2)
            fn(k, c + 2 * k, pl.ds(pl.multiple_of(lax.rem(n, 2) * tile, tile), tile))
            return 0

        lax.fori_loop(0, 4, step, 0)

    def first_norm(k, i, at):
        z1 = X[i, at, :].astype(F32) + ACC[k, at, :] + CXR[0, k, at, :].astype(F32)
        n1, rstd = norm_of(z1)
        N1[k, at, :] = n1
        R1[k, at, :] = jnp.broadcast_to(rstd, (tile, LANES))
        F4[i, at, :] = (n1 * g1_ref[...] + b1_ref[...]).astype(BF16)

    over_tiles(first_norm)
    h_copies = spread()
    e3(2, 1)
    for copy in h_copies:
        copy.wait_recv()
    turn_rows(F4, TT)
    e2(3)

    def ff_up(s, i):
        at = at_quarter(i)
        g = mm(F4[i], wmat(1, s))
        u = mm(F4[i], wmat(2, s))
        GP[s, at, :] = g.astype(BF16)
        UP[s, at, :] = u.astype(BF16)
        RR[s, at, :] = (g * jax.nn.sigmoid(g) * u).astype(BF16)
        return 0

    lax.fori_loop(0, 4, lambda i, _: ff_up(0, i), 0)
    e4(2)
    e3(3, 1)
    lax.fori_loop(0, 4, lambda i, _: ff_up(1, i), 0)
    e4(3)
    f4(LAST)

    def down_part(i):
        at = at_quarter(i)
        return mt(RR[0, at, :], wmat(3, 0)) + mt(RR[1, at, :], wmat(3, 1))

    for copy in h_copies:
        sent(copy)
    exchange(1, down_part)
    ct_far.wait_recv()

    def second_norm(k, i, at):
        h = N1[k, at, :] * g1_ref[...] + b1_ref[...]
        z2 = h + ACC[k, at, :] + CXR[1, k, at, :].astype(F32)
        n2, rstd = norm_of(z2)
        OB[0, k, at, :] = (n2 * g2_ref[...] + b2_ref[...]).astype(BF16)
        dy = CT[k, at, :].astype(F32)
        NG[2:3, :] += colsum(dy * n2)
        NG[3:4, :] += colsum(dy)
        dz = grad_of_norm(dy * g2_ref[...], n2, rstd)
        DZ[k, at, :] = dz
        F4[i, at, :] = dz.astype(BF16)

    over_tiles(second_norm)
    d_copies = spread()
    o_far = rc(OB.at[0, 1 - xi], out_h.at[xi], dev_x)
    o_own = lc(OB.at[0, xi], out_h.at[xi])

    slots = {3: G, 1: W.at[3], 2: W.at[1], 0: W.at[2]}
    rs = {}
    by_x = {0: 1, 1: 1, 2: 1, 3: 2}

    def g_at(p, s, zz, yy):
        return cut(slots[pieces[p][0]].at[s, zz, yy], p)

    def into(ref, p, *at):
        return cut(ref.at[(pieces[p][0],) + at], p)

    def plus(target, *others):
        total = target[...].astype(F32)
        for other in others:
            total = total + other[...].astype(F32)
        target[...] = total.astype(BF16)

    def early(p):
        return pl.ds(0, by_x[p]), pl.ds(by_x[p], nz - by_x[p])

    def r1_far(p):
        nx = by_x[p]
        near, far = early(p)
        rs[p, "dx"] = rc(g_at(p, 1, near, oy), into(S1X, p, pl.ds(0, nx)), dev_x)
        rs[p, "dy"] = rc(g_at(p, 1, far, oy), into(S1Y, p, pl.ds(0, nz - nx)), dev_y)
        rs[p, "x0"] = rc(g_at(p, 1, near, y), into(S2X, p, near), dev_x)

    def r1_near(p):
        _, far = early(p)
        rs[p, "y0"] = rc(g_at(p, 0, far, oy), into(S2Y, p, far), dev_y)

    def r2(p):
        nx = by_x[p]
        near, far = early(p)
        rs[p, "dx"].wait_recv()
        for j in range(nx):
            plus(g_at(p, 0, j, oy), into(S1X, p, j))
        rs[p, "y1"] = rc(g_at(p, 0, near, oy), into(S2Y, p, near), dev_y)
        rs[p, "dy"].wait_recv()
        for j in range(nx, nz):
            plus(g_at(p, 1, j, y), into(S1Y, p, j - nx))
        rs[p, "x1"] = rc(g_at(p, 1, far, y), into(S2X, p, far), dev_x)

    def r3(p):
        for name in ("x0", "y0", "y1", "x1"):
            rs[p, name].wait_recv()
        for j in range(nz):
            plus(g_at(p, 0, j, y), into(S2X, p, j), into(S2Y, p, j))
        rs[p, "z"] = [rc(g_at(p, 0, zs[j], y), into(ZR, p, z), dev_z[j]) for j in range(1, nz)]

    def place(p):
        k = pieces[p][0]
        return cut(N1.at[k // 2, pl.ds((k % 2) * rows, rows)], p)

    def r4(p):
        for copy in rs[p, "z"]:
            copy.wait_recv()
        total = g_at(p, 0, z, y)[...].astype(F32)
        for j in range(1, nz):
            total = total + into(ZR, p, zfrom[j])[...].astype(F32)
        target = place(p)
        target[...] = total
        rs[p, "out"] = lc(target, cut(gw_h.at[pieces[p][0]], p))

    def q1(p):
        rs[p, "z"] = [
            rc(cut(slots[3].at[:, zs[j]], p), ZB.at[z], dev_z[j]) for j in range(1, nz)
        ]

    def q2(p):
        for copy in rs[p, "z"]:
            copy.wait_recv()
        for s in range(2):
            for yy in range(NY):
                plus(g_at(p, s, z, yy), *(ZB.at[zfrom[j], s, yy] for j in range(1, nz)))
        rs[p, "dx"] = rc(g_at(p, 1, z, oy).at[top_rows], into(S1X, p, 0).at[top_rows], dev_x)
        rs[p, "dy"] = rc(g_at(p, 1, z, oy).at[low_rows], into(S1Y, p, 0).at[low_rows], dev_y)
        rs[p, "x0"] = rc(g_at(p, 1, z, y).at[top_rows], into(S2X, p, 0).at[top_rows], dev_x)
        rs[p, "y0"] = rc(g_at(p, 0, z, oy).at[low_rows], into(S2Y, p, 0).at[low_rows], dev_y)

    def q3(p):
        rs[p, "dx"].wait_recv()
        plus(g_at(p, 0, z, oy).at[top_rows], into(S1X, p, 0).at[top_rows])
        rs[p, "y1"] = rc(g_at(p, 0, z, oy).at[top_rows], into(S2Y, p, 0).at[top_rows], dev_y)
        rs[p, "dy"].wait_recv()
        plus(g_at(p, 1, z, y).at[low_rows], into(S1Y, p, 0).at[low_rows])
        rs[p, "x1"] = rc(g_at(p, 1, z, y).at[low_rows], into(S2X, p, 0).at[low_rows], dev_x)

    def q4(p):
        for name in ("x0", "y0", "y1", "x1"):
            rs[p, name].wait_recv()
        total = g_at(p, 0, z, y)[...].astype(F32)
        total = total + into(S2X, p, 0)[...].astype(F32) + into(S2Y, p, 0)[...].astype(F32)
        target = place(p)
        target[...] = total
        rs[p, "out"] = lc(target, cut(gw_h.at[3], p))

    def weight_grad(p, s, left, right):
        k, lo, n = pieces[p]
        block = NY * rows

        def step(j, _):
            at = pl.ds(pl.multiple_of(j * block, block), block)
            part = mm(left[at, :], right[s, :, lo : lo + n]).astype(BF16)
            slots[k][s, j, :, :, lo : lo + n] = part.reshape(NY, rows, n)
            return 0

        lax.fori_loop(0, nz, step, 0)

    for copy in d_copies:
        copy.wait_recv()
    turn_rows(F4, DT)
    weight_grad(LAST, 0, DT, RR)
    weight_grad(LAST, 1, DT, RR)
    q1(LAST)
    weight_grad(3, 1, DT, RR)
    r1_far(3)
    weight_grad(3, 0, DT, RR)
    r1_near(3)

    def ff_back(n, _):
        s = lax.div(n, 4)
        i = lax.rem(n, 4)
        at = at_quarter(i)
        dr = mm(F4[i], wmat(3, s))
        g = GP[s, at, :].astype(F32)
        u = UP[s, at, :].astype(F32)
        sg = jax.nn.sigmoid(g)
        GP[s, at, :] = (dr * u * sg * (1.0 + g * (1.0 - sg))).astype(BF16)
        UP[s, at, :] = (dr * g * sg).astype(BF16)
        return 0

    lax.fori_loop(0, 8, ff_back, 0)
    r2(3)
    e_sent(3)
    e_sent(LAST)
    weight_grad(1, 1, TT, GP)
    r1_far(1)
    weight_grad(1, 0, TT, GP)
    r1_near(1)

    def hidden_part(i):
        at = at_quarter(i)
        return (
            mt(GP[0, at, :], wmat(1, 0))
            + mt(UP[0, at, :], wmat(2, 0))
            + mt(GP[1, at, :], wmat(1, 1))
            + mt(UP[1, at, :], wmat(2, 1))
        )

    for copy in d_copies:
        sent(copy)
    exchange(2, hidden_part)

    def first_norm_back(k, i, at):
        dh = DZ[k, at, :] + ACC[k, at, :] + CXR[0, k, at, :].astype(F32)
        n1 = N1[k, at, :]
        NG[0:1, :] += colsum(dh * n1)
        NG[1:2, :] += colsum(dh)
        dz = grad_of_norm(dh * g1_ref[...], n1, R1[k, at, :1])
        DZ[k, at, :] = dz
        F4[i, at, :] = dz.astype(BF16)

    over_tiles(first_norm_back)
    b_copies = spread()
    n_core = rc(NG, NR.at[0], dev_c)
    e_sent(1)
    e_sent(2)
    weight_grad(2, 1, TT, UP)
    r1_far(2)
    weight_grad(2, 0, TT, UP)
    r1_near(2)
    r3(3)
    r2(1)
    for copy in b_copies:
        copy.wait_recv()
    n_core.wait_recv()
    NS[0] = NG[...] + NR[0]
    n_x = rc(NS.at[0], NR.at[1], dev_x)
    turn_rows(F4, DT)

    def out_grad(n, _):
        s = lax.div(n, nz)
        j = lax.rem(n, nz)
        block = NY * rows
        at = pl.ds(pl.multiple_of(j * block, block), block)
        part = mm(DT[at, :], ATT[s]).astype(BF16)
        slots[0][s, j, :, :, 4 * LANES :] = part.reshape(NY, rows, 2 * LANES)
        return 0

    lax.fori_loop(0, 2 * nz, out_grad, 0)

    def head_lanes(h):
        return pl.ds(pl.multiple_of(h * LANES, LANES), LANES)

    def att_grad(i, _):
        at = at_quarter(i)
        for s in range(2):
            da = mm(F4[i], wmat(0, s, 4 * LANES))
            pair = da[:, LANES:]
            lone = pltpu.roll(da[:, :LANES], HD, 1)
            zero = jnp.zeros_like(pair)
            views = (
                jnp.where(low_half, pair, zero),
                jnp.where(low_half, zero, pair),
                jnp.where(low_half, lone, zero),
            )
            for hh in range(3):
                h = 3 * s + hh
                v = views[hh].astype(BF16)
                GP[0, at, h * LANES : (h + 1) * LANES] = v
                vt = v.T
                TT[h * LANES : (h + 1) * LANES, at] = vt
                part = vt[HD:] if hh == 1 else vt[:HD]
                DEL[h, :, at] = colsum(part.astype(F32) * ATTT[h, :, at].astype(F32))
        return 0

    lax.fori_loop(0, 4, att_grad, 0)
    n_x.wait_recv()
    NS[1] = NS[0] + NR[1]
    n_y = rc(NS.at[1], NR.at[2], dev_y)
    q2(LAST)

    def attend_back(s, first, heads):
        def head(hh, _):
            h = 3 * s + hh
            DKA[...] = jnp.zeros_like(DKA)
            DVA[...] = jnp.zeros_like(DVA)
            hl = head_lanes(h)

            def step(qb, _):
                at = at_quarter(qb)
                p = jnp.exp(scores_of(s, hh, h, at) - LSE[h, :, at])
                dpt = mm(PK[s, 2 + 2 * lax.div(hh, 2)], TT[hl, at])
                ds = (p * (dpt - DEL[h, :, at])).astype(BF16)
                DVA[...] += mm(p.astype(BF16), GP[0, at, hl])
                DKA[...] += mm(ds, PK[s, 3 * lax.div(hh, 2), at, :])
                dq = mm(KT[h], ds) * 0.125
                a, b = dq[: HD // 2], dq[HD // 2 :]
                cos, sin = COSF[:, at], SINF[:, at]
                VT[h, : HD // 2, at] = (a * cos + b * sin).astype(BF16)
                VT[h, HD // 2 :, at] = (b * cos - a * sin).astype(BF16)
                return 0

            lax.fori_loop(0, 4, step, 0)

            def finish(i, _):
                at = at_quarter(i)
                dk = DKA[at, :] * 0.125
                UP[0, at, hl] = (dk * COSL[at, :] - swap(dk) * SINL[at, :]).astype(BF16)
                GP[0, at, hl] = DVA[at, :].astype(BF16)
                return 0

            lax.fori_loop(0, 4, finish, 0)
            return 0

        lax.fori_loop(first, first + heads, head, 0)

    def join_heads(s):
        def gather(i, _):
            at = at_quarter(i)

            def part(ref, hh):
                h = 3 * s + hh
                return ref[0, at, h * LANES : (h + 1) * LANES].astype(F32)

            dq0 = jnp.concatenate([VT[3 * s, :, at], VT[3 * s + 1, :, at]], axis=0).T
            dq2 = jnp.concatenate([VT[3 * s + 2, :, at]] * 2, axis=0).T
            dk2 = pltpu.roll(part(UP, 2), HD, 1)
            dv2 = part(GP, 2)
            RR[s, at, 0:LANES] = dq0
            RR[s, at, LANES : 2 * LANES] = jnp.where(low_half, part(UP, 0), part(UP, 1)).astype(BF16)
            RR[s, at, 2 * LANES : 3 * LANES] = jnp.where(
                low_half, part(GP, 0), part(GP, 1)
            ).astype(BF16)
            RR[s, at, 3 * LANES : 4 * LANES] = jnp.where(low_half, dq2.astype(F32), dk2).astype(BF16)
            RR[s, at, 4 * LANES : 5 * LANES] = jnp.where(
                low_half, dv2, jnp.zeros_like(dv2)
            ).astype(BF16)
            return 0

        lax.fori_loop(0, 4, gather, 0)

    def in_grad(s):
        block = NY * rows

        def step(j, _):
            at = pl.ds(pl.multiple_of(j * block, block), block)
            part = mm(XT[at, :], RR[s, :, : 5 * LANES])
            mixed = slots[0][s, j, :, :, 4 * LANES : 5 * LANES].reshape(block, LANES)
            mixed = (part[:, 4 * LANES :] + mixed.astype(F32)).astype(BF16)
            slots[0][s, j, :, :, : 4 * LANES] = (
                part[:, : 4 * LANES].astype(BF16).reshape(NY, rows, 4 * LANES)
            )
            slots[0][s, j, :, :, 4 * LANES : 5 * LANES] = mixed.reshape(NY, rows, LANES)
            return 0

        lax.fori_loop(0, nz, step, 0)

    attend_back(1, 0, 1)
    r2(2)
    r3(1)
    attend_back(1, 1, 2)
    q3(LAST)
    r4(3)
    join_heads(1)
    in_grad(1)
    r1_far(0)
    n_y.wait_recv()
    NS[2] = NS[1] + NR[2]
    NZR[z] = NS[2]
    n_z = [rc(NS.at[2], NZR.at[z], dev_z[j]) for j in range(1, nz)]
    attend_back(0, 0, 2)
    r3(2)
    q4(LAST)
    attend_back(0, 2, 1)
    join_heads(0)
    in_grad(0)
    r1_near(0)
    r2(0)
    r4(1)

    def input_part(i):
        at = at_quarter(i)
        return mt(RR[0, at, : 5 * LANES], wmat(0, 0, 0, 5 * LANES)) + mt(
            RR[1, at, : 5 * LANES], wmat(0, 1, 0, 5 * LANES)
        )

    exchange(3, input_part)

    def input_grad(k, i, at):
        g = DZ[k, at, :] + ACC[k, at, :] + CXR[1, k, at, :].astype(F32)
        OB[1, k, at, :] = g.astype(BF16)

    over_tiles(input_grad)
    i_far = rc(OB.at[1, 1 - xi], gin_h.at[xi], dev_x)
    i_own = lc(OB.at[1, xi], gin_h.at[xi])
    r4(2)
    for copy in n_z:
        copy.wait_recv()
    total = NZR[0]
    for j in range(1, nz):
        total = total + NZR[j]
    ng_out[...] = total
    r3(0)
    r4(0)
    o_far.wait_recv()
    i_far.wait_recv()
    o_own.wait()
    i_own.wait()
    for p in range(5):
        rs[p, "out"].wait()
    for copy in list(sends.values()):
        sent(copy)


def layer_per_device(
    dp_size,
    layer_input,
    cotangent,
    segment_ids,
    query_weight,
    key_weight,
    value_weight,
    output_weight,
    gate_weight,
    up_weight,
    down_weight,
    first_gain,
    first_bias,
    second_gain,
    second_bias,
):
    _, quarter, width = layer_input.shape
    length = 4 * quarter
    rows = query_weight.shape[0]
    nz = dp_size // NY
    tables = [jnp.asarray(t) for t in lane_tables(length)]
    anywhere = pl.BlockSpec(memory_space=pl.ANY)
    vmem = pl.BlockSpec(memory_space=pltpu.VMEM)
    half = HD // 2
    copies = 134
    part = query_weight.shape[1]
    scratch = [
        ((4, 2, nz, NY, rows, width), BF16),
        ((2, nz, NY, rows, width), BF16),
        ((4, nz // 2, rows, width), BF16),
        ((4, nz - 1, rows, width), BF16),
        ((4, nz, rows, width), BF16),
        ((4, nz, rows, width), BF16),
        ((4, nz, rows, width), BF16),
        ((4, quarter, width), BF16),
        ((width, length), BF16),
        ((width, length), BF16),
        ((width, length), BF16),
        ((2, quarter, width), BF16),
        ((length, LANES), F32),
        ((length, LANES), F32),
        ((length, LANES), F32),
        ((half, length), F32),
        ((half, length), F32),
        ((2, 5, length, LANES), BF16),
        ((6, LANES, length), BF16),
        ((6, HD, length), BF16),
        ((6, HD, length), BF16),
        ((6, 1, length), F32),
        ((6, 1, length), F32),
        ((2, length, 2 * LANES), BF16),
        ((6, HD, length), BF16),
        ((2, quarter, width), F32),
        ((2, quarter, LANES), F32),
        ((4, quarter, width), BF16),
        ((2, length, width), BF16),
        ((2, length, width), BF16),
        ((2, length, width), BF16),
        ((2, quarter, width), F32),
        ((2, quarter, width), BF16),
        ((2, 2, quarter, width), BF16),
        ((2, quarter, width), F32),
        ((2, 2, quarter, width), BF16),
        ((length, LANES), F32),
        ((length, LANES), F32),
        ((2, length), jnp.int32),
        ((rows, part), BF16),
        ((rows, part), BF16),
        ((rows, part), BF16),
        ((part, rows), BF16),
        ((4, 1, width), F32),
        ((8, width), F32),
        ((3, 8, width), F32),
        ((3, 8, width), F32),
        ((nz, 8, width), F32),
        ((nz, 2, NY, rows, width // 2), BF16),
    ]
    outputs, grad_input, grads, norms = pl.pallas_call(
        functools.partial(layer_kernel, nz),
        out_shape=(
            jax.ShapeDtypeStruct(layer_input.shape, BF16),
            jax.ShapeDtypeStruct(layer_input.shape, BF16),
            jax.ShapeDtypeStruct((4, rows, width), F32),
            jax.ShapeDtypeStruct((8, width), F32),
        ),
        in_specs=[anywhere] * 18,
        out_specs=(anywhere, anywhere, anywhere, vmem),
        scratch_shapes=[pltpu.VMEM(shape, kind) for shape, kind in scratch]
        + [
            pltpu.SemaphoreType.DMA((25,)),
            pltpu.SemaphoreType.DMA((copies,)),
            pltpu.SemaphoreType.DMA((copies,)),
        ],
        compiler_params=pltpu.CompilerParams(
            collective_id=0, has_side_effects=True, vmem_limit_bytes=VMEM_BYTES
        ),
    )(
        layer_input,
        cotangent,
        segment_ids,
        query_weight,
        key_weight,
        value_weight,
        output_weight,
        gate_weight,
        up_weight,
        down_weight.T,
        first_gain,
        first_bias,
        second_gain,
        second_bias,
        *tables,
    )
    vector = jax.ShapeDtypeStruct((width,), F32)
    like = lambda a: jax.ShapeDtypeStruct(a.shape, F32)
    results = pl.pallas_call(
        place_kernel,
        out_shape=(
            jax.ShapeDtypeStruct(layer_input.shape, BF16),
            jax.ShapeDtypeStruct(layer_input.shape, BF16),
            like(query_weight),
            like(key_weight),
            like(value_weight),
            like(output_weight),
            like(gate_weight),
            like(up_weight),
            jax.ShapeDtypeStruct(down_weight.shape[::-1], F32),
            vector,
            vector,
            vector,
            vector,
        ),
        in_specs=[anywhere] * 4,
        out_specs=(anywhere, anywhere) + (vmem,) * 4 + (anywhere,) * 3 + (vmem,) * 4,
        scratch_shapes=[
            pltpu.VMEM(layer_input.shape, BF16),
            pltpu.VMEM(layer_input.shape, BF16),
            pltpu.VMEM((4, rows, width), F32),
            pltpu.VMEM((8, width), F32),
            pltpu.SemaphoreType.DMA((7,)),
            pltpu.SemaphoreType.DMA((5,)),
        ],
        compiler_params=pltpu.CompilerParams(vmem_limit_bytes=VMEM_BYTES),
    )(outputs, grad_input, grads, norms)
    return (*results[:8], results[8].T, *results[9:])


def place_kernel(
    out_i,
    gin_i,
    gw,
    ng,
    out_o,
    gin_o,
    gq,
    gk,
    gv,
    go,
    gg,
    gu,
    gd,
    n0,
    n1,
    n2,
    n3,
    OUT,
    GIN,
    GW,
    NB,
    sem,
    osem,
):
    loads = [
        pltpu.make_async_copy(src, dst, sem.at[i])
        for i, (src, dst) in enumerate(
            [
                (gw.at[0], GW.at[0]),
                (ng, NB),
                (gw.at[1], GW.at[1]),
                (gw.at[2], GW.at[2]),
                (gw.at[3], GW.at[3]),
                (out_i, OUT),
                (gin_i, GIN),
            ]
        )
    ]
    for copy in loads:
        copy.start()
    stores = [
        pltpu.make_async_copy(src, dst, osem.at[i])
        for i, (src, dst) in enumerate(
            [(GW.at[1], gg), (GW.at[2], gu), (GW.at[3], gd), (OUT, out_o), (GIN, gin_o)]
        )
    ]
    for load, store in zip(loads[2:], stores):
        load.wait()
        store.start()
    loads[0].wait()
    two = 2 * HD
    b = [GW[0, :, i * two : (i + 1) * two] for i in range(6)]
    gq[...] = jnp.concatenate([b[0], b[3][:, :HD]], axis=1)
    gk[...] = jnp.concatenate([b[1], b[3][:, HD:]], axis=1)
    gv[...] = jnp.concatenate([b[2], b[4][:, :HD]], axis=1)
    go[...] = jnp.concatenate([b[5], b[4][:, HD:]], axis=1).T
    loads[1].wait()
    for i, n in enumerate((n0, n1, n2, n3)):
        n[...] = NB[i, :]
    for store in stores:
        store.wait()


VMEM_BYTES = 64 << 20


def solution(mesh):
    in_specs = (
        P("dp", "tensor", None),
        P("dp", "tensor", None),
        P("dp", None),
        P("dp", "tensor"),
        P("dp", "tensor"),
        P("dp", "tensor"),
        P("tensor", "dp"),
        P("dp", "tensor"),
        P("dp", "tensor"),
        P("tensor", "dp"),
        P(),
        P(),
        P(),
        P(),
    )
    out_specs = (
        P("dp", "tensor", None),
        P("dp", "tensor", None),
        P("dp", "tensor"),
        P("dp", "tensor"),
        P("dp", "tensor"),
        P("tensor", "dp"),
        P("dp", "tensor"),
        P("dp", "tensor"),
        P("tensor", "dp"),
        P(),
        P(),
        P(),
        P(),
    )
    dp_size, tensor_size = mesh.shape["dp"], mesh.shape["tensor"]

    def whole(*arrays):
        layer_input, query_weight, gate_weight = arrays[0], arrays[3], arrays[7]
        batch, length, width = layer_input.shape
        fits = (
            tensor_size == 4
            and dp_size % (2 * NY) == 0
            and batch == 2 * dp_size
            and width % (16 * dp_size) == 0
            and query_weight.shape[1] == 12 * HD
            and query_weight.shape[1] == width
            and gate_weight.shape[1] == 4 * width
            and length % 1024 == 0
        )
        program = functools.partial(layer_per_device, dp_size) if fits else per_device
        return jax.shard_map(
            program, mesh=mesh, in_specs=in_specs, out_specs=out_specs, check_vma=False
        )(*arrays)

    return whole
```

```python
import functools

import jax
import jax.numpy as jnp
import numpy as np
from jax import lax
from jax.experimental import pallas as pl
from jax.experimental.pallas import tpu as pltpu
from jax.sharding import PartitionSpec as P

HD = 64


eps_norm = 1e-06
rope_base = 1000.0
mask_fill = -1e30


def layer_norm(field_rows, gain_vec, bias_vec):
    row_mean = jnp.mean(field_rows, axis=-1, keepdims=True)
    centred = field_rows - row_mean
    variance = jnp.mean(centred * centred, axis=-1, keepdims=True)
    return centred * lax.rsqrt(variance + eps_norm) * gain_vec + bias_vec


def rotary_tables(length, head_dim):
    half_dim = head_dim // 2
    frequency = rope_base ** (-(2.0 * jnp.arange(half_dim, dtype=jnp.float32)) / head_dim)
    angles = jnp.arange(length, dtype=jnp.float32)[:, None] * frequency[None, :]
    return (jnp.cos(angles), jnp.sin(angles))


def rotate(heads_data, cos_table, sine_table):
    half_dim = heads_data.shape[-1] // 2
    first_half = heads_data[..., :half_dim]
    second_half = heads_data[..., half_dim:]
    cos_part = cos_table[:, None, :]
    sine_part = sine_table[:, None, :]
    return jnp.concatenate(
        [
            first_half * cos_part - second_half * sine_part,
            second_half * cos_part + first_half * sine_part,
        ],
        axis=-1,
    )


def swiglu(gate_pre, up_pre):
    return jax.nn.silu(gate_pre) * up_pre


def contract_rows(left, right):
    return lax.dot_general(
        left, right, (((0,), (0,)), ((), ())), preferred_element_type=jnp.float32
    )


def times_transpose(left, right):
    return lax.dot_general(
        left, right, (((1,), (1,)), ((), ())), preferred_element_type=jnp.float32
    )


def per_device(
    layer_input,
    cotangent,
    segment_ids,
    query_weight,
    key_weight,
    value_weight,
    output_weight,
    gate_weight,
    up_weight,
    down_weight,
    first_gain,
    first_bias,
    second_gain,
    second_bias,
):
    model_width = layer_input.shape[2]
    length = segment_ids.shape[1]
    block_rows = min(512, length)
    block_count = length // block_rows
    local_heads = query_weight.shape[1] // HD
    local_width = local_heads * HD
    score_scale = HD ** (-0.5)
    cos_table, sine_table = rotary_tables(length, HD)

    def fetch_weights():
        row_parts = (
            lax.all_gather(query_weight, "dp", axis=0, tiled=True),
            lax.all_gather(key_weight, "dp", axis=0, tiled=True),
            lax.all_gather(value_weight, "dp", axis=0, tiled=True),
            lax.all_gather(gate_weight, "dp", axis=0, tiled=True),
            lax.all_gather(up_weight, "dp", axis=0, tiled=True),
        )
        col_parts = (
            lax.all_gather(output_weight, "dp", axis=1, tiled=True),
            lax.all_gather(down_weight, "dp", axis=1, tiled=True),
        )
        return tuple(row_parts) + tuple(col_parts)

    def micro_step(weights, row_input, row_cotangent, segment_row):
        query_full, key_full, value_full, gate_full, up_full, output_full, down_full = weights
        full_input = lax.all_gather(row_input, "tensor", axis=0, tiled=True)
        query_pre = jnp.dot(full_input, query_full, preferred_element_type=jnp.float32).reshape(
            length, local_heads, HD
        )
        key_pre = jnp.dot(full_input, key_full, preferred_element_type=jnp.float32).reshape(
            length, local_heads, HD
        )
        value_rows = (
            jnp.dot(full_input, value_full, preferred_element_type=jnp.float32)
            .astype(jnp.bfloat16)
            .reshape(length, local_heads, HD)
        )
        query_rows = rotate(query_pre, cos_table, sine_table).astype(jnp.bfloat16)
        key_rows = rotate(key_pre, cos_table, sine_table).astype(jnp.bfloat16)
        query_blocks = query_rows.reshape(block_count, block_rows, local_heads, HD)
        segment_blocks = segment_row.reshape(block_count, block_rows)

        def block_scores(query_block, segment_block):
            scores = (
                jnp.einsum(
                    "qhd,khd->hqk", query_block, key_rows, preferred_element_type=jnp.float32
                )
                * score_scale
            )
            allowed = segment_block[:, None] == segment_row[None, :]
            return jnp.where(allowed[None, :, :], scores, mask_fill)

        def attend_forward(block_inputs):
            scores = block_scores(block_inputs[0], block_inputs[1])
            row_max = jnp.max(scores, axis=-1, keepdims=True)
            exponent_terms = jnp.exp(scores - row_max)
            row_total = jnp.sum(exponent_terms, axis=-1, keepdims=True)
            probabilities = (exponent_terms / row_total).astype(jnp.bfloat16)
            mixed_rows = jnp.einsum(
                "hqk,khd->qhd", probabilities, value_rows, preferred_element_type=jnp.float32
            )
            return (mixed_rows, (row_max + jnp.log(row_total))[..., 0])

        mixed_blocks, log_totals = lax.map(attend_forward, (query_blocks, segment_blocks))
        attended = mixed_blocks.reshape(length, local_width).astype(jnp.bfloat16)
        attention_branch = lax.psum_scatter(
            jnp.dot(attended, output_full, preferred_element_type=jnp.float32).astype(jnp.bfloat16),
            "tensor",
            scatter_dimension=0,
            tiled=True,
        ).astype(jnp.float32)
        first_sum = row_input.astype(jnp.float32) + attention_branch
        hidden_state, first_back = jax.vjp(layer_norm, first_sum, first_gain, first_bias)
        full_hidden = lax.all_gather(
            hidden_state.astype(jnp.bfloat16), "tensor", axis=0, tiled=True
        )
        gate_pre = jnp.dot(full_hidden, gate_full, preferred_element_type=jnp.float32)
        up_pre = jnp.dot(full_hidden, up_full, preferred_element_type=jnp.float32)
        activated_exact, swiglu_back = jax.vjp(swiglu, gate_pre, up_pre)
        activated = activated_exact.astype(jnp.bfloat16)
        feed_branch = lax.psum_scatter(
            jnp.dot(activated, down_full, preferred_element_type=jnp.float32).astype(jnp.bfloat16),
            "tensor",
            scatter_dimension=0,
            tiled=True,
        ).astype(jnp.float32)
        layer_output, second_back = jax.vjp(
            layer_norm, hidden_state + feed_branch, second_gain, second_bias
        )
        grad_second_sum, grad_second_gain, grad_second_bias = second_back(
            row_cotangent.astype(jnp.float32)
        )
        grad_second_full = lax.all_gather(
            grad_second_sum.astype(jnp.bfloat16), "tensor", axis=0, tiled=True
        )
        grad_activated = times_transpose(grad_second_full, down_full)
        grad_down = contract_rows(activated, grad_second_full)
        grad_gate_pre, grad_up_pre = swiglu_back(grad_activated)
        gate_low = grad_gate_pre.astype(jnp.bfloat16)
        up_low = grad_up_pre.astype(jnp.bfloat16)
        grad_hidden = grad_second_sum + lax.psum_scatter(
            (times_transpose(gate_low, gate_full) + times_transpose(up_low, up_full)).astype(
                jnp.bfloat16
            ),
            "tensor",
            scatter_dimension=0,
            tiled=True,
        ).astype(jnp.float32)
        grad_gate = contract_rows(full_hidden, gate_low)
        grad_up = contract_rows(full_hidden, up_low)
        grad_first_sum, grad_first_gain, grad_first_bias = first_back(grad_hidden)
        grad_first_full = lax.all_gather(
            grad_first_sum.astype(jnp.bfloat16), "tensor", axis=0, tiled=True
        )
        grad_attended = (
            times_transpose(grad_first_full, output_full)
            .astype(jnp.bfloat16)
            .reshape(block_count, block_rows, local_heads, HD)
        )
        grad_output = contract_rows(attended, grad_first_full)

        def attend_backward(sums_carry, block_inputs):
            key_sum, value_sum = sums_carry
            query_block, segment_block, log_block, grad_block = block_inputs
            scores = block_scores(query_block, segment_block)
            probabilities = jnp.exp(scores - log_block[..., None])
            grad_softmax = jnp.einsum(
                "qhd,khd->hqk", grad_block, value_rows, preferred_element_type=jnp.float32
            )
            value_sum = value_sum + jnp.einsum(
                "hqk,qhd->khd",
                probabilities.astype(jnp.bfloat16),
                grad_block,
                preferred_element_type=jnp.float32,
            )
            row_inner = jnp.sum(probabilities * grad_softmax, axis=-1, keepdims=True)
            grad_scores = (probabilities * (grad_softmax - row_inner)).astype(jnp.bfloat16)
            grad_query_block = (
                jnp.einsum(
                    "hqk,khd->qhd", grad_scores, key_rows, preferred_element_type=jnp.float32
                )
                * score_scale
            )
            key_sum = (
                key_sum
                + jnp.einsum(
                    "hqk,qhd->khd", grad_scores, query_block, preferred_element_type=jnp.float32
                )
                * score_scale
            )
            return ((key_sum, value_sum), grad_query_block)

        zero_heads = jnp.zeros((length, local_heads, HD), jnp.float32)
        (grad_key_rot, grad_value_rows), grad_query_blocks = lax.scan(
            attend_backward,
            (zero_heads, zero_heads),
            (query_blocks, segment_blocks, log_totals, grad_attended),
        )
        grad_query_low = (
            rotate(grad_query_blocks.reshape(length, local_heads, HD), cos_table, -sine_table)
            .astype(jnp.bfloat16)
            .reshape(length, local_width)
        )
        grad_key_low = (
            rotate(grad_key_rot, cos_table, -sine_table)
            .astype(jnp.bfloat16)
            .reshape(length, local_width)
        )
        grad_value_low = grad_value_rows.astype(jnp.bfloat16).reshape(length, local_width)
        query_part = times_transpose(grad_query_low, query_full)
        key_part = times_transpose(grad_key_low, key_full)
        value_part = times_transpose(grad_value_low, value_full)
        grad_input = grad_first_sum + lax.psum_scatter(
            (query_part + key_part + value_part).astype(jnp.bfloat16),
            "tensor",
            scatter_dimension=0,
            tiled=True,
        ).astype(jnp.float32)
        row_grads = (
            contract_rows(full_input, grad_query_low),
            contract_rows(full_input, grad_key_low),
            contract_rows(full_input, grad_value_low),
            grad_gate,
            grad_up,
        )
        col_grads = (grad_output, grad_down)
        norm_parts = (grad_first_gain, grad_first_bias, grad_second_gain, grad_second_bias)
        return (
            layer_output.astype(jnp.bfloat16),
            grad_input.astype(jnp.bfloat16),
            (row_grads, col_grads, norm_parts),
        )

    norm_zero = tuple(
        (
            jnp.zeros(gain_like.shape, jnp.float32)
            for gain_like in (first_gain, first_bias, second_gain, second_bias)
        )
    )
    row_zero = tuple(
        (
            jnp.zeros((model_width, weight_part.shape[1]), jnp.float32)
            for weight_part in (query_weight, key_weight, value_weight, gate_weight, up_weight)
        )
    )
    col_zero = (
        jnp.zeros((output_weight.shape[0], model_width), jnp.float32),
        jnp.zeros((down_weight.shape[0], model_width), jnp.float32),
    )

    def scan_step(totals, batch_rows):
        weights = fetch_weights()
        layer_output, grad_input, grad_terms = micro_step(
            weights, batch_rows[0], batch_rows[1], batch_rows[2]
        )
        return (jax.tree.map(jnp.add, totals, grad_terms), (layer_output, grad_input))

    totals, (outputs, grad_inputs) = lax.scan(
        scan_step, (row_zero, col_zero, norm_zero), (layer_input, cotangent, segment_ids)
    )
    row_grads, col_grads, norm_parts = totals
    row_done = lax.psum_scatter(row_grads, "dp", scatter_dimension=0, tiled=True)
    col_done = (
        lax.psum_scatter(col_grads[0], "dp", scatter_dimension=1, tiled=True),
        lax.psum_scatter(col_grads[1], "dp", scatter_dimension=1, tiled=True),
    )
    norm_done = lax.psum(norm_parts, ("dp", "tensor"))
    totals = (tuple(row_done), tuple(col_done), tuple(norm_done))
    row_done, col_done, norm_done = totals
    return (
        outputs,
        grad_inputs,
        row_done[0],
        row_done[1],
        row_done[2],
        col_done[0],
        row_done[3],
        row_done[4],
        col_done[1],
        norm_done[0],
        norm_done[1],
        norm_done[2],
        norm_done[3],
    )


F32 = jnp.float32
BF16 = jnp.bfloat16
NY = 2
LANES = 128
MESH = pl.DeviceIdType.MESH


def mm(left, right):
    return lax.dot_general(left, right, (((1,), (0,)), ((), ())), preferred_element_type=F32)


def mt(left, right):
    return lax.dot_general(left, right, (((1,), (1,)), ((), ())), preferred_element_type=F32)


def lane_tables(length):
    half = HD // 2
    steps = np.arange(half, dtype=np.float32)
    frequency = np.float32(rope_base) ** (-(np.float32(2.0) * steps) / np.float32(HD))
    angles = np.arange(length, dtype=np.float32)[:, None] * frequency[None, :]
    angles = angles.astype(np.float32)
    cos, sin = np.cos(angles).astype(np.float32), np.sin(angles).astype(np.float32)
    cos_lane = np.concatenate([cos] * 4, axis=1)
    sin_lane = np.concatenate([-sin, sin, -sin, sin], axis=1)
    return cos_lane, sin_lane, np.ascontiguousarray(cos.T), np.ascontiguousarray(sin.T)


def norm_of(v):
    mu = jnp.mean(v, axis=-1, keepdims=True)
    cen = v - mu
    rstd = lax.rsqrt(jnp.mean(cen * cen, axis=-1, keepdims=True) + eps_norm)
    return cen * rstd, rstd


def grad_of_norm(dn, n, rstd):
    m0 = jnp.mean(dn, axis=-1, keepdims=True)
    m1 = jnp.mean(dn * n, axis=-1, keepdims=True)
    return (dn - m0 - n * m1) * rstd


def colsum(v):
    return jnp.sum(v, axis=0, keepdims=True)


def layer_kernel(
    nz,
    xin,
    cot,
    seg_h,
    wq_h,
    wk_h,
    wv_h,
    wo_h,
    wg_h,
    wu_h,
    wd_h,
    g1_h,
    b1_h,
    g2_h,
    b2_h,
    cosl_h,
    sinl_h,
    cosf_h,
    sinf_h,
    out_h,
    gin_h,
    gw_h,
    ng_out,
    W,
    G,
    S1X,
    S1Y,
    S2X,
    S2Y,
    ZR,
    X,
    XT,
    TT,
    DT,
    CT,
    SC,
    COSL,
    SINL,
    COSF,
    SINF,
    PK,
    QZ,
    KT,
    VT,
    LSE,
    DEL,
    ATT,
    ATTT,
    N1,
    R1,
    F4,
    GP,
    UP,
    RR,
    DZ,
    CXS,
    CXR,
    ACC,
    OB,
    DKA,
    DVA,
    SEG,
    WQ,
    WK,
    WV,
    WO,
    VEC,
    NG,
    NR,
    NS,
    NZR,
    ZB,
    loc,
    ssem,
    rsem,
):
    quarter, width = X.shape[1], X.shape[2]
    length = 4 * quarter
    rows = W.shape[4]
    dp = lax.axis_index("dp")
    tt = lax.axis_index("tensor")
    c = lax.rem(tt, 2)
    xi = lax.div(tt, 2)
    z = lax.div(dp, NY)
    y = lax.rem(dp, NY)
    oy = 1 - y
    t_x = lax.rem(tt + 2, 4)
    dev_x = (dp, t_x)
    dev_c = (dp, tt + 1 - 2 * c)
    dev_y = (dp + 1 - 2 * y, tt)
    zs = [lax.rem(z + j, nz) for j in range(nz)]
    zfrom = [lax.rem(z + nz - j, nz) for j in range(nz)]
    dev_z = [(zs[j] * NY + y, tt) for j in range(nz)]
    hz = nz // 2
    count = [0]
    lcount = [0]
    sends = {}

    def rc(src, dst, dev):
        i = count[0]
        count[0] += 1
        copy = pltpu.make_async_remote_copy(
            src_ref=src,
            dst_ref=dst,
            send_sem=ssem.at[i],
            recv_sem=rsem.at[i],
            device_id=dev,
            device_id_type=MESH,
        )
        copy.start()
        sends[id(copy)] = copy
        return copy

    def sent(copy):
        copy.wait_send()
        del sends[id(copy)]

    def lc(src, dst):
        i = lcount[0]
        lcount[0] += 1
        copy = pltpu.make_async_copy(src, dst, loc.at[i])
        copy.start()
        return copy

    l_out, l_att = lc(wo_h, WO), [lc(wq_h, WQ), lc(wk_h, WK), lc(wv_h, WV)]
    l_w = [lc(wg_h, W.at[1, 0, z, y]), lc(wu_h, W.at[2, 0, z, y]), lc(wd_h, W.at[3, 0, z, y])]
    l_seg = lc(seg_h, SEG)
    l_vec = [lc(h, VEC.at[i, 0]) for i, h in enumerate((g1_h, b1_h, g2_h, b2_h))]
    l_x = lc(xin.at[xi], X.at[tt])
    l_ct = lc(cot.at[xi], CT.at[xi])
    l_tab = [lc(cosl_h, COSL), lc(sinl_h, SINL), lc(cosf_h, COSF), lc(sinf_h, SINF)]

    barrier = pltpu.get_barrier_semaphore()
    peers = [dev_x, dev_c, dev_y] + dev_z[1:]
    for dev in peers:
        pl.semaphore_signal(barrier, inc=1, device_id=dev, device_id_type=MESH)
    l_out.wait()
    for copy in l_att:
        copy.wait()
    shards = [W.at[0, 0, z, y], wg_h, wu_h, wd_h]
    two = 2 * HD
    turned_out = WO[...].T
    shards[0][:, :two] = WQ[:, :two]
    shards[0][:, two : 2 * two] = WK[:, :two]
    shards[0][:, 2 * two : 3 * two] = WV[:, :two]
    shards[0][:, 3 * two : 4 * two] = jnp.concatenate([WQ[:, two:], WK[:, two:]], axis=1)
    shards[0][:, 4 * two : 5 * two] = jnp.concatenate([WV[:, two:], turned_out[:, two:]], axis=1)
    shards[0][:, 5 * two :] = turned_out[:, :two]
    pl.semaphore_wait(barrier, len(peers))

    ag = {}
    split = width // 3
    pieces = [
        (0, 0, width),
        (1, 0, width),
        (2, 0, width),
        (3, 0, split),
        (3, split, width - split),
        (0, 0, 3 * LANES),
        (0, 3 * LANES, 2 * LANES),
        (0, 5 * LANES, LANES),
    ]
    LAST, QKV, REST, OUT = 4, 5, 6, 7

    def cut(view, p):
        _, lo, n = pieces[p]
        return view if n == width else view.at[..., pl.ds(lo, n)]

    def w_at(p, s, zz, yy):
        return cut(W.at[pieces[p][0], s, zz, yy], p)

    def own_shard(p):
        return cut(shards[pieces[p][0]], p)

    def e1_plane(p):
        own = own_shard(p)
        ag[p, "x"] = [rc(own, w_at(p, 1, z, y), dev_x)]
        ag[p, "y"] = [rc(own, w_at(p, 0, z, y), dev_y)]

    def e1(p):
        own = own_shard(p)
        ag[p, "z"] = [rc(own, w_at(p, 0, z, y), dev_z[j]) for j in range(1, nz)]
        e1_plane(p)

    def e2(p):
        for j in range(1, nz):
            ag[p, "z"][j - 1].wait_recv()
            part = w_at(p, 0, zfrom[j], y)
            ag[p, "x"].append(rc(part, w_at(p, 1, zfrom[j], y), dev_x))
            ag[p, "y"].append(rc(part, part, dev_y))

    def e3(p, by_x):
        ag[p, "d"] = []
        for j in range(nz):
            ag[p, "x"][j].wait_recv()
            if j < nz - by_x:
                part = w_at(p, 1, zfrom[j], y)
                ag[p, "d"].append(rc(part, part, dev_y))
            ag[p, "y"][j].wait_recv()
            if j >= nz - by_x:
                ag[p, "d"].append(rc(w_at(p, 0, zfrom[j], oy), w_at(p, 1, zfrom[j], oy), dev_x))

    def e4(p):
        for copy in ag[p, "d"]:
            copy.wait_recv()

    top_rows, low_rows = pl.ds(0, rows // 2), pl.ds(rows // 2, rows // 2)

    def f2(p):
        ag[p, "x"][0].wait_recv()
        part = w_at(p, 1, z, y).at[top_rows]
        ag[p, "d"] = [rc(part, part, dev_y)]
        ag[p, "y"][0].wait_recv()
        ag[p, "d"].append(
            rc(w_at(p, 0, z, oy).at[low_rows], w_at(p, 1, z, oy).at[low_rows], dev_x)
        )

    def f3(p):
        for copy in ag[p, "d"]:
            copy.wait_recv()
        plane = cut(W.at[3, :, z], p)
        ag[p, "z"] = [rc(plane, plane, dev_z[j]) for j in range(1, nz)]

    def f4(p):
        for copy in ag[p, "z"]:
            copy.wait_recv()

    def e_sent(p):
        for copy in ag[p, "z"] + ag[p, "x"] + ag[p, "y"] + ag[p, "d"]:
            sent(copy)

    e1(0)
    e1(3)
    e1_plane(LAST)
    e1(2)
    x_far = rc(xin.at[1 - xi], X.at[tt], dev_x)
    x_core = rc(xin.at[xi], X.at[tt], dev_c)

    l_seg.wait()
    seg = SEG
    g1_ref, b1_ref, g2_ref, b2_ref = (VEC.at[i] for i in range(4))
    SC[...] = jnp.broadcast_to(seg[pl.ds(xi, 1), :].astype(F32), (LANES, length)).T
    NG[...] = jnp.zeros_like(NG)
    lane = lax.broadcasted_iota(jnp.int32, (1, LANES), 1)
    low_half = lane < HD
    swap_low = lax.rem(lane, HD) < (HD // 2)

    def swap(v):
        return jnp.where(swap_low, pltpu.roll(v, LANES - HD // 2, 1), pltpu.roll(v, HD // 2, 1))

    def at_quarter(i):
        return pl.ds(pl.multiple_of(i * quarter, quarter), quarter)

    def wmat(k, s, lo=0, hi=None):
        hi = width if hi is None else hi
        return W[k, s, :, :, :, lo:hi].reshape(width, hi - lo)

    def turn_rows(src, dst):
        def step(i, _):
            dst[:, at_quarter(i)] = src[i].T
            return 0

        lax.fori_loop(0, 4, step, 0)

    f2(LAST)
    e1(1)
    e2(0)
    x_far.wait_recv()
    x_core2 = rc(X.at[t_x], X.at[t_x], dev_c)
    x_core.wait_recv()
    l_x.wait()
    l_ct.wait()
    for copy in l_w + l_vec + l_tab:
        copy.wait()
    x_core2.wait_recv()
    turn_rows(X, XT)
    e2(3)
    f3(LAST)
    e3(0, 1)

    def project(s):
        def step(i, _):
            at = at_quarter(i)
            y5 = mm(X[i], wmat(0, s, 0, 5 * LANES))
            cos, sin = COSL[at, :], SINL[at, :]
            turned = []
            for b in range(5):
                v = y5[:, b * LANES : (b + 1) * LANES]
                if b in (0, 1, 3):
                    v = v * cos + swap(v) * sin
                v = v.astype(BF16)
                PK[s, b, at, :] = v
                turned.append(v.T)
            zero = jnp.zeros((HD, quarter), BF16)
            q0 = turned[0] * BF16(0.125)
            q2 = turned[3] * BF16(0.125)
            QZ[3 * s, :HD, at] = q0[:HD]
            QZ[3 * s, HD:, at] = zero
            QZ[3 * s + 1, :HD, at] = zero
            QZ[3 * s + 1, HD:, at] = q0[HD:]
            QZ[3 * s + 2, :HD, at] = zero
            QZ[3 * s + 2, HD:, at] = q2[:HD]
            KT[3 * s, :, at] = turned[1][:HD]
            KT[3 * s + 1, :, at] = turned[1][HD:]
            KT[3 * s + 2, :, at] = turned[3][HD:]
            VT[3 * s, :, at] = turned[2][:HD]
            VT[3 * s + 1, :, at] = turned[2][HD:]
            VT[3 * s + 2, :, at] = turned[4][:HD]
            return 0

        lax.fori_loop(0, 4, step, 0)

    def scores_of(s, hh, h, at):
        st = mm(PK[s, 1 + 2 * lax.div(hh, 2)], QZ[h, :, at])
        key_seg = jnp.concatenate([SC[...]] * (quarter // LANES), axis=1)
        query_seg = seg[pl.ds(xi, 1), at].astype(F32)
        return jnp.where(key_seg == query_seg, st, mask_fill)

    def attend(first, heads):
        def step(n, _):
            h = first + lax.div(n, 4)
            s, hh = lax.div(h, 3), lax.rem(h, 3)
            at = at_quarter(lax.rem(n, 4))
            st = scores_of(s, hh, h, at)
            top = jnp.max(st, axis=0, keepdims=True)
            p = jnp.exp(st - top)
            total = jnp.sum(p, axis=0, keepdims=True)
            ot = mm(VT[h], p.astype(BF16)) * (1.0 / total)
            LSE[h, :, at] = top + jnp.log(total)
            ATTT[h, :, at] = ot.astype(BF16)
            return 0

        lax.fori_loop(0, 4 * heads, step, 0)

    def turn_heads(s):
        def turn(i, _):
            at = at_quarter(i)
            pair = jnp.concatenate([ATTT[3 * s, :, at], ATTT[3 * s + 1, :, at]], axis=0)
            lone = jnp.concatenate([jnp.zeros((HD, quarter), BF16), ATTT[3 * s + 2, :, at]], axis=0)
            ATT[s, at, :LANES] = lone.T
            ATT[s, at, LANES:] = pair.T
            return 0

        lax.fori_loop(0, 4, turn, 0)

    project(0)
    e2(2)
    e3(3, 1)
    e4(0)
    project(1)
    e2(1)
    attend(0, 2)
    e3(2, 2)
    attend(2, 2)
    e4(3)
    attend(4, 2)
    e3(1, 2)
    turn_heads(0)
    turn_heads(1)
    last_exchange = []

    def exchange(n, part):
        if last_exchange:
            sent(last_exchange.pop())

        def other(k, _):
            CXS[k] = part(1 - c + 2 * k).astype(BF16)
            return 0

        lax.fori_loop(0, 2, other, 0)
        copy = rc(CXS, CXR.at[n % 2], dev_c)
        last_exchange.append(copy)

        def own(k, _):
            ACC[k] = part(c + 2 * k)
            return 0

        lax.fori_loop(0, 2, own, 0)
        copy.wait_recv()

    def spread():
        return [rc(F4.at[c + 2 * k], F4.at[c + 2 * k], dev_c) for k in range(2)]

    def out_part(i):
        at = at_quarter(i)
        return mt(ATT[0, at, :], wmat(0, 0, 4 * LANES)) + mt(ATT[1, at, :], wmat(0, 1, 4 * LANES))

    exchange(0, out_part)
    ct_far = rc(cot.at[1 - xi], CT.at[xi], dev_x)
    tile = quarter // 2

    def over_tiles(fn):
        def step(n, _):
            k = lax.div(n, 2)
            fn(k, c + 2 * k, pl.ds(pl.multiple_of(lax.rem(n, 2) * tile, tile), tile))
            return 0

        lax.fori_loop(0, 4, step, 0)

    def first_norm(k, i, at):
        z1 = X[i, at, :].astype(F32) + ACC[k, at, :] + CXR[0, k, at, :].astype(F32)
        n1, rstd = norm_of(z1)
        N1[k, at, :] = n1
        R1[k, at, :] = jnp.broadcast_to(rstd, (tile, LANES))
        F4[i, at, :] = (n1 * g1_ref[...] + b1_ref[...]).astype(BF16)

    over_tiles(first_norm)
    h_copies = spread()
    for copy in h_copies:
        copy.wait_recv()
    turn_rows(F4, TT)

    def ff_up(s, i):
        at = at_quarter(i)
        g = mm(F4[i], wmat(1, s))
        u = mm(F4[i], wmat(2, s))
        GP[s, at, :] = g.astype(BF16)
        UP[s, at, :] = u.astype(BF16)
        RR[s, at, :] = (g * jax.nn.sigmoid(g) * u).astype(BF16)
        return 0

    lax.fori_loop(0, 4, lambda i, _: ff_up(0, i), 0)
    e4(2)
    e4(1)
    lax.fori_loop(0, 4, lambda i, _: ff_up(1, i), 0)
    f4(LAST)

    def down_part(i):
        at = at_quarter(i)
        return mt(RR[0, at, :], wmat(3, 0)) + mt(RR[1, at, :], wmat(3, 1))

    for copy in h_copies:
        sent(copy)
    exchange(1, down_part)
    ct_far.wait_recv()

    def second_norm(k, i, at):
        h = N1[k, at, :] * g1_ref[...] + b1_ref[...]
        z2 = h + ACC[k, at, :] + CXR[1, k, at, :].astype(F32)
        n2, rstd = norm_of(z2)
        OB[0, k, at, :] = (n2 * g2_ref[...] + b2_ref[...]).astype(BF16)
        dy = CT[k, at, :].astype(F32)
        NG[2:3, :] += colsum(dy * n2)
        NG[3:4, :] += colsum(dy)
        dz = grad_of_norm(dy * g2_ref[...], n2, rstd)
        DZ[k, at, :] = dz
        F4[i, at, :] = dz.astype(BF16)

    over_tiles(second_norm)
    d_copies = spread()
    o_far = rc(OB.at[0, 1 - xi], out_h.at[xi], dev_x)
    o_own = lc(OB.at[0, xi], out_h.at[xi])

    slots = {3: G, 1: W.at[3], 2: W.at[1], 0: W.at[2]}
    rs = {}
    by_x = {1: 1, 2: 2, 3: 1, QKV: 2, REST: 2, OUT: 1}

    def g_at(p, s, zz, yy):
        return cut(slots[pieces[p][0]].at[s, zz, yy], p)

    def into(ref, p, *at):
        return cut(ref.at[(pieces[p][0],) + at], p)

    def plus(target, *others):
        total = target[...].astype(F32)
        for other in others:
            total = total + other[...].astype(F32)
        target[...] = total.astype(BF16)

    def early(p):
        return pl.ds(0, by_x[p]), pl.ds(by_x[p], nz - by_x[p])

    def r1_far(p):
        nx = by_x[p]
        near, far = early(p)
        rs[p, "dx"] = rc(g_at(p, 1, near, oy), into(S1X, p, pl.ds(0, nx)), dev_x)
        rs[p, "dy"] = rc(g_at(p, 1, far, oy), into(S1Y, p, pl.ds(0, nz - nx)), dev_y)
        rs[p, "x0"] = rc(g_at(p, 1, near, y), into(S2X, p, near), dev_x)

    def r1_near(p):
        _, far = early(p)
        rs[p, "y0"] = rc(g_at(p, 0, far, oy), into(S2Y, p, far), dev_y)

    def r2(p):
        nx = by_x[p]
        near, far = early(p)
        rs[p, "dx"].wait_recv()
        for j in range(nx):
            plus(g_at(p, 0, j, oy), into(S1X, p, j))
        rs[p, "y1"] = rc(g_at(p, 0, near, oy), into(S2Y, p, near), dev_y)
        rs[p, "dy"].wait_recv()
        for j in range(nx, nz):
            plus(g_at(p, 1, j, y), into(S1Y, p, j - nx))
        rs[p, "x1"] = rc(g_at(p, 1, far, y), into(S2X, p, far), dev_x)

    def r3(p):
        for name in ("x0", "y0", "y1", "x1"):
            rs[p, name].wait_recv()
        for j in range(nz):
            plus(g_at(p, 0, j, y), into(S2X, p, j), into(S2Y, p, j))
        rs[p, "z"] = [rc(g_at(p, 0, zs[j], y), into(ZR, p, z), dev_z[j]) for j in range(1, nz)]

    def place(p):
        k = pieces[p][0]
        return cut(N1.at[k // 2, pl.ds((k % 2) * rows, rows)], p)

    def r4(p):
        for copy in rs[p, "z"]:
            copy.wait_recv()
        total = g_at(p, 0, z, y)[...].astype(F32)
        for j in range(1, nz):
            total = total + into(ZR, p, zfrom[j])[...].astype(F32)
        target = place(p)
        target[...] = total
        rs[p, "out"] = lc(target, cut(gw_h.at[pieces[p][0]], p))

    def q1(p):
        rs[p, "z"] = [
            rc(cut(slots[3].at[:, zs[j]], p), ZB.at[z], dev_z[j]) for j in range(1, nz)
        ]

    def q2(p):
        for copy in rs[p, "z"]:
            copy.wait_recv()
        for s in range(2):
            for yy in range(NY):
                plus(g_at(p, s, z, yy), *(ZB.at[zfrom[j], s, yy] for j in range(1, nz)))
        rs[p, "dx"] = rc(g_at(p, 1, z, oy).at[top_rows], into(S1X, p, 0).at[top_rows], dev_x)
        rs[p, "dy"] = rc(g_at(p, 1, z, oy).at[low_rows], into(S1Y, p, 0).at[low_rows], dev_y)
        rs[p, "x0"] = rc(g_at(p, 1, z, y).at[top_rows], into(S2X, p, 0).at[top_rows], dev_x)
        rs[p, "y0"] = rc(g_at(p, 0, z, oy).at[low_rows], into(S2Y, p, 0).at[low_rows], dev_y)

    def q3(p):
        rs[p, "dx"].wait_recv()
        plus(g_at(p, 0, z, oy).at[top_rows], into(S1X, p, 0).at[top_rows])
        rs[p, "y1"] = rc(g_at(p, 0, z, oy).at[top_rows], into(S2Y, p, 0).at[top_rows], dev_y)
        rs[p, "dy"].wait_recv()
        plus(g_at(p, 1, z, y).at[low_rows], into(S1Y, p, 0).at[low_rows])
        rs[p, "x1"] = rc(g_at(p, 1, z, y).at[low_rows], into(S2X, p, 0).at[low_rows], dev_x)

    def q4(p):
        for name in ("x0", "y0", "y1", "x1"):
            rs[p, name].wait_recv()
        total = g_at(p, 0, z, y)[...].astype(F32)
        total = total + into(S2X, p, 0)[...].astype(F32) + into(S2Y, p, 0)[...].astype(F32)
        target = place(p)
        target[...] = total
        rs[p, "out"] = lc(target, cut(gw_h.at[3], p))

    def weight_grad(p, s, left, right):
        k, lo, n = pieces[p]
        block = NY * rows

        def step(j, _):
            at = pl.ds(pl.multiple_of(j * block, block), block)
            part = mm(left[at, :], right[s, :, lo : lo + n]).astype(BF16)
            slots[k][s, j, :, :, lo : lo + n] = part.reshape(NY, rows, n)
            return 0

        lax.fori_loop(0, nz, step, 0)


    def turn_half(first):
        def step(k, _):
            i = first + 2 * k
            DT[:, at_quarter(i)] = F4[i].T
            return 0

        lax.fori_loop(0, 2, step, 0)

    turn_half(c)
    for copy in d_copies:
        copy.wait_recv()
    turn_half(1 - c)
    weight_grad(LAST, 0, DT, RR)
    weight_grad(LAST, 1, DT, RR)
    q1(LAST)
    weight_grad(3, 1, DT, RR)
    weight_grad(3, 0, DT, RR)
    r1_far(3)
    r1_near(3)

    def ff_back(n, _):
        s = lax.div(n, 4)
        i = lax.rem(n, 4)
        at = at_quarter(i)
        dr = mm(F4[i], wmat(3, s))
        g = GP[s, at, :].astype(F32)
        u = UP[s, at, :].astype(F32)
        sg = jax.nn.sigmoid(g)
        GP[s, at, :] = (dr * u * sg * (1.0 + g * (1.0 - sg))).astype(BF16)
        UP[s, at, :] = (dr * g * sg).astype(BF16)
        return 0

    lax.fori_loop(0, 8, ff_back, 0)
    e_sent(3)
    e_sent(LAST)
    weight_grad(1, 1, TT, GP)
    r1_far(1)
    weight_grad(1, 0, TT, GP)
    r2(3)

    def hidden_part(i):
        at = at_quarter(i)
        return (
            mt(GP[0, at, :], wmat(1, 0))
            + mt(UP[0, at, :], wmat(2, 0))
            + mt(GP[1, at, :], wmat(1, 1))
            + mt(UP[1, at, :], wmat(2, 1))
        )

    for copy in d_copies:
        sent(copy)
    exchange(2, hidden_part)

    def first_norm_back(k, i, at):
        dh = DZ[k, at, :] + ACC[k, at, :] + CXR[0, k, at, :].astype(F32)
        n1 = N1[k, at, :]
        NG[0:1, :] += colsum(dh * n1)
        NG[1:2, :] += colsum(dh)
        dz = grad_of_norm(dh * g1_ref[...], n1, R1[k, at, :1])
        DZ[k, at, :] = dz
        F4[i, at, :] = dz.astype(BF16)

    over_tiles(first_norm_back)
    b_copies = spread()
    n_core = rc(NG, NR.at[0], dev_c)
    e_sent(1)
    e_sent(2)
    r1_near(1)
    weight_grad(2, 1, TT, UP)
    r2(1)
    weight_grad(2, 0, TT, UP)
    for copy in b_copies:
        copy.wait_recv()
    n_core.wait_recv()
    NS[0] = NG[...] + NR[0]
    n_x = rc(NS.at[0], NR.at[1], dev_x)
    turn_rows(F4, DT)
    r1_far(2)
    def out_grad(n, _):
        s = lax.div(n, nz)
        j = lax.rem(n, nz)
        block = NY * rows
        at = pl.ds(pl.multiple_of(j * block, block), block)
        part = mm(DT[at, :], ATT[s]).astype(BF16)
        slots[0][s, j, :, :, 4 * LANES :] = part.reshape(NY, rows, 2 * LANES)
        return 0

    lax.fori_loop(0, 2 * nz, out_grad, 0)

    def head_lanes(h):
        return pl.ds(pl.multiple_of(h * LANES, LANES), LANES)

    def att_grad(i, _):
        at = at_quarter(i)
        for s in range(2):
            da = mm(F4[i], wmat(0, s, 4 * LANES))
            pair = da[:, LANES:]
            lone = pltpu.roll(da[:, :LANES], HD, 1)
            zero = jnp.zeros_like(pair)
            views = (
                jnp.where(low_half, pair, zero),
                jnp.where(low_half, zero, pair),
                jnp.where(low_half, lone, zero),
            )
            for hh in range(3):
                h = 3 * s + hh
                v = views[hh].astype(BF16)
                GP[0, at, h * LANES : (h + 1) * LANES] = v
                vt = v.T
                TT[h * LANES : (h + 1) * LANES, at] = vt
                part = vt[HD:] if hh == 1 else vt[:HD]
                DEL[h, :, at] = colsum(part.astype(F32) * ATTT[h, :, at].astype(F32))
        return 0

    lax.fori_loop(0, 4, att_grad, 0)
    n_x.wait_recv()
    NS[1] = NS[0] + NR[1]
    n_y = rc(NS.at[1], NR.at[2], dev_y)
    def attend_back(s, first, heads):
        def head(hh, _):
            h = 3 * s + hh
            DKA[...] = jnp.zeros_like(DKA)
            DVA[...] = jnp.zeros_like(DVA)
            hl = head_lanes(h)

            def step(qb, _):
                at = at_quarter(qb)
                p = jnp.exp(scores_of(s, hh, h, at) - LSE[h, :, at])
                dpt = mm(PK[s, 2 + 2 * lax.div(hh, 2)], TT[hl, at])
                ds = (p * (dpt - DEL[h, :, at])).astype(BF16)
                DVA[...] += mm(p.astype(BF16), GP[0, at, hl])
                DKA[...] += mm(ds, PK[s, 3 * lax.div(hh, 2), at, :])
                dq = mm(KT[h], ds) * 0.125
                a, b = dq[: HD // 2], dq[HD // 2 :]
                cos, sin = COSF[:, at], SINF[:, at]
                VT[h, : HD // 2, at] = (a * cos + b * sin).astype(BF16)
                VT[h, HD // 2 :, at] = (b * cos - a * sin).astype(BF16)
                return 0

            lax.fori_loop(0, 4, step, 0)

            def finish(i, _):
                at = at_quarter(i)
                dk = DKA[at, :] * 0.125
                UP[0, at, hl] = (dk * COSL[at, :] - swap(dk) * SINL[at, :]).astype(BF16)
                GP[0, at, hl] = DVA[at, :].astype(BF16)
                return 0

            lax.fori_loop(0, 4, finish, 0)
            return 0

        lax.fori_loop(first, first + heads, head, 0)

    def join_heads(s):
        def gather(i, _):
            at = at_quarter(i)

            def part(ref, hh):
                h = 3 * s + hh
                return ref[0, at, h * LANES : (h + 1) * LANES].astype(F32)

            dq0 = jnp.concatenate([VT[3 * s, :, at], VT[3 * s + 1, :, at]], axis=0).T
            dq2 = jnp.concatenate([VT[3 * s + 2, :, at]] * 2, axis=0).T
            dk2 = pltpu.roll(part(UP, 2), HD, 1)
            dv2 = part(GP, 2)
            RR[s, at, 0:LANES] = dq0
            RR[s, at, LANES : 2 * LANES] = jnp.where(low_half, part(UP, 0), part(UP, 1)).astype(BF16)
            RR[s, at, 2 * LANES : 3 * LANES] = jnp.where(
                low_half, part(GP, 0), part(GP, 1)
            ).astype(BF16)
            RR[s, at, 3 * LANES : 4 * LANES] = jnp.where(low_half, dq2.astype(F32), dk2).astype(BF16)
            RR[s, at, 4 * LANES : 5 * LANES] = jnp.where(
                low_half, dv2, jnp.zeros_like(dv2)
            ).astype(BF16)
            return 0

        lax.fori_loop(0, 4, gather, 0)

    def in_grad(s, p):
        block = NY * rows
        _, lo, n = pieces[p]

        def step(j, _):
            at = pl.ds(pl.multiple_of(j * block, block), block)
            part = mm(XT[at, :], RR[s, :, lo : lo + n])
            if p == REST:
                mixed = slots[0][s, j, :, :, 4 * LANES : 5 * LANES].reshape(block, LANES)
                mixed = (part[:, LANES:] + mixed.astype(F32)).astype(BF16)
                part = part[:, :LANES]
                slots[0][s, j, :, :, 4 * LANES : 5 * LANES] = mixed.reshape(NY, rows, LANES)
                n_out = LANES
            else:
                n_out = n
            slots[0][s, j, :, :, lo : lo + n_out] = part.astype(BF16).reshape(NY, rows, n_out)
            return 0

        lax.fori_loop(0, nz, step, 0)

    attend_back(1, 0, 1)
    r1_near(2)
    r3(3)
    attend_back(1, 1, 1)
    r3(1)
    attend_back(1, 2, 1)
    r2(2)
    join_heads(1)
    r1_far(OUT)
    in_grad(1, QKV)
    r1_far(QKV)
    in_grad(1, REST)
    r1_near(OUT)
    n_y.wait_recv()
    NS[2] = NS[1] + NR[2]
    NZR[z] = NS[2]
    n_z = [rc(NS.at[2], NZR.at[z], dev_z[j]) for j in range(1, nz)]
    attend_back(0, 0, 2)
    r1_far(REST)
    r3(2)
    attend_back(0, 2, 1)
    r2(OUT)
    join_heads(0)
    in_grad(0, QKV)
    r1_near(QKV)
    r2(QKV)
    q2(LAST)
    r4(3)
    in_grad(0, REST)
    r1_near(REST)
    def input_part(i):
        at = at_quarter(i)
        return mt(RR[0, at, : 5 * LANES], wmat(0, 0, 0, 5 * LANES)) + mt(
            RR[1, at, : 5 * LANES], wmat(0, 1, 0, 5 * LANES)
        )

    exchange(3, input_part)

    def input_grad(k, i, at):
        g = DZ[k, at, :] + ACC[k, at, :] + CXR[1, k, at, :].astype(F32)
        OB[1, k, at, :] = g.astype(BF16)

    over_tiles(input_grad)
    r3(OUT)
    r2(REST)
    i_far = rc(OB.at[1, 1 - xi], gin_h.at[xi], dev_x)
    i_own = lc(OB.at[1, xi], gin_h.at[xi])
    r4(1)
    r3(QKV)
    q3(LAST)
    for copy in n_z:
        copy.wait_recv()
    total = NZR[0]
    for j in range(1, nz):
        total = total + NZR[j]
    ng_out[...] = total
    r3(REST)
    r4(OUT)
    r4(2)
    r4(QKV)
    q4(LAST)
    r4(REST)
    o_far.wait_recv()
    i_far.wait_recv()
    o_own.wait()
    i_own.wait()
    for p in (1, 2, 3, LAST, QKV, REST, OUT):
        rs[p, "out"].wait()
    for copy in list(sends.values()):
        sent(copy)


def layer_per_device(
    dp_size,
    layer_input,
    cotangent,
    segment_ids,
    query_weight,
    key_weight,
    value_weight,
    output_weight,
    gate_weight,
    up_weight,
    down_weight,
    first_gain,
    first_bias,
    second_gain,
    second_bias,
):
    _, quarter, width = layer_input.shape
    length = 4 * quarter
    rows = query_weight.shape[0]
    nz = dp_size // NY
    tables = [jnp.asarray(t) for t in lane_tables(length)]
    anywhere = pl.BlockSpec(memory_space=pl.ANY)
    vmem = pl.BlockSpec(memory_space=pltpu.VMEM)
    half = HD // 2
    copies = 152
    part = query_weight.shape[1]
    scratch = [
        ((4, 2, nz, NY, rows, width), BF16),
        ((2, nz, NY, rows, width), BF16),
        ((4, nz // 2, rows, width), BF16),
        ((4, nz - 1, rows, width), BF16),
        ((4, nz, rows, width), BF16),
        ((4, nz, rows, width), BF16),
        ((4, nz, rows, width), BF16),
        ((4, quarter, width), BF16),
        ((width, length), BF16),
        ((width, length), BF16),
        ((width, length), BF16),
        ((2, quarter, width), BF16),
        ((length, LANES), F32),
        ((length, LANES), F32),
        ((length, LANES), F32),
        ((half, length), F32),
        ((half, length), F32),
        ((2, 5, length, LANES), BF16),
        ((6, LANES, length), BF16),
        ((6, HD, length), BF16),
        ((6, HD, length), BF16),
        ((6, 1, length), F32),
        ((6, 1, length), F32),
        ((2, length, 2 * LANES), BF16),
        ((6, HD, length), BF16),
        ((2, quarter, width), F32),
        ((2, quarter, LANES), F32),
        ((4, quarter, width), BF16),
        ((2, length, width), BF16),
        ((2, length, width), BF16),
        ((2, length, width), BF16),
        ((2, quarter, width), F32),
        ((2, quarter, width), BF16),
        ((2, 2, quarter, width), BF16),
        ((2, quarter, width), F32),
        ((2, 2, quarter, width), BF16),
        ((length, LANES), F32),
        ((length, LANES), F32),
        ((2, length), jnp.int32),
        ((rows, part), BF16),
        ((rows, part), BF16),
        ((rows, part), BF16),
        ((part, rows), BF16),
        ((4, 1, width), F32),
        ((8, width), F32),
        ((3, 8, width), F32),
        ((3, 8, width), F32),
        ((nz, 8, width), F32),
        ((nz, 2, NY, rows, width - width // 3), BF16),
    ]
    outputs, grad_input, grads, norms = pl.pallas_call(
        functools.partial(layer_kernel, nz),
        out_shape=(
            jax.ShapeDtypeStruct(layer_input.shape, BF16),
            jax.ShapeDtypeStruct(layer_input.shape, BF16),
            jax.ShapeDtypeStruct((4, rows, width), F32),
            jax.ShapeDtypeStruct((8, width), F32),
        ),
        in_specs=[anywhere] * 18,
        out_specs=(anywhere, anywhere, anywhere, vmem),
        scratch_shapes=[pltpu.VMEM(shape, kind) for shape, kind in scratch]
        + [
            pltpu.SemaphoreType.DMA((27,)),
            pltpu.SemaphoreType.DMA((copies,)),
            pltpu.SemaphoreType.DMA((copies,)),
        ],
        compiler_params=pltpu.CompilerParams(
            collective_id=0, has_side_effects=True, vmem_limit_bytes=VMEM_BYTES
        ),
    )(
        layer_input,
        cotangent,
        segment_ids,
        query_weight,
        key_weight,
        value_weight,
        output_weight,
        gate_weight,
        up_weight,
        down_weight.T,
        first_gain,
        first_bias,
        second_gain,
        second_bias,
        *tables,
    )
    vector = jax.ShapeDtypeStruct((width,), F32)
    like = lambda a: jax.ShapeDtypeStruct(a.shape, F32)
    results = pl.pallas_call(
        place_kernel,
        out_shape=(
            jax.ShapeDtypeStruct(layer_input.shape, BF16),
            jax.ShapeDtypeStruct(layer_input.shape, BF16),
            like(query_weight),
            like(key_weight),
            like(value_weight),
            like(output_weight),
            like(gate_weight),
            like(up_weight),
            jax.ShapeDtypeStruct(down_weight.shape[::-1], F32),
            vector,
            vector,
            vector,
            vector,
        ),
        in_specs=[anywhere] * 4,
        out_specs=(anywhere, anywhere) + (vmem,) * 4 + (anywhere,) * 3 + (vmem,) * 4,
        scratch_shapes=[
            pltpu.VMEM(layer_input.shape, BF16),
            pltpu.VMEM(layer_input.shape, BF16),
            pltpu.VMEM((4, rows, width), F32),
            pltpu.VMEM((8, width), F32),
            pltpu.SemaphoreType.DMA((7,)),
            pltpu.SemaphoreType.DMA((5,)),
        ],
        compiler_params=pltpu.CompilerParams(vmem_limit_bytes=VMEM_BYTES),
    )(outputs, grad_input, grads, norms)
    return (*results[:8], results[8].T, *results[9:])


def place_kernel(
    out_i,
    gin_i,
    gw,
    ng,
    out_o,
    gin_o,
    gq,
    gk,
    gv,
    go,
    gg,
    gu,
    gd,
    n0,
    n1,
    n2,
    n3,
    OUT,
    GIN,
    GW,
    NB,
    sem,
    osem,
):
    loads = [
        pltpu.make_async_copy(src, dst, sem.at[i])
        for i, (src, dst) in enumerate(
            [
                (gw.at[0], GW.at[0]),
                (ng, NB),
                (gw.at[1], GW.at[1]),
                (gw.at[2], GW.at[2]),
                (gw.at[3], GW.at[3]),
                (out_i, OUT),
                (gin_i, GIN),
            ]
        )
    ]
    for copy in loads:
        copy.start()
    stores = [
        pltpu.make_async_copy(src, dst, osem.at[i])
        for i, (src, dst) in enumerate(
            [(GW.at[1], gg), (GW.at[2], gu), (GW.at[3], gd), (OUT, out_o), (GIN, gin_o)]
        )
    ]
    for load, store in zip(loads[2:], stores):
        load.wait()
        store.start()
    loads[0].wait()
    two = 2 * HD
    b = [GW[0, :, i * two : (i + 1) * two] for i in range(6)]
    gq[...] = jnp.concatenate([b[0], b[3][:, :HD]], axis=1)
    gk[...] = jnp.concatenate([b[1], b[3][:, HD:]], axis=1)
    gv[...] = jnp.concatenate([b[2], b[4][:, :HD]], axis=1)
    go[...] = jnp.concatenate([b[5], b[4][:, HD:]], axis=1).T
    loads[1].wait()
    for i, n in enumerate((n0, n1, n2, n3)):
        n[...] = NB[i, :]
    for store in stores:
        store.wait()


VMEM_BYTES = 64 << 20


def solution(mesh):
    in_specs = (
        P("dp", "tensor", None),
        P("dp", "tensor", None),
        P("dp", None),
        P("dp", "tensor"),
        P("dp", "tensor"),
        P("dp", "tensor"),
        P("tensor", "dp"),
        P("dp", "tensor"),
        P("dp", "tensor"),
        P("tensor", "dp"),
        P(),
        P(),
        P(),
        P(),
    )
    out_specs = (
        P("dp", "tensor", None),
        P("dp", "tensor", None),
        P("dp", "tensor"),
        P("dp", "tensor"),
        P("dp", "tensor"),
        P("tensor", "dp"),
        P("dp", "tensor"),
        P("dp", "tensor"),
        P("tensor", "dp"),
        P(),
        P(),
        P(),
        P(),
    )
    dp_size, tensor_size = mesh.shape["dp"], mesh.shape["tensor"]

    def whole(*arrays):
        layer_input, query_weight, gate_weight = arrays[0], arrays[3], arrays[7]
        batch, length, width = layer_input.shape
        fits = (
            tensor_size == 4
            and dp_size % (2 * NY) == 0
            and batch == 2 * dp_size
            and width % (16 * dp_size) == 0
            and query_weight.shape[1] == 12 * HD
            and query_weight.shape[1] == width
            and gate_weight.shape[1] == 4 * width
            and length % 1024 == 0
        )
        program = functools.partial(layer_per_device, dp_size) if fits else per_device
        return jax.shard_map(
            program, mesh=mesh, in_specs=in_specs, out_specs=out_specs, check_vma=False
        )(*arrays)

    return whole
```

```python
import functools

import jax
import jax.numpy as jnp
import numpy as np
from jax import lax
from jax.experimental import pallas as pl
from jax.experimental.pallas import tpu as pltpu
from jax.sharding import PartitionSpec as P

HD = 64


eps_norm = 1e-06
rope_base = 1000.0
mask_fill = -1e30


def layer_norm(field_rows, gain_vec, bias_vec):
    row_mean = jnp.mean(field_rows, axis=-1, keepdims=True)
    centred = field_rows - row_mean
    variance = jnp.mean(centred * centred, axis=-1, keepdims=True)
    return centred * lax.rsqrt(variance + eps_norm) * gain_vec + bias_vec


def rotary_tables(length, head_dim):
    half_dim = head_dim // 2
    frequency = rope_base ** (-(2.0 * jnp.arange(half_dim, dtype=jnp.float32)) / head_dim)
    angles = jnp.arange(length, dtype=jnp.float32)[:, None] * frequency[None, :]
    return (jnp.cos(angles), jnp.sin(angles))


def rotate(heads_data, cos_table, sine_table):
    half_dim = heads_data.shape[-1] // 2
    first_half = heads_data[..., :half_dim]
    second_half = heads_data[..., half_dim:]
    cos_part = cos_table[:, None, :]
    sine_part = sine_table[:, None, :]
    return jnp.concatenate(
        [
            first_half * cos_part - second_half * sine_part,
            second_half * cos_part + first_half * sine_part,
        ],
        axis=-1,
    )


def swiglu(gate_pre, up_pre):
    return jax.nn.silu(gate_pre) * up_pre


def contract_rows(left, right):
    return lax.dot_general(
        left, right, (((0,), (0,)), ((), ())), preferred_element_type=jnp.float32
    )


def times_transpose(left, right):
    return lax.dot_general(
        left, right, (((1,), (1,)), ((), ())), preferred_element_type=jnp.float32
    )


def per_device(
    layer_input,
    cotangent,
    segment_ids,
    query_weight,
    key_weight,
    value_weight,
    output_weight,
    gate_weight,
    up_weight,
    down_weight,
    first_gain,
    first_bias,
    second_gain,
    second_bias,
):
    model_width = layer_input.shape[2]
    length = segment_ids.shape[1]
    block_rows = min(512, length)
    block_count = length // block_rows
    local_heads = query_weight.shape[1] // HD
    local_width = local_heads * HD
    score_scale = HD ** (-0.5)
    cos_table, sine_table = rotary_tables(length, HD)

    def fetch_weights():
        row_parts = (
            lax.all_gather(query_weight, "dp", axis=0, tiled=True),
            lax.all_gather(key_weight, "dp", axis=0, tiled=True),
            lax.all_gather(value_weight, "dp", axis=0, tiled=True),
            lax.all_gather(gate_weight, "dp", axis=0, tiled=True),
            lax.all_gather(up_weight, "dp", axis=0, tiled=True),
        )
        col_parts = (
            lax.all_gather(output_weight, "dp", axis=1, tiled=True),
            lax.all_gather(down_weight, "dp", axis=1, tiled=True),
        )
        return tuple(row_parts) + tuple(col_parts)

    def micro_step(weights, row_input, row_cotangent, segment_row):
        query_full, key_full, value_full, gate_full, up_full, output_full, down_full = weights
        full_input = lax.all_gather(row_input, "tensor", axis=0, tiled=True)
        query_pre = jnp.dot(full_input, query_full, preferred_element_type=jnp.float32).reshape(
            length, local_heads, HD
        )
        key_pre = jnp.dot(full_input, key_full, preferred_element_type=jnp.float32).reshape(
            length, local_heads, HD
        )
        value_rows = (
            jnp.dot(full_input, value_full, preferred_element_type=jnp.float32)
            .astype(jnp.bfloat16)
            .reshape(length, local_heads, HD)
        )
        query_rows = rotate(query_pre, cos_table, sine_table).astype(jnp.bfloat16)
        key_rows = rotate(key_pre, cos_table, sine_table).astype(jnp.bfloat16)
        query_blocks = query_rows.reshape(block_count, block_rows, local_heads, HD)
        segment_blocks = segment_row.reshape(block_count, block_rows)

        def block_scores(query_block, segment_block):
            scores = (
                jnp.einsum(
                    "qhd,khd->hqk", query_block, key_rows, preferred_element_type=jnp.float32
                )
                * score_scale
            )
            allowed = segment_block[:, None] == segment_row[None, :]
            return jnp.where(allowed[None, :, :], scores, mask_fill)

        def attend_forward(block_inputs):
            scores = block_scores(block_inputs[0], block_inputs[1])
            row_max = jnp.max(scores, axis=-1, keepdims=True)
            exponent_terms = jnp.exp(scores - row_max)
            row_total = jnp.sum(exponent_terms, axis=-1, keepdims=True)
            probabilities = (exponent_terms / row_total).astype(jnp.bfloat16)
            mixed_rows = jnp.einsum(
                "hqk,khd->qhd", probabilities, value_rows, preferred_element_type=jnp.float32
            )
            return (mixed_rows, (row_max + jnp.log(row_total))[..., 0])

        mixed_blocks, log_totals = lax.map(attend_forward, (query_blocks, segment_blocks))
        attended = mixed_blocks.reshape(length, local_width).astype(jnp.bfloat16)
        attention_branch = lax.psum_scatter(
            jnp.dot(attended, output_full, preferred_element_type=jnp.float32).astype(jnp.bfloat16),
            "tensor",
            scatter_dimension=0,
            tiled=True,
        ).astype(jnp.float32)
        first_sum = row_input.astype(jnp.float32) + attention_branch
        hidden_state, first_back = jax.vjp(layer_norm, first_sum, first_gain, first_bias)
        full_hidden = lax.all_gather(
            hidden_state.astype(jnp.bfloat16), "tensor", axis=0, tiled=True
        )
        gate_pre = jnp.dot(full_hidden, gate_full, preferred_element_type=jnp.float32)
        up_pre = jnp.dot(full_hidden, up_full, preferred_element_type=jnp.float32)
        activated_exact, swiglu_back = jax.vjp(swiglu, gate_pre, up_pre)
        activated = activated_exact.astype(jnp.bfloat16)
        feed_branch = lax.psum_scatter(
            jnp.dot(activated, down_full, preferred_element_type=jnp.float32).astype(jnp.bfloat16),
            "tensor",
            scatter_dimension=0,
            tiled=True,
        ).astype(jnp.float32)
        layer_output, second_back = jax.vjp(
            layer_norm, hidden_state + feed_branch, second_gain, second_bias
        )
        grad_second_sum, grad_second_gain, grad_second_bias = second_back(
            row_cotangent.astype(jnp.float32)
        )
        grad_second_full = lax.all_gather(
            grad_second_sum.astype(jnp.bfloat16), "tensor", axis=0, tiled=True
        )
        grad_activated = times_transpose(grad_second_full, down_full)
        grad_down = contract_rows(activated, grad_second_full)
        grad_gate_pre, grad_up_pre = swiglu_back(grad_activated)
        gate_low = grad_gate_pre.astype(jnp.bfloat16)
        up_low = grad_up_pre.astype(jnp.bfloat16)
        grad_hidden = grad_second_sum + lax.psum_scatter(
            (times_transpose(gate_low, gate_full) + times_transpose(up_low, up_full)).astype(
                jnp.bfloat16
            ),
            "tensor",
            scatter_dimension=0,
            tiled=True,
        ).astype(jnp.float32)
        grad_gate = contract_rows(full_hidden, gate_low)
        grad_up = contract_rows(full_hidden, up_low)
        grad_first_sum, grad_first_gain, grad_first_bias = first_back(grad_hidden)
        grad_first_full = lax.all_gather(
            grad_first_sum.astype(jnp.bfloat16), "tensor", axis=0, tiled=True
        )
        grad_attended = (
            times_transpose(grad_first_full, output_full)
            .astype(jnp.bfloat16)
            .reshape(block_count, block_rows, local_heads, HD)
        )
        grad_output = contract_rows(attended, grad_first_full)

        def attend_backward(sums_carry, block_inputs):
            key_sum, value_sum = sums_carry
            query_block, segment_block, log_block, grad_block = block_inputs
            scores = block_scores(query_block, segment_block)
            probabilities = jnp.exp(scores - log_block[..., None])
            grad_softmax = jnp.einsum(
                "qhd,khd->hqk", grad_block, value_rows, preferred_element_type=jnp.float32
            )
            value_sum = value_sum + jnp.einsum(
                "hqk,qhd->khd",
                probabilities.astype(jnp.bfloat16),
                grad_block,
                preferred_element_type=jnp.float32,
            )
            row_inner = jnp.sum(probabilities * grad_softmax, axis=-1, keepdims=True)
            grad_scores = (probabilities * (grad_softmax - row_inner)).astype(jnp.bfloat16)
            grad_query_block = (
                jnp.einsum(
                    "hqk,khd->qhd", grad_scores, key_rows, preferred_element_type=jnp.float32
                )
                * score_scale
            )
            key_sum = (
                key_sum
                + jnp.einsum(
                    "hqk,qhd->khd", grad_scores, query_block, preferred_element_type=jnp.float32
                )
                * score_scale
            )
            return ((key_sum, value_sum), grad_query_block)

        zero_heads = jnp.zeros((length, local_heads, HD), jnp.float32)
        (grad_key_rot, grad_value_rows), grad_query_blocks = lax.scan(
            attend_backward,
            (zero_heads, zero_heads),
            (query_blocks, segment_blocks, log_totals, grad_attended),
        )
        grad_query_low = (
            rotate(grad_query_blocks.reshape(length, local_heads, HD), cos_table, -sine_table)
            .astype(jnp.bfloat16)
            .reshape(length, local_width)
        )
        grad_key_low = (
            rotate(grad_key_rot, cos_table, -sine_table)
            .astype(jnp.bfloat16)
            .reshape(length, local_width)
        )
        grad_value_low = grad_value_rows.astype(jnp.bfloat16).reshape(length, local_width)
        query_part = times_transpose(grad_query_low, query_full)
        key_part = times_transpose(grad_key_low, key_full)
        value_part = times_transpose(grad_value_low, value_full)
        grad_input = grad_first_sum + lax.psum_scatter(
            (query_part + key_part + value_part).astype(jnp.bfloat16),
            "tensor",
            scatter_dimension=0,
            tiled=True,
        ).astype(jnp.float32)
        row_grads = (
            contract_rows(full_input, grad_query_low),
            contract_rows(full_input, grad_key_low),
            contract_rows(full_input, grad_value_low),
            grad_gate,
            grad_up,
        )
        col_grads = (grad_output, grad_down)
        norm_parts = (grad_first_gain, grad_first_bias, grad_second_gain, grad_second_bias)
        return (
            layer_output.astype(jnp.bfloat16),
            grad_input.astype(jnp.bfloat16),
            (row_grads, col_grads, norm_parts),
        )

    norm_zero = tuple(
        (
            jnp.zeros(gain_like.shape, jnp.float32)
            for gain_like in (first_gain, first_bias, second_gain, second_bias)
        )
    )
    row_zero = tuple(
        (
            jnp.zeros((model_width, weight_part.shape[1]), jnp.float32)
            for weight_part in (query_weight, key_weight, value_weight, gate_weight, up_weight)
        )
    )
    col_zero = (
        jnp.zeros((output_weight.shape[0], model_width), jnp.float32),
        jnp.zeros((down_weight.shape[0], model_width), jnp.float32),
    )

    def scan_step(totals, batch_rows):
        weights = fetch_weights()
        layer_output, grad_input, grad_terms = micro_step(
            weights, batch_rows[0], batch_rows[1], batch_rows[2]
        )
        return (jax.tree.map(jnp.add, totals, grad_terms), (layer_output, grad_input))

    totals, (outputs, grad_inputs) = lax.scan(
        scan_step, (row_zero, col_zero, norm_zero), (layer_input, cotangent, segment_ids)
    )
    row_grads, col_grads, norm_parts = totals
    row_done = lax.psum_scatter(row_grads, "dp", scatter_dimension=0, tiled=True)
    col_done = (
        lax.psum_scatter(col_grads[0], "dp", scatter_dimension=1, tiled=True),
        lax.psum_scatter(col_grads[1], "dp", scatter_dimension=1, tiled=True),
    )
    norm_done = lax.psum(norm_parts, ("dp", "tensor"))
    totals = (tuple(row_done), tuple(col_done), tuple(norm_done))
    row_done, col_done, norm_done = totals
    return (
        outputs,
        grad_inputs,
        row_done[0],
        row_done[1],
        row_done[2],
        col_done[0],
        row_done[3],
        row_done[4],
        col_done[1],
        norm_done[0],
        norm_done[1],
        norm_done[2],
        norm_done[3],
    )


F32 = jnp.float32
BF16 = jnp.bfloat16
NY = 2
LANES = 128
IDS = 16
MESH = pl.DeviceIdType.MESH


def mm(left, right):
    return lax.dot_general(left, right, (((1,), (0,)), ((), ())), preferred_element_type=F32)


def mt(left, right):
    return lax.dot_general(left, right, (((1,), (1,)), ((), ())), preferred_element_type=F32)


def lane_tables(length):
    half = HD // 2
    steps = np.arange(half, dtype=np.float32)
    frequency = np.float32(rope_base) ** (-(np.float32(2.0) * steps) / np.float32(HD))
    angles = np.arange(length, dtype=np.float32)[:, None] * frequency[None, :]
    angles = angles.astype(np.float32)
    cos, sin = np.cos(angles).astype(np.float32), np.sin(angles).astype(np.float32)
    cos_lane = np.concatenate([cos] * 4, axis=1)
    sin_lane = np.concatenate([-sin, sin, -sin, sin], axis=1)
    return cos_lane, sin_lane, np.ascontiguousarray(cos.T), np.ascontiguousarray(sin.T)


def norm_of(v):
    mu = jnp.mean(v, axis=-1, keepdims=True)
    cen = v - mu
    rstd = lax.rsqrt(jnp.mean(cen * cen, axis=-1, keepdims=True) + eps_norm)
    return cen * rstd, rstd


def grad_of_norm(dn, n, rstd):
    m0 = jnp.mean(dn, axis=-1, keepdims=True)
    m1 = jnp.mean(dn * n, axis=-1, keepdims=True)
    return (dn - m0 - n * m1) * rstd


def colsum(v):
    return jnp.sum(v, axis=0, keepdims=True)


def layer_kernel(
    nz,
    xin,
    cot,
    seg_h,
    wq_h,
    wk_h,
    wv_h,
    wo_h,
    wg_h,
    wu_h,
    wd_h,
    g1_h,
    b1_h,
    g2_h,
    b2_h,
    cosl_h,
    sinl_h,
    cosf_h,
    sinf_h,
    out_h,
    gin_h,
    gw_h,
    ng_out,
    W,
    G,
    S1X,
    S1Y,
    S2X,
    S2Y,
    ZR,
    X,
    XT,
    TT,
    DT,
    CT,
    SEGQ,
    SEGK,
    COSL,
    SINL,
    COSF,
    SINF,
    PK,
    QZ,
    KT,
    VT,
    LSE,
    DEL,
    ATT,
    ATTT,
    N1,
    F4,
    GP,
    UP,
    RR,
    DZ,
    CXS,
    CXR,
    ACC,
    OB,
    DKA,
    DVA,
    SEG,
    WQ,
    WK,
    WV,
    WO,
    VEC,
    NG,
    NR,
    NS,
    NZR,
    ZB,
    loc,
    ssem,
    rsem,
):
    quarter, width = X.shape[1], X.shape[2]
    length = 4 * quarter
    rows = W.shape[4]
    dp = lax.axis_index("dp")
    tt = lax.axis_index("tensor")
    c = lax.rem(tt, 2)
    xi = lax.div(tt, 2)
    z = lax.div(dp, NY)
    y = lax.rem(dp, NY)
    oy = 1 - y
    t_x = lax.rem(tt + 2, 4)
    dev_x = (dp, t_x)
    dev_c = (dp, tt + 1 - 2 * c)
    dev_y = (dp + 1 - 2 * y, tt)
    zs = [lax.rem(z + j, nz) for j in range(nz)]
    zfrom = [lax.rem(z + nz - j, nz) for j in range(nz)]
    dev_z = [(zs[j] * NY + y, tt) for j in range(nz)]
    hz = nz // 2
    count = [0]
    lcount = [0]
    sends = {}

    def rc(src, dst, dev):
        i = count[0]
        count[0] += 1
        copy = pltpu.make_async_remote_copy(
            src_ref=src,
            dst_ref=dst,
            send_sem=ssem.at[i],
            recv_sem=rsem.at[i],
            device_id=dev,
            device_id_type=MESH,
        )
        copy.start()
        sends[id(copy)] = copy
        return copy

    def sent(copy):
        copy.wait_send()
        del sends[id(copy)]

    def lc(src, dst):
        i = lcount[0]
        lcount[0] += 1
        copy = pltpu.make_async_copy(src, dst, loc.at[i])
        copy.start()
        return copy

    l_out, l_att = lc(wo_h, WO), [lc(wq_h, WQ), lc(wk_h, WK), lc(wv_h, WV)]
    l_w = [lc(wg_h, W.at[1, 0, z, y]), lc(wu_h, W.at[2, 0, z, y]), lc(wd_h, W.at[3, 0, z, y])]
    l_seg = lc(seg_h, SEG)
    l_vec = [lc(h, VEC.at[i, 0]) for i, h in enumerate((g1_h, b1_h, g2_h, b2_h))]
    l_x = lc(xin.at[xi], X.at[tt])
    l_ct = lc(cot.at[xi], CT.at[xi])
    l_tab = [lc(cosl_h, COSL), lc(sinl_h, SINL), lc(cosf_h, COSF), lc(sinf_h, SINF)]

    barrier = pltpu.get_barrier_semaphore()
    peers = [dev_x, dev_c, dev_y] + dev_z[1:]
    for dev in peers:
        pl.semaphore_signal(barrier, inc=1, device_id=dev, device_id_type=MESH)
    l_out.wait()
    for copy in l_att:
        copy.wait()
    shards = [W.at[0, 0, z, y], wg_h, wu_h, wd_h]
    two = 2 * HD
    turned_out = WO[...].T
    shards[0][:, :two] = WQ[:, :two]
    shards[0][:, two : 2 * two] = WK[:, :two]
    shards[0][:, 2 * two : 3 * two] = WV[:, :two]
    shards[0][:, 3 * two : 4 * two] = jnp.concatenate([WQ[:, two:], WK[:, two:]], axis=1)
    shards[0][:, 4 * two : 5 * two] = jnp.concatenate([WV[:, two:], turned_out[:, two:]], axis=1)
    shards[0][:, 5 * two :] = turned_out[:, :two]
    pl.semaphore_wait(barrier, len(peers))

    ag = {}
    split = width // 3
    pieces = [
        (0, 0, width),
        (1, 0, width),
        (2, 0, width),
        (3, 0, split),
        (3, split, width - split),
        (0, 0, 3 * LANES),
        (0, 3 * LANES, 2 * LANES),
        (0, 5 * LANES, LANES),
    ]
    LAST, QKV, REST, OUT = 4, 5, 6, 7

    def cut(view, p):
        _, lo, n = pieces[p]
        return view if n == width else view.at[..., pl.ds(lo, n)]

    def w_at(p, s, zz, yy):
        return cut(W.at[pieces[p][0], s, zz, yy], p)

    def own_shard(p):
        return cut(shards[pieces[p][0]], p)

    def e1_plane(p):
        own = own_shard(p)
        ag[p, "x"] = [rc(own, w_at(p, 1, z, y), dev_x)]
        ag[p, "y"] = [rc(own, w_at(p, 0, z, y), dev_y)]

    def e1(p):
        own = own_shard(p)
        ag[p, "z"] = [rc(own, w_at(p, 0, z, y), dev_z[j]) for j in range(1, nz)]
        e1_plane(p)

    def e2(p):
        for j in range(1, nz):
            ag[p, "z"][j - 1].wait_recv()
            part = w_at(p, 0, zfrom[j], y)
            ag[p, "x"].append(rc(part, w_at(p, 1, zfrom[j], y), dev_x))
            ag[p, "y"].append(rc(part, part, dev_y))

    def e3(p, by_x):
        ag[p, "d"] = []
        for j in range(nz):
            ag[p, "x"][j].wait_recv()
            if j < nz - by_x:
                part = w_at(p, 1, zfrom[j], y)
                ag[p, "d"].append(rc(part, part, dev_y))
            ag[p, "y"][j].wait_recv()
            if j >= nz - by_x:
                ag[p, "d"].append(rc(w_at(p, 0, zfrom[j], oy), w_at(p, 1, zfrom[j], oy), dev_x))

    def e4(p):
        for copy in ag[p, "d"]:
            copy.wait_recv()

    top_rows, low_rows = pl.ds(0, rows // 2), pl.ds(rows // 2, rows // 2)

    def f2(p):
        ag[p, "x"][0].wait_recv()
        part = w_at(p, 1, z, y).at[top_rows]
        ag[p, "d"] = [rc(part, part, dev_y)]
        ag[p, "y"][0].wait_recv()
        ag[p, "d"].append(
            rc(w_at(p, 0, z, oy).at[low_rows], w_at(p, 1, z, oy).at[low_rows], dev_x)
        )

    def f3(p):
        for copy in ag[p, "d"]:
            copy.wait_recv()
        plane = cut(W.at[3, :, z], p)
        ag[p, "z"] = [rc(plane, plane, dev_z[j]) for j in range(1, nz)]

    def f4(p):
        for copy in ag[p, "z"]:
            copy.wait_recv()

    def e_sent(p):
        for copy in ag[p, "z"] + ag[p, "x"] + ag[p, "y"] + ag[p, "d"]:
            sent(copy)

    e1(0)
    e1(3)
    e1_plane(LAST)
    e1(2)
    x_far = rc(xin.at[1 - xi], X.at[tt], dev_x)
    x_core = rc(xin.at[xi], X.at[tt], dev_c)

    l_seg.wait()
    seg = SEG
    g1_ref, b1_ref, g2_ref, b2_ref = (VEC.at[i] for i in range(4))
    row_ids = jnp.broadcast_to(seg[pl.ds(xi, 1), :], (LANES, length))
    same = row_ids == lax.broadcasted_iota(jnp.int32, (LANES, length), 0)
    known = lax.broadcasted_iota(jnp.int32, (LANES, length), 0) < IDS
    SEGQ[...] = jnp.where(jnp.logical_or(same, jnp.logical_not(known)), 0.0, mask_fill).astype(BF16)
    SEGK[...] = jnp.where(same, 1.0, 0.0).astype(F32).T.astype(BF16)
    NG[...] = jnp.zeros_like(NG)
    lane = lax.broadcasted_iota(jnp.int32, (1, LANES), 1)
    low_half = lane < HD
    swap_low = lax.rem(lane, HD) < (HD // 2)

    def swap(v):
        return jnp.where(swap_low, pltpu.roll(v, LANES - HD // 2, 1), pltpu.roll(v, HD // 2, 1))

    def at_quarter(i):
        return pl.ds(pl.multiple_of(i * quarter, quarter), quarter)

    def wmat(k, s, lo=0, hi=None):
        hi = width if hi is None else hi
        return W[k, s, :, :, :, lo:hi].reshape(width, hi - lo)

    def turn_rows(src, dst):
        def step(i, _):
            dst[:, at_quarter(i)] = src[i].T
            return 0

        lax.fori_loop(0, 4, step, 0)

    f2(LAST)
    e1(1)
    e2(0)
    x_far.wait_recv()
    x_core2 = rc(X.at[t_x], X.at[t_x], dev_c)
    x_core.wait_recv()
    l_x.wait()
    l_ct.wait()
    for copy in l_w + l_vec + l_tab:
        copy.wait()
    x_core2.wait_recv()
    turn_rows(X, XT)
    e2(3)
    f3(LAST)
    e3(0, 1)

    def project(s):
        def step(i, _):
            at = at_quarter(i)
            y5 = mm(X[i], wmat(0, s, 0, 5 * LANES))
            cos, sin = COSL[at, :], SINL[at, :]
            turned = []
            for b in range(5):
                v = y5[:, b * LANES : (b + 1) * LANES]
                if b in (0, 1, 3):
                    v = v * cos + swap(v) * sin
                v = v.astype(BF16)
                PK[s, b, at, :] = v
                turned.append(v.T)
            zero = jnp.zeros((HD, quarter), BF16)
            q0 = turned[0] * BF16(0.125)
            q2 = turned[3] * BF16(0.125)
            QZ[3 * s, :HD, at] = q0[:HD]
            QZ[3 * s, HD:, at] = zero
            QZ[3 * s + 1, :HD, at] = zero
            QZ[3 * s + 1, HD:, at] = q0[HD:]
            QZ[3 * s + 2, :HD, at] = zero
            QZ[3 * s + 2, HD:, at] = q2[:HD]
            KT[3 * s, :, at] = turned[1][:HD]
            KT[3 * s + 1, :, at] = turned[1][HD:]
            KT[3 * s + 2, :, at] = turned[3][HD:]
            VT[3 * s, :, at] = turned[2][:HD]
            VT[3 * s + 1, :, at] = turned[2][HD:]
            VT[3 * s + 2, :, at] = turned[4][:HD]
            return 0

        lax.fori_loop(0, 4, step, 0)

    def spans():
        for qb in range(4):
            lo = max(0, qb * quarter - length // 2 + 1) // quarter * quarter
            hi = min(length, -(-(qb * quarter + quarter - 1 + length // 2) // quarter) * quarter)
            yield pl.ds(qb * quarter, quarter), pl.ds(lo, hi - lo)

    def scores_of(s, hh, h, at, keys):
        left = jnp.concatenate([PK[s, 1 + 2 * lax.div(hh, 2), keys, :], SEGK[keys, :]], axis=1)
        right = jnp.concatenate([QZ[h, :, at], SEGQ[:, at]], axis=0)
        return mm(left, right)

    def attend(first, heads):
        def step(n, _):
            h = first + n
            s, hh = lax.div(h, 3), lax.rem(h, 3)
            for at, keys in spans():
                st = scores_of(s, hh, h, at, keys)
                top = jnp.max(st, axis=0, keepdims=True)
                p = jnp.exp(st - top)
                total = jnp.sum(p, axis=0, keepdims=True)
                ot = mm(VT[h, :, keys], p.astype(BF16)) * (1.0 / total)
                LSE[pl.ds(h, 1), at] = top + jnp.log(total)
                ATTT[h, :, at] = ot.astype(BF16)
            return 0

        lax.fori_loop(0, heads, step, 0)

    def turn_heads(s):
        def turn(i, _):
            at = at_quarter(i)
            pair = jnp.concatenate([ATTT[3 * s, :, at], ATTT[3 * s + 1, :, at]], axis=0)
            lone = jnp.concatenate([jnp.zeros((HD, quarter), BF16), ATTT[3 * s + 2, :, at]], axis=0)
            ATT[s, at, :LANES] = lone.T
            ATT[s, at, LANES:] = pair.T
            return 0

        lax.fori_loop(0, 4, turn, 0)

    project(0)
    e2(2)
    e3(3, 1)
    e4(0)
    project(1)
    e2(1)
    attend(0, 2)
    e3(2, 2)
    attend(2, 2)
    e4(3)
    attend(4, 2)
    e3(1, 2)
    turn_heads(0)
    turn_heads(1)
    last_exchange = []

    def exchange(n, part):
        if last_exchange:
            sent(last_exchange.pop())

        def other(k, _):
            CXS[k] = part(1 - c + 2 * k).astype(BF16)
            return 0

        lax.fori_loop(0, 2, other, 0)
        copy = rc(CXS, CXR.at[n % 2], dev_c)
        last_exchange.append(copy)

        def own(k, _):
            ACC[k] = part(c + 2 * k)
            return 0

        lax.fori_loop(0, 2, own, 0)
        copy.wait_recv()

    def spread():
        return [rc(F4.at[c + 2 * k], F4.at[c + 2 * k], dev_c) for k in range(2)]

    def out_part(i):
        at = at_quarter(i)
        return mt(ATT[0, at, :], wmat(0, 0, 4 * LANES)) + mt(ATT[1, at, :], wmat(0, 1, 4 * LANES))

    exchange(0, out_part)
    ct_far = rc(cot.at[1 - xi], CT.at[xi], dev_x)
    tile = quarter // 2

    def over_tiles(fn):
        def step(n, _):
            k = lax.div(n, 2)
            fn(k, c + 2 * k, pl.ds(pl.multiple_of(lax.rem(n, 2) * tile, tile), tile))
            return 0

        lax.fori_loop(0, 4, step, 0)

    def kept_rows(k, at):
        return pl.ds(pl.multiple_of(k * quarter + at.start, tile), tile)

    def first_norm(k, i, at):
        z1 = X[i, at, :].astype(F32) + ACC[k, at, :] + CXR[0, k, at, :].astype(F32)
        n1, rstd = norm_of(z1)
        N1[k, at, :] = n1
        DKA[kept_rows(k, at), :] = jnp.broadcast_to(rstd, (tile, LANES))
        F4[i, at, :] = (n1 * g1_ref[...] + b1_ref[...]).astype(BF16)

    over_tiles(first_norm)
    h_copies = spread()
    for copy in h_copies:
        copy.wait_recv()
    turn_rows(F4, TT)

    def all_rows(ref):
        return ref[...].reshape(length, width)

    def w_cols(k, s, at):
        return W[k, s, :, :, :, at].reshape(width, at.size)

    def block_of(n):
        return pl.ds(pl.multiple_of(n * 2 * LANES, 2 * LANES), 2 * LANES)

    def ff_up(s, n):
        at = block_of(n)
        g = mm(all_rows(F4), w_cols(1, s, at))
        u = mm(all_rows(F4), w_cols(2, s, at))
        GP[s, :, at] = g.astype(BF16)
        UP[s, :, at] = u.astype(BF16)
        RR[s, :, at] = (g * jax.nn.sigmoid(g) * u).astype(BF16)
        return 0

    lax.fori_loop(0, 3, lambda n, _: ff_up(0, n), 0)
    e4(2)
    e4(1)
    lax.fori_loop(0, 3, lambda n, _: ff_up(1, n), 0)
    f4(LAST)

    def down_part(i):
        at = at_quarter(i)
        return mt(RR[0, at, :], wmat(3, 0)) + mt(RR[1, at, :], wmat(3, 1))

    for copy in h_copies:
        sent(copy)
    exchange(1, down_part)
    ct_far.wait_recv()

    def second_norm(k, i, at):
        h = N1[k, at, :] * g1_ref[...] + b1_ref[...]
        z2 = h + ACC[k, at, :] + CXR[1, k, at, :].astype(F32)
        n2, rstd = norm_of(z2)
        OB[k, at, :] = (n2 * g2_ref[...] + b2_ref[...]).astype(BF16)
        dy = CT[k, at, :].astype(F32)
        NG[2:3, :] += colsum(dy * n2)
        NG[3:4, :] += colsum(dy)
        dz = grad_of_norm(dy * g2_ref[...], n2, rstd)
        DZ[k, at, :] = dz
        F4[i, at, :] = dz.astype(BF16)

    over_tiles(second_norm)
    d_copies = spread()
    o_far = rc(OB.at[1 - xi], out_h.at[xi], dev_x)
    o_own = lc(OB.at[xi], out_h.at[xi])

    slots = {3: G, 1: W.at[3], 2: W.at[1], 0: W.at[2]}
    rs = {}
    by_x = {1: 1, 2: 2, 3: 1, QKV: 2, REST: 2, OUT: 1}

    def g_at(p, s, zz, yy):
        return cut(slots[pieces[p][0]].at[s, zz, yy], p)

    def into(ref, p, *at):
        return cut(ref.at[(pieces[p][0],) + at], p)

    def plus(target, *others):
        total = target[...].astype(F32)
        for other in others:
            total = total + other[...].astype(F32)
        target[...] = total.astype(BF16)

    def early(p):
        return pl.ds(0, by_x[p]), pl.ds(by_x[p], nz - by_x[p])

    def r1_far(p):
        nx = by_x[p]
        near, far = early(p)
        rs[p, "dx"] = rc(g_at(p, 1, near, oy), into(S1X, p, pl.ds(0, nx)), dev_x)
        rs[p, "dy"] = rc(g_at(p, 1, far, oy), into(S1Y, p, pl.ds(0, nz - nx)), dev_y)
        rs[p, "x0"] = rc(g_at(p, 1, near, y), into(S2X, p, near), dev_x)

    def r1_near(p):
        _, far = early(p)
        rs[p, "y0"] = rc(g_at(p, 0, far, oy), into(S2Y, p, far), dev_y)

    def r2(p):
        nx = by_x[p]
        near, far = early(p)
        rs[p, "dx"].wait_recv()
        for j in range(nx):
            plus(g_at(p, 0, j, oy), into(S1X, p, j))
        rs[p, "y1"] = rc(g_at(p, 0, near, oy), into(S2Y, p, near), dev_y)
        rs[p, "dy"].wait_recv()
        for j in range(nx, nz):
            plus(g_at(p, 1, j, y), into(S1Y, p, j - nx))
        rs[p, "x1"] = rc(g_at(p, 1, far, y), into(S2X, p, far), dev_x)

    def r3(p):
        for name in ("x0", "y0", "y1", "x1"):
            rs[p, name].wait_recv()
        for j in range(nz):
            plus(g_at(p, 0, j, y), into(S2X, p, j), into(S2Y, p, j))
        rs[p, "z"] = [rc(g_at(p, 0, zs[j], y), into(ZR, p, z), dev_z[j]) for j in range(1, nz)]

    def place(p):
        k = pieces[p][0]
        return cut(N1.at[k // 2, pl.ds((k % 2) * rows, rows)], p)

    def r4(p):
        for copy in rs[p, "z"]:
            copy.wait_recv()
        total = g_at(p, 0, z, y)[...].astype(F32)
        for j in range(1, nz):
            total = total + into(ZR, p, zfrom[j])[...].astype(F32)
        target = place(p)
        target[...] = total
        rs[p, "out"] = lc(target, cut(gw_h.at[pieces[p][0]], p))

    def q1(p):
        rs[p, "z"] = [
            rc(cut(slots[3].at[:, zs[j]], p), ZB.at[z], dev_z[j]) for j in range(1, nz)
        ]

    def q2(p):
        for copy in rs[p, "z"]:
            copy.wait_recv()
        for s in range(2):
            for yy in range(NY):
                plus(g_at(p, s, z, yy), *(ZB.at[zfrom[j], s, yy] for j in range(1, nz)))
        rs[p, "dx"] = rc(g_at(p, 1, z, oy).at[top_rows], into(S1X, p, 0).at[top_rows], dev_x)
        rs[p, "dy"] = rc(g_at(p, 1, z, oy).at[low_rows], into(S1Y, p, 0).at[low_rows], dev_y)
        rs[p, "x0"] = rc(g_at(p, 1, z, y).at[top_rows], into(S2X, p, 0).at[top_rows], dev_x)
        rs[p, "y0"] = rc(g_at(p, 0, z, oy).at[low_rows], into(S2Y, p, 0).at[low_rows], dev_y)

    def q3(p):
        rs[p, "dx"].wait_recv()
        plus(g_at(p, 0, z, oy).at[top_rows], into(S1X, p, 0).at[top_rows])
        rs[p, "y1"] = rc(g_at(p, 0, z, oy).at[top_rows], into(S2Y, p, 0).at[top_rows], dev_y)
        rs[p, "dy"].wait_recv()
        plus(g_at(p, 1, z, y).at[low_rows], into(S1Y, p, 0).at[low_rows])
        rs[p, "x1"] = rc(g_at(p, 1, z, y).at[low_rows], into(S2X, p, 0).at[low_rows], dev_x)

    def q4(p):
        for name in ("x0", "y0", "y1", "x1"):
            rs[p, name].wait_recv()
        total = g_at(p, 0, z, y)[...].astype(F32)
        total = total + into(S2X, p, 0)[...].astype(F32) + into(S2Y, p, 0)[...].astype(F32)
        target = place(p)
        target[...] = total
        rs[p, "out"] = lc(target, cut(gw_h.at[3], p))

    def weight_grad(p, s, left, right):
        k, lo, n = pieces[p]
        block = 2 * LANES

        def step(j, _):
            at = pl.ds(pl.multiple_of(lo + j * block, block), block)
            part = mm(left[...], right[s, :, at]).astype(BF16)
            slots[k][s, :, :, :, at] = part.reshape(nz, NY, rows, block)
            return 0

        lax.fori_loop(0, n // block, step, 0)


    def turn_half(first):
        def step(k, _):
            i = first + 2 * k
            DT[:, at_quarter(i)] = F4[i].T
            return 0

        lax.fori_loop(0, 2, step, 0)

    turn_half(c)
    for copy in d_copies:
        copy.wait_recv()
    turn_half(1 - c)
    weight_grad(LAST, 0, DT, RR)
    weight_grad(LAST, 1, DT, RR)
    q1(LAST)
    weight_grad(3, 1, DT, RR)
    weight_grad(3, 0, DT, RR)
    r1_far(3)
    r1_near(3)

    def ff_back(n, _):
        s = lax.div(n, 3)
        at = block_of(lax.rem(n, 3))
        dr = mm(all_rows(F4), w_cols(3, s, at))
        g = GP[s, :, at].astype(F32)
        u = UP[s, :, at].astype(F32)
        sg = jax.nn.sigmoid(g)
        GP[s, :, at] = (dr * u * sg * (1.0 + g * (1.0 - sg))).astype(BF16)
        UP[s, :, at] = (dr * g * sg).astype(BF16)
        return 0

    lax.fori_loop(0, 6, ff_back, 0)
    e_sent(3)
    e_sent(LAST)
    weight_grad(1, 1, TT, GP)
    r1_far(1)
    weight_grad(1, 0, TT, GP)
    r2(3)

    def hidden_part(i):
        at = at_quarter(i)
        return (
            mt(GP[0, at, :], wmat(1, 0))
            + mt(UP[0, at, :], wmat(2, 0))
            + mt(GP[1, at, :], wmat(1, 1))
            + mt(UP[1, at, :], wmat(2, 1))
        )

    for copy in d_copies:
        sent(copy)
    exchange(2, hidden_part)

    def first_norm_back(k, i, at):
        dh = DZ[k, at, :] + ACC[k, at, :] + CXR[0, k, at, :].astype(F32)
        n1 = N1[k, at, :]
        NG[0:1, :] += colsum(dh * n1)
        NG[1:2, :] += colsum(dh)
        dz = grad_of_norm(dh * g1_ref[...], n1, DKA[kept_rows(k, at), :1])
        DZ[k, at, :] = dz
        F4[i, at, :] = dz.astype(BF16)

    over_tiles(first_norm_back)
    b_copies = spread()
    n_core = rc(NG, NR.at[0], dev_c)
    e_sent(1)
    e_sent(2)
    r1_near(1)
    weight_grad(2, 1, TT, UP)
    r2(1)
    weight_grad(2, 0, TT, UP)
    for copy in b_copies:
        copy.wait_recv()
    n_core.wait_recv()
    NS[0] = NG[...] + NR[0]
    n_x = rc(NS.at[0], NR.at[1], dev_x)
    turn_rows(F4, DT)
    r1_far(2)
    def out_grad(s, _):
        part = mm(DT[...], ATT[s]).astype(BF16)
        slots[0][s, :, :, :, 4 * LANES :] = part.reshape(nz, NY, rows, 2 * LANES)
        return 0

    lax.fori_loop(0, 2, out_grad, 0)

    def head_lanes(h):
        return pl.ds(pl.multiple_of(h * LANES, LANES), LANES)

    def att_grad(i, _):
        at = at_quarter(i)
        for s in range(2):
            da = mm(F4[i], wmat(0, s, 4 * LANES))
            pair = da[:, LANES:]
            lone = pltpu.roll(da[:, :LANES], HD, 1)
            zero = jnp.zeros_like(pair)
            views = (
                jnp.where(low_half, pair, zero),
                jnp.where(low_half, zero, pair),
                jnp.where(low_half, lone, zero),
            )
            for hh in range(3):
                h = 3 * s + hh
                v = views[hh].astype(BF16)
                GP[0, at, h * LANES : (h + 1) * LANES] = v
                vt = v.T
                TT[h * LANES : (h + 1) * LANES, at] = vt
                part = vt[HD:] if hh == 1 else vt[:HD]
                DEL[h : h + 1, at] = colsum(part.astype(F32) * ATTT[h, :, at].astype(F32))
        return 0

    lax.fori_loop(0, 4, att_grad, 0)
    n_x.wait_recv()
    NS[1] = NS[0] + NR[1]
    n_y = rc(NS.at[1], NR.at[2], dev_y)
    def attend_back(s, first, heads):
        def head(hh, _):
            h = 3 * s + hh
            DKA[...] = jnp.zeros_like(DKA)
            DVA[...] = jnp.zeros_like(DVA)
            hl = head_lanes(h)

            for at, keys in spans():
                p = jnp.exp(scores_of(s, hh, h, at, keys) - LSE[pl.ds(h, 1), at])
                dpt = mm(PK[s, 2 + 2 * lax.div(hh, 2), keys, :], TT[hl, at])
                ds = (p * (dpt - DEL[pl.ds(h, 1), at])).astype(BF16)
                DVA[keys, :] += mm(p.astype(BF16), GP[0, at, hl])
                DKA[keys, :] += mm(ds, PK[s, 3 * lax.div(hh, 2), at, :])
                dq = mm(KT[h, :, keys], ds) * 0.125
                a, b = dq[: HD // 2], dq[HD // 2 :]
                cos, sin = COSF[:, at], SINF[:, at]
                VT[h, : HD // 2, at] = (a * cos + b * sin).astype(BF16)
                VT[h, HD // 2 :, at] = (b * cos - a * sin).astype(BF16)

            def finish(i, _):
                at = at_quarter(i)
                dk = DKA[at, :] * 0.125
                UP[0, at, hl] = (dk * COSL[at, :] - swap(dk) * SINL[at, :]).astype(BF16)
                GP[0, at, hl] = DVA[at, :].astype(BF16)
                return 0

            lax.fori_loop(0, 4, finish, 0)
            return 0

        lax.fori_loop(first, first + heads, head, 0)

    def join_heads(s):
        def gather(i, _):
            at = at_quarter(i)

            def part(ref, hh):
                h = 3 * s + hh
                return ref[0, at, h * LANES : (h + 1) * LANES].astype(F32)

            dq0 = jnp.concatenate([VT[3 * s, :, at], VT[3 * s + 1, :, at]], axis=0).T
            dq2 = jnp.concatenate([VT[3 * s + 2, :, at]] * 2, axis=0).T
            dk2 = pltpu.roll(part(UP, 2), HD, 1)
            dv2 = part(GP, 2)
            RR[s, at, 0:LANES] = dq0
            RR[s, at, LANES : 2 * LANES] = jnp.where(low_half, part(UP, 0), part(UP, 1)).astype(BF16)
            RR[s, at, 2 * LANES : 3 * LANES] = jnp.where(
                low_half, part(GP, 0), part(GP, 1)
            ).astype(BF16)
            RR[s, at, 3 * LANES : 4 * LANES] = jnp.where(low_half, dq2.astype(F32), dk2).astype(BF16)
            RR[s, at, 4 * LANES : 5 * LANES] = jnp.where(
                low_half, dv2, jnp.zeros_like(dv2)
            ).astype(BF16)
            return 0

        lax.fori_loop(0, 4, gather, 0)

    def in_grad(s, p):
        _, lo, n = pieces[p]
        part = mm(XT[...], RR[s, :, lo : lo + n])
        if p == REST:
            mixed = slots[0][s, :, :, :, 4 * LANES : 5 * LANES].reshape(width, LANES)
            mixed = part[:, LANES:] + mixed.astype(F32)
            part = jnp.concatenate([part[:, :LANES], mixed], axis=1)
        slots[0][s, :, :, :, lo : lo + n] = part.astype(BF16).reshape(nz, NY, rows, n)

    attend_back(1, 0, 1)
    r1_near(2)
    r3(3)
    attend_back(1, 1, 1)
    r3(1)
    attend_back(1, 2, 1)
    r2(2)
    join_heads(1)
    r1_far(OUT)
    in_grad(1, QKV)
    r1_far(QKV)
    in_grad(1, REST)
    r1_near(OUT)
    n_y.wait_recv()
    NS[2] = NS[1] + NR[2]
    NZR[z] = NS[2]
    n_z = [rc(NS.at[2], NZR.at[z], dev_z[j]) for j in range(1, nz)]
    attend_back(0, 0, 2)
    r1_far(REST)
    r3(2)
    attend_back(0, 2, 1)
    r2(OUT)
    join_heads(0)
    in_grad(0, QKV)
    r1_near(QKV)
    r2(QKV)
    q2(LAST)
    r4(3)
    in_grad(0, REST)
    r1_near(REST)
    def input_part(i):
        at = at_quarter(i)
        return mt(RR[0, at, : 5 * LANES], wmat(0, 0, 0, 5 * LANES)) + mt(
            RR[1, at, : 5 * LANES], wmat(0, 1, 0, 5 * LANES)
        )

    exchange(3, input_part)

    def input_grad(k, i, at):
        g = DZ[k, at, :] + ACC[k, at, :] + CXR[1, k, at, :].astype(F32)
        CT[k, at, :] = g.astype(BF16)

    over_tiles(input_grad)
    r3(OUT)
    r2(REST)
    i_far = rc(CT.at[1 - xi], gin_h.at[xi], dev_x)
    i_own = lc(CT.at[xi], gin_h.at[xi])
    r4(1)
    r3(QKV)
    q3(LAST)
    for copy in n_z:
        copy.wait_recv()
    total = NZR[0]
    for j in range(1, nz):
        total = total + NZR[j]
    ng_out[...] = total
    r3(REST)
    r4(OUT)
    r4(2)
    r4(QKV)
    q4(LAST)
    r4(REST)
    o_far.wait_recv()
    i_far.wait_recv()
    o_own.wait()
    i_own.wait()
    for p in (1, 2, 3, LAST, QKV, REST, OUT):
        rs[p, "out"].wait()
    for copy in list(sends.values()):
        sent(copy)


def layer_per_device(
    dp_size,
    layer_input,
    cotangent,
    segment_ids,
    query_weight,
    key_weight,
    value_weight,
    output_weight,
    gate_weight,
    up_weight,
    down_weight,
    first_gain,
    first_bias,
    second_gain,
    second_bias,
):
    _, quarter, width = layer_input.shape
    length = 4 * quarter
    rows = query_weight.shape[0]
    nz = dp_size // NY
    tables = [jnp.asarray(t) for t in lane_tables(length)]
    anywhere = pl.BlockSpec(memory_space=pl.ANY)
    vmem = pl.BlockSpec(memory_space=pltpu.VMEM)
    half = HD // 2
    copies = 152
    part = query_weight.shape[1]
    scratch = [
        ((4, 2, nz, NY, rows, width), BF16),
        ((2, nz, NY, rows, width), BF16),
        ((4, nz // 2, rows, width), BF16),
        ((4, nz - 1, rows, width), BF16),
        ((4, nz, rows, width), BF16),
        ((4, nz, rows, width), BF16),
        ((4, nz, rows, width), BF16),
        ((4, quarter, width), BF16),
        ((width, length), BF16),
        ((width, length), BF16),
        ((width, length), BF16),
        ((2, quarter, width), BF16),
        ((LANES, length), BF16),
        ((length, LANES), BF16),
        ((length, LANES), F32),
        ((length, LANES), F32),
        ((half, length), F32),
        ((half, length), F32),
        ((2, 5, length, LANES), BF16),
        ((6, LANES, length), BF16),
        ((6, HD, length), BF16),
        ((6, HD, length), BF16),
        ((8, length), F32),
        ((8, length), F32),
        ((2, length, 2 * LANES), BF16),
        ((6, HD, length), BF16),
        ((2, quarter, width), F32),
        ((4, quarter, width), BF16),
        ((2, length, width), BF16),
        ((2, length, width), BF16),
        ((2, length, width), BF16),
        ((2, quarter, width), F32),
        ((2, quarter, width), BF16),
        ((2, 2, quarter, width), BF16),
        ((2, quarter, width), F32),
        ((2, quarter, width), BF16),
        ((length, LANES), F32),
        ((length, LANES), F32),
        ((2, length), jnp.int32),
        ((rows, part), BF16),
        ((rows, part), BF16),
        ((rows, part), BF16),
        ((part, rows), BF16),
        ((4, 1, width), F32),
        ((8, width), F32),
        ((3, 8, width), F32),
        ((3, 8, width), F32),
        ((nz, 8, width), F32),
        ((nz, 2, NY, rows, width - width // 3), BF16),
    ]
    outputs, grad_input, grads, norms = pl.pallas_call(
        functools.partial(layer_kernel, nz),
        out_shape=(
            jax.ShapeDtypeStruct(layer_input.shape, BF16),
            jax.ShapeDtypeStruct(layer_input.shape, BF16),
            jax.ShapeDtypeStruct((4, rows, width), F32),
            jax.ShapeDtypeStruct((8, width), F32),
        ),
        in_specs=[anywhere] * 18,
        out_specs=(anywhere, anywhere, anywhere, vmem),
        scratch_shapes=[pltpu.VMEM(shape, kind) for shape, kind in scratch]
        + [
            pltpu.SemaphoreType.DMA((27,)),
            pltpu.SemaphoreType.DMA((copies,)),
            pltpu.SemaphoreType.DMA((copies,)),
        ],
        compiler_params=pltpu.CompilerParams(
            collective_id=0, has_side_effects=True, vmem_limit_bytes=VMEM_BYTES
        ),
    )(
        layer_input,
        cotangent,
        segment_ids,
        query_weight,
        key_weight,
        value_weight,
        output_weight,
        gate_weight,
        up_weight,
        down_weight.T,
        first_gain,
        first_bias,
        second_gain,
        second_bias,
        *tables,
    )
    vector = jax.ShapeDtypeStruct((width,), F32)
    like = lambda a: jax.ShapeDtypeStruct(a.shape, F32)
    results = pl.pallas_call(
        place_kernel,
        out_shape=(
            jax.ShapeDtypeStruct(layer_input.shape, BF16),
            jax.ShapeDtypeStruct(layer_input.shape, BF16),
            like(query_weight),
            like(key_weight),
            like(value_weight),
            like(output_weight),
            like(gate_weight),
            like(up_weight),
            jax.ShapeDtypeStruct(down_weight.shape[::-1], F32),
            vector,
            vector,
            vector,
            vector,
        ),
        in_specs=[anywhere] * 4,
        out_specs=(anywhere, anywhere) + (vmem,) * 4 + (anywhere,) * 3 + (vmem,) * 4,
        scratch_shapes=[
            pltpu.VMEM(layer_input.shape, BF16),
            pltpu.VMEM(layer_input.shape, BF16),
            pltpu.VMEM((4, rows, width), F32),
            pltpu.VMEM((8, width), F32),
            pltpu.SemaphoreType.DMA((7,)),
            pltpu.SemaphoreType.DMA((5,)),
        ],
        compiler_params=pltpu.CompilerParams(vmem_limit_bytes=VMEM_BYTES),
    )(outputs, grad_input, grads, norms)
    return (*results[:8], results[8].T, *results[9:])


def place_kernel(
    out_i,
    gin_i,
    gw,
    ng,
    out_o,
    gin_o,
    gq,
    gk,
    gv,
    go,
    gg,
    gu,
    gd,
    n0,
    n1,
    n2,
    n3,
    OUT,
    GIN,
    GW,
    NB,
    sem,
    osem,
):
    loads = [
        pltpu.make_async_copy(src, dst, sem.at[i])
        for i, (src, dst) in enumerate(
            [
                (gw.at[0], GW.at[0]),
                (ng, NB),
                (gw.at[1], GW.at[1]),
                (gw.at[2], GW.at[2]),
                (gw.at[3], GW.at[3]),
                (out_i, OUT),
                (gin_i, GIN),
            ]
        )
    ]
    for copy in loads:
        copy.start()
    stores = [
        pltpu.make_async_copy(src, dst, osem.at[i])
        for i, (src, dst) in enumerate(
            [(GW.at[1], gg), (GW.at[2], gu), (GW.at[3], gd), (OUT, out_o), (GIN, gin_o)]
        )
    ]
    for load, store in zip(loads[2:], stores):
        load.wait()
        store.start()
    loads[0].wait()
    two = 2 * HD
    b = [GW[0, :, i * two : (i + 1) * two] for i in range(6)]
    gq[...] = jnp.concatenate([b[0], b[3][:, :HD]], axis=1)
    gk[...] = jnp.concatenate([b[1], b[3][:, HD:]], axis=1)
    gv[...] = jnp.concatenate([b[2], b[4][:, :HD]], axis=1)
    go[...] = jnp.concatenate([b[5], b[4][:, HD:]], axis=1).T
    loads[1].wait()
    for i, n in enumerate((n0, n1, n2, n3)):
        n[...] = NB[i, :]
    for store in stores:
        store.wait()


VMEM_BYTES = 64 << 20


def solution(mesh):
    in_specs = (
        P("dp", "tensor", None),
        P("dp", "tensor", None),
        P("dp", None),
        P("dp", "tensor"),
        P("dp", "tensor"),
        P("dp", "tensor"),
        P("tensor", "dp"),
        P("dp", "tensor"),
        P("dp", "tensor"),
        P("tensor", "dp"),
        P(),
        P(),
        P(),
        P(),
    )
    out_specs = (
        P("dp", "tensor", None),
        P("dp", "tensor", None),
        P("dp", "tensor"),
        P("dp", "tensor"),
        P("dp", "tensor"),
        P("tensor", "dp"),
        P("dp", "tensor"),
        P("dp", "tensor"),
        P("tensor", "dp"),
        P(),
        P(),
        P(),
        P(),
    )
    dp_size, tensor_size = mesh.shape["dp"], mesh.shape["tensor"]

    def whole(*arrays):
        layer_input, query_weight, gate_weight = arrays[0], arrays[3], arrays[7]
        batch, length, width = layer_input.shape
        fits = (
            tensor_size == 4
            and dp_size % (2 * NY) == 0
            and batch == 2 * dp_size
            and width % (16 * dp_size) == 0
            and query_weight.shape[1] == 12 * HD
            and query_weight.shape[1] == width
            and gate_weight.shape[1] == 4 * width
            and length % 1024 == 0
        )
        program = functools.partial(layer_per_device, dp_size) if fits else per_device
        return jax.shard_map(
            program, mesh=mesh, in_specs=in_specs, out_specs=out_specs, check_vma=False
        )(*arrays)

    return whole
```

```python
import functools

import jax
import jax.numpy as jnp
import numpy as np
from jax import lax
from jax.experimental import pallas as pl
from jax.experimental.pallas import tpu as pltpu
from jax.sharding import PartitionSpec as P

HD = 64


eps_norm = 1e-06
rope_base = 1000.0
mask_fill = -1e30


def layer_norm(field_rows, gain_vec, bias_vec):
    row_mean = jnp.mean(field_rows, axis=-1, keepdims=True)
    centred = field_rows - row_mean
    variance = jnp.mean(centred * centred, axis=-1, keepdims=True)
    return centred * lax.rsqrt(variance + eps_norm) * gain_vec + bias_vec


def rotary_tables(length, head_dim):
    half_dim = head_dim // 2
    frequency = rope_base ** (-(2.0 * jnp.arange(half_dim, dtype=jnp.float32)) / head_dim)
    angles = jnp.arange(length, dtype=jnp.float32)[:, None] * frequency[None, :]
    return (jnp.cos(angles), jnp.sin(angles))


def rotate(heads_data, cos_table, sine_table):
    half_dim = heads_data.shape[-1] // 2
    first_half = heads_data[..., :half_dim]
    second_half = heads_data[..., half_dim:]
    cos_part = cos_table[:, None, :]
    sine_part = sine_table[:, None, :]
    return jnp.concatenate(
        [
            first_half * cos_part - second_half * sine_part,
            second_half * cos_part + first_half * sine_part,
        ],
        axis=-1,
    )


def swiglu(gate_pre, up_pre):
    return jax.nn.silu(gate_pre) * up_pre


def contract_rows(left, right):
    return lax.dot_general(
        left, right, (((0,), (0,)), ((), ())), preferred_element_type=jnp.float32
    )


def times_transpose(left, right):
    return lax.dot_general(
        left, right, (((1,), (1,)), ((), ())), preferred_element_type=jnp.float32
    )


def per_device(
    layer_input,
    cotangent,
    segment_ids,
    query_weight,
    key_weight,
    value_weight,
    output_weight,
    gate_weight,
    up_weight,
    down_weight,
    first_gain,
    first_bias,
    second_gain,
    second_bias,
):
    model_width = layer_input.shape[2]
    length = segment_ids.shape[1]
    block_rows = min(512, length)
    block_count = length // block_rows
    local_heads = query_weight.shape[1] // HD
    local_width = local_heads * HD
    score_scale = HD ** (-0.5)
    cos_table, sine_table = rotary_tables(length, HD)

    def fetch_weights():
        row_parts = (
            lax.all_gather(query_weight, "dp", axis=0, tiled=True),
            lax.all_gather(key_weight, "dp", axis=0, tiled=True),
            lax.all_gather(value_weight, "dp", axis=0, tiled=True),
            lax.all_gather(gate_weight, "dp", axis=0, tiled=True),
            lax.all_gather(up_weight, "dp", axis=0, tiled=True),
        )
        col_parts = (
            lax.all_gather(output_weight, "dp", axis=1, tiled=True),
            lax.all_gather(down_weight, "dp", axis=1, tiled=True),
        )
        return tuple(row_parts) + tuple(col_parts)

    def micro_step(weights, row_input, row_cotangent, segment_row):
        query_full, key_full, value_full, gate_full, up_full, output_full, down_full = weights
        full_input = lax.all_gather(row_input, "tensor", axis=0, tiled=True)
        query_pre = jnp.dot(full_input, query_full, preferred_element_type=jnp.float32).reshape(
            length, local_heads, HD
        )
        key_pre = jnp.dot(full_input, key_full, preferred_element_type=jnp.float32).reshape(
            length, local_heads, HD
        )
        value_rows = (
            jnp.dot(full_input, value_full, preferred_element_type=jnp.float32)
            .astype(jnp.bfloat16)
            .reshape(length, local_heads, HD)
        )
        query_rows = rotate(query_pre, cos_table, sine_table).astype(jnp.bfloat16)
        key_rows = rotate(key_pre, cos_table, sine_table).astype(jnp.bfloat16)
        query_blocks = query_rows.reshape(block_count, block_rows, local_heads, HD)
        segment_blocks = segment_row.reshape(block_count, block_rows)

        def block_scores(query_block, segment_block):
            scores = (
                jnp.einsum(
                    "qhd,khd->hqk", query_block, key_rows, preferred_element_type=jnp.float32
                )
                * score_scale
            )
            allowed = segment_block[:, None] == segment_row[None, :]
            return jnp.where(allowed[None, :, :], scores, mask_fill)

        def attend_forward(block_inputs):
            scores = block_scores(block_inputs[0], block_inputs[1])
            row_max = jnp.max(scores, axis=-1, keepdims=True)
            exponent_terms = jnp.exp(scores - row_max)
            row_total = jnp.sum(exponent_terms, axis=-1, keepdims=True)
            probabilities = (exponent_terms / row_total).astype(jnp.bfloat16)
            mixed_rows = jnp.einsum(
                "hqk,khd->qhd", probabilities, value_rows, preferred_element_type=jnp.float32
            )
            return (mixed_rows, (row_max + jnp.log(row_total))[..., 0])

        mixed_blocks, log_totals = lax.map(attend_forward, (query_blocks, segment_blocks))
        attended = mixed_blocks.reshape(length, local_width).astype(jnp.bfloat16)
        attention_branch = lax.psum_scatter(
            jnp.dot(attended, output_full, preferred_element_type=jnp.float32).astype(jnp.bfloat16),
            "tensor",
            scatter_dimension=0,
            tiled=True,
        ).astype(jnp.float32)
        first_sum = row_input.astype(jnp.float32) + attention_branch
        hidden_state, first_back = jax.vjp(layer_norm, first_sum, first_gain, first_bias)
        full_hidden = lax.all_gather(
            hidden_state.astype(jnp.bfloat16), "tensor", axis=0, tiled=True
        )
        gate_pre = jnp.dot(full_hidden, gate_full, preferred_element_type=jnp.float32)
        up_pre = jnp.dot(full_hidden, up_full, preferred_element_type=jnp.float32)
        activated_exact, swiglu_back = jax.vjp(swiglu, gate_pre, up_pre)
        activated = activated_exact.astype(jnp.bfloat16)
        feed_branch = lax.psum_scatter(
            jnp.dot(activated, down_full, preferred_element_type=jnp.float32).astype(jnp.bfloat16),
            "tensor",
            scatter_dimension=0,
            tiled=True,
        ).astype(jnp.float32)
        layer_output, second_back = jax.vjp(
            layer_norm, hidden_state + feed_branch, second_gain, second_bias
        )
        grad_second_sum, grad_second_gain, grad_second_bias = second_back(
            row_cotangent.astype(jnp.float32)
        )
        grad_second_full = lax.all_gather(
            grad_second_sum.astype(jnp.bfloat16), "tensor", axis=0, tiled=True
        )
        grad_activated = times_transpose(grad_second_full, down_full)
        grad_down = contract_rows(activated, grad_second_full)
        grad_gate_pre, grad_up_pre = swiglu_back(grad_activated)
        gate_low = grad_gate_pre.astype(jnp.bfloat16)
        up_low = grad_up_pre.astype(jnp.bfloat16)
        grad_hidden = grad_second_sum + lax.psum_scatter(
            (times_transpose(gate_low, gate_full) + times_transpose(up_low, up_full)).astype(
                jnp.bfloat16
            ),
            "tensor",
            scatter_dimension=0,
            tiled=True,
        ).astype(jnp.float32)
        grad_gate = contract_rows(full_hidden, gate_low)
        grad_up = contract_rows(full_hidden, up_low)
        grad_first_sum, grad_first_gain, grad_first_bias = first_back(grad_hidden)
        grad_first_full = lax.all_gather(
            grad_first_sum.astype(jnp.bfloat16), "tensor", axis=0, tiled=True
        )
        grad_attended = (
            times_transpose(grad_first_full, output_full)
            .astype(jnp.bfloat16)
            .reshape(block_count, block_rows, local_heads, HD)
        )
        grad_output = contract_rows(attended, grad_first_full)

        def attend_backward(sums_carry, block_inputs):
            key_sum, value_sum = sums_carry
            query_block, segment_block, log_block, grad_block = block_inputs
            scores = block_scores(query_block, segment_block)
            probabilities = jnp.exp(scores - log_block[..., None])
            grad_softmax = jnp.einsum(
                "qhd,khd->hqk", grad_block, value_rows, preferred_element_type=jnp.float32
            )
            value_sum = value_sum + jnp.einsum(
                "hqk,qhd->khd",
                probabilities.astype(jnp.bfloat16),
                grad_block,
                preferred_element_type=jnp.float32,
            )
            row_inner = jnp.sum(probabilities * grad_softmax, axis=-1, keepdims=True)
            grad_scores = (probabilities * (grad_softmax - row_inner)).astype(jnp.bfloat16)
            grad_query_block = (
                jnp.einsum(
                    "hqk,khd->qhd", grad_scores, key_rows, preferred_element_type=jnp.float32
                )
                * score_scale
            )
            key_sum = (
                key_sum
                + jnp.einsum(
                    "hqk,qhd->khd", grad_scores, query_block, preferred_element_type=jnp.float32
                )
                * score_scale
            )
            return ((key_sum, value_sum), grad_query_block)

        zero_heads = jnp.zeros((length, local_heads, HD), jnp.float32)
        (grad_key_rot, grad_value_rows), grad_query_blocks = lax.scan(
            attend_backward,
            (zero_heads, zero_heads),
            (query_blocks, segment_blocks, log_totals, grad_attended),
        )
        grad_query_low = (
            rotate(grad_query_blocks.reshape(length, local_heads, HD), cos_table, -sine_table)
            .astype(jnp.bfloat16)
            .reshape(length, local_width)
        )
        grad_key_low = (
            rotate(grad_key_rot, cos_table, -sine_table)
            .astype(jnp.bfloat16)
            .reshape(length, local_width)
        )
        grad_value_low = grad_value_rows.astype(jnp.bfloat16).reshape(length, local_width)
        query_part = times_transpose(grad_query_low, query_full)
        key_part = times_transpose(grad_key_low, key_full)
        value_part = times_transpose(grad_value_low, value_full)
        grad_input = grad_first_sum + lax.psum_scatter(
            (query_part + key_part + value_part).astype(jnp.bfloat16),
            "tensor",
            scatter_dimension=0,
            tiled=True,
        ).astype(jnp.float32)
        row_grads = (
            contract_rows(full_input, grad_query_low),
            contract_rows(full_input, grad_key_low),
            contract_rows(full_input, grad_value_low),
            grad_gate,
            grad_up,
        )
        col_grads = (grad_output, grad_down)
        norm_parts = (grad_first_gain, grad_first_bias, grad_second_gain, grad_second_bias)
        return (
            layer_output.astype(jnp.bfloat16),
            grad_input.astype(jnp.bfloat16),
            (row_grads, col_grads, norm_parts),
        )

    norm_zero = tuple(
        (
            jnp.zeros(gain_like.shape, jnp.float32)
            for gain_like in (first_gain, first_bias, second_gain, second_bias)
        )
    )
    row_zero = tuple(
        (
            jnp.zeros((model_width, weight_part.shape[1]), jnp.float32)
            for weight_part in (query_weight, key_weight, value_weight, gate_weight, up_weight)
        )
    )
    col_zero = (
        jnp.zeros((output_weight.shape[0], model_width), jnp.float32),
        jnp.zeros((down_weight.shape[0], model_width), jnp.float32),
    )

    def scan_step(totals, batch_rows):
        weights = fetch_weights()
        layer_output, grad_input, grad_terms = micro_step(
            weights, batch_rows[0], batch_rows[1], batch_rows[2]
        )
        return (jax.tree.map(jnp.add, totals, grad_terms), (layer_output, grad_input))

    totals, (outputs, grad_inputs) = lax.scan(
        scan_step, (row_zero, col_zero, norm_zero), (layer_input, cotangent, segment_ids)
    )
    row_grads, col_grads, norm_parts = totals
    row_done = lax.psum_scatter(row_grads, "dp", scatter_dimension=0, tiled=True)
    col_done = (
        lax.psum_scatter(col_grads[0], "dp", scatter_dimension=1, tiled=True),
        lax.psum_scatter(col_grads[1], "dp", scatter_dimension=1, tiled=True),
    )
    norm_done = lax.psum(norm_parts, ("dp", "tensor"))
    totals = (tuple(row_done), tuple(col_done), tuple(norm_done))
    row_done, col_done, norm_done = totals
    return (
        outputs,
        grad_inputs,
        row_done[0],
        row_done[1],
        row_done[2],
        col_done[0],
        row_done[3],
        row_done[4],
        col_done[1],
        norm_done[0],
        norm_done[1],
        norm_done[2],
        norm_done[3],
    )


F32 = jnp.float32
BF16 = jnp.bfloat16
NY = 2
LANES = 128
IDS = 16
MESH = pl.DeviceIdType.MESH


def mm(left, right):
    return lax.dot_general(left, right, (((1,), (0,)), ((), ())), preferred_element_type=F32)


def mt(left, right):
    return lax.dot_general(left, right, (((1,), (1,)), ((), ())), preferred_element_type=F32)


def lane_tables(length):
    half = HD // 2
    steps = np.arange(half, dtype=np.float32)
    frequency = np.float32(rope_base) ** (-(np.float32(2.0) * steps) / np.float32(HD))
    angles = np.arange(length, dtype=np.float32)[:, None] * frequency[None, :]
    angles = angles.astype(np.float32)
    cos, sin = np.cos(angles).astype(np.float32), np.sin(angles).astype(np.float32)
    cos_lane = np.concatenate([cos] * 4, axis=1)
    sin_lane = np.concatenate([-sin, sin, -sin, sin], axis=1)
    return cos_lane, sin_lane, np.ascontiguousarray(cos.T), np.ascontiguousarray(sin.T)


def norm_of(v):
    mu = jnp.mean(v, axis=-1, keepdims=True)
    cen = v - mu
    rstd = lax.rsqrt(jnp.mean(cen * cen, axis=-1, keepdims=True) + eps_norm)
    return cen * rstd, rstd


def grad_of_norm(dn, n, rstd):
    m0 = jnp.mean(dn, axis=-1, keepdims=True)
    m1 = jnp.mean(dn * n, axis=-1, keepdims=True)
    return (dn - m0 - n * m1) * rstd


def colsum(v):
    return jnp.sum(v, axis=0, keepdims=True)


def layer_kernel(
    nz,
    xin,
    cot,
    seg_h,
    wq_h,
    wk_h,
    wv_h,
    wo_h,
    wg_h,
    wu_h,
    wd_h,
    g1_h,
    b1_h,
    g2_h,
    b2_h,
    cosl_h,
    sinl_h,
    cosf_h,
    sinf_h,
    out_h,
    gin_h,
    gw_h,
    ng_out,
    W,
    G,
    S1X,
    S1Y,
    S2X,
    S2Y,
    ZR,
    X,
    XT,
    TT,
    DT,
    CT,
    SEGQ,
    SEGK,
    COSL,
    SINL,
    COSF,
    SINF,
    PK,
    QZ,
    KT,
    VT,
    LSE,
    DEL,
    ATT,
    ATTT,
    N1,
    F4,
    GP,
    UP,
    RR,
    DZ,
    CXS,
    CXR,
    ACC,
    OB,
    DKA,
    DVA,
    SEG,
    WQ,
    WK,
    WV,
    WO,
    VEC,
    NG,
    NR,
    NS,
    NZR,
    ZB,
    loc,
    ssem,
    rsem,
):
    quarter, width = X.shape[1], X.shape[2]
    length = 4 * quarter
    rows = W.shape[4]
    dp = lax.axis_index("dp")
    tt = lax.axis_index("tensor")
    c = lax.rem(tt, 2)
    xi = lax.div(tt, 2)
    z = lax.div(dp, NY)
    y = lax.rem(dp, NY)
    oy = 1 - y
    t_x = lax.rem(tt + 2, 4)
    dev_x = (dp, t_x)
    dev_c = (dp, tt + 1 - 2 * c)
    dev_y = (dp + 1 - 2 * y, tt)
    zs = [lax.rem(z + j, nz) for j in range(nz)]
    zfrom = [lax.rem(z + nz - j, nz) for j in range(nz)]
    dev_z = [(zs[j] * NY + y, tt) for j in range(nz)]
    hz = nz // 2
    count = [0]
    lcount = [0]
    sends = {}

    def rc(src, dst, dev):
        i = count[0]
        count[0] += 1
        copy = pltpu.make_async_remote_copy(
            src_ref=src,
            dst_ref=dst,
            send_sem=ssem.at[i],
            recv_sem=rsem.at[i],
            device_id=dev,
            device_id_type=MESH,
        )
        copy.start()
        sends[id(copy)] = copy
        return copy

    def sent(copy):
        copy.wait_send()
        del sends[id(copy)]

    def lc(src, dst):
        i = lcount[0]
        lcount[0] += 1
        copy = pltpu.make_async_copy(src, dst, loc.at[i])
        copy.start()
        return copy

    l_out, l_att = lc(wo_h, WO), [lc(wq_h, WQ), lc(wk_h, WK), lc(wv_h, WV)]
    l_w = [lc(wg_h, W.at[1, 0, z, y]), lc(wu_h, W.at[2, 0, z, y]), lc(wd_h, W.at[3, 0, z, y])]
    l_seg = lc(seg_h, SEG)
    l_vec = [lc(h, VEC.at[i, 0]) for i, h in enumerate((g1_h, b1_h, g2_h, b2_h))]
    l_x = lc(xin.at[xi], X.at[tt])
    l_ct = lc(cot.at[xi], CT.at[xi])
    l_tab = [lc(cosl_h, COSL), lc(sinl_h, SINL), lc(cosf_h, COSF), lc(sinf_h, SINF)]

    barrier = pltpu.get_barrier_semaphore()
    peers = [dev_x, dev_c, dev_y] + dev_z[1:]
    for dev in peers:
        pl.semaphore_signal(barrier, inc=1, device_id=dev, device_id_type=MESH)
    l_out.wait()
    for copy in l_att:
        copy.wait()
    shards = [W.at[0, 0, z, y], wg_h, wu_h, wd_h]
    two = 2 * HD
    turned_out = WO[...].T
    shards[0][:, :two] = WQ[:, :two]
    shards[0][:, two : 2 * two] = WK[:, :two]
    shards[0][:, 2 * two : 3 * two] = WV[:, :two]
    shards[0][:, 3 * two : 4 * two] = jnp.concatenate([WQ[:, two:], WK[:, two:]], axis=1)
    shards[0][:, 4 * two : 5 * two] = jnp.concatenate([WV[:, two:], turned_out[:, two:]], axis=1)
    shards[0][:, 5 * two :] = turned_out[:, :two]
    pl.semaphore_wait(barrier, len(peers))

    ag = {}
    split = width // 3
    pieces = [
        (0, 0, width),
        (1, 0, width),
        (2, 0, width),
        (3, 0, split),
        (3, split, width - split),
        (0, 0, 3 * LANES),
        (0, 3 * LANES, 2 * LANES),
        (0, 5 * LANES, LANES),
    ]
    LAST, QKV, REST, OUT = 4, 5, 6, 7

    def cut(view, p):
        _, lo, n = pieces[p]
        return view if n == width else view.at[..., pl.ds(lo, n)]

    def w_at(p, s, zz, yy):
        return cut(W.at[pieces[p][0], s, zz, yy], p)

    def own_shard(p):
        return cut(shards[pieces[p][0]], p)

    def e1_plane(p):
        own = own_shard(p)
        ag[p, "x"] = [rc(own, w_at(p, 1, z, y), dev_x)]
        ag[p, "y"] = [rc(own, w_at(p, 0, z, y), dev_y)]

    def e1(p):
        own = own_shard(p)
        ag[p, "z"] = [rc(own, w_at(p, 0, z, y), dev_z[j]) for j in range(1, nz)]
        e1_plane(p)

    def e2(p):
        for j in range(1, nz):
            ag[p, "z"][j - 1].wait_recv()
            part = w_at(p, 0, zfrom[j], y)
            ag[p, "x"].append(rc(part, w_at(p, 1, zfrom[j], y), dev_x))
            ag[p, "y"].append(rc(part, part, dev_y))

    def e3(p, by_x):
        ag[p, "d"] = []
        for j in range(nz):
            ag[p, "x"][j].wait_recv()
            if j < nz - by_x:
                part = w_at(p, 1, zfrom[j], y)
                ag[p, "d"].append(rc(part, part, dev_y))
            ag[p, "y"][j].wait_recv()
            if j >= nz - by_x:
                ag[p, "d"].append(rc(w_at(p, 0, zfrom[j], oy), w_at(p, 1, zfrom[j], oy), dev_x))

    def e4(p):
        for copy in ag[p, "d"]:
            copy.wait_recv()

    top_rows, low_rows = pl.ds(0, rows // 2), pl.ds(rows // 2, rows // 2)

    def f2(p):
        ag[p, "x"][0].wait_recv()
        part = w_at(p, 1, z, y).at[top_rows]
        ag[p, "d"] = [rc(part, part, dev_y)]
        ag[p, "y"][0].wait_recv()
        ag[p, "d"].append(
            rc(w_at(p, 0, z, oy).at[low_rows], w_at(p, 1, z, oy).at[low_rows], dev_x)
        )

    def f3(p):
        for copy in ag[p, "d"]:
            copy.wait_recv()
        plane = cut(W.at[3, :, z], p)
        ag[p, "z"] = [rc(plane, plane, dev_z[j]) for j in range(1, nz)]

    def f4(p):
        for copy in ag[p, "z"]:
            copy.wait_recv()

    def e_sent(p):
        for copy in ag[p, "z"] + ag[p, "x"] + ag[p, "y"] + ag[p, "d"]:
            sent(copy)

    e1(0)
    e1(3)
    e1_plane(LAST)
    e1(2)
    x_far = rc(xin.at[1 - xi], X.at[tt], dev_x)
    x_core = rc(xin.at[xi], X.at[tt], dev_c)

    l_seg.wait()
    seg = SEG
    g1_ref, b1_ref, g2_ref, b2_ref = (VEC.at[i] for i in range(4))
    row_ids = jnp.broadcast_to(seg[pl.ds(xi, 1), :], (LANES, length))
    same = row_ids == lax.broadcasted_iota(jnp.int32, (LANES, length), 0)
    known = lax.broadcasted_iota(jnp.int32, (LANES, length), 0) < IDS
    SEGQ[...] = jnp.where(jnp.logical_or(same, jnp.logical_not(known)), 0.0, mask_fill).astype(BF16)
    SEGK[...] = jnp.where(same, 1.0, 0.0).astype(F32).T.astype(BF16)
    NG[...] = jnp.zeros_like(NG)
    lane = lax.broadcasted_iota(jnp.int32, (1, LANES), 1)
    low_half = lane < HD
    swap_low = lax.rem(lane, HD) < (HD // 2)

    def swap(v):
        return jnp.where(swap_low, pltpu.roll(v, LANES - HD // 2, 1), pltpu.roll(v, HD // 2, 1))

    def at_quarter(i):
        return pl.ds(pl.multiple_of(i * quarter, quarter), quarter)

    def wmat(k, s, lo=0, hi=None):
        hi = width if hi is None else hi
        return W[k, s, :, :, :, lo:hi].reshape(width, hi - lo)

    def turn_rows(src, dst):
        def step(i, _):
            dst[:, at_quarter(i)] = src[i].T
            return 0

        lax.fori_loop(0, 4, step, 0)

    f2(LAST)
    e1(1)
    e2(0)
    x_far.wait_recv()
    x_core2 = rc(X.at[t_x], X.at[t_x], dev_c)
    x_core.wait_recv()
    l_x.wait()
    l_ct.wait()
    for copy in l_w + l_vec + l_tab:
        copy.wait()
    x_core2.wait_recv()
    turn_rows(X, XT)
    e2(3)
    f3(LAST)
    e3(0, 1)

    def project(s):
        def step(i, _):
            at = at_quarter(i)
            y5 = mm(X[i], wmat(0, s, 0, 5 * LANES))
            cos, sin = COSL[at, :], SINL[at, :]
            turned = []
            for b in range(5):
                v = y5[:, b * LANES : (b + 1) * LANES]
                if b in (0, 1, 3):
                    v = v * cos + swap(v) * sin
                v = v.astype(BF16)
                PK[s, b, at, :] = v
                turned.append(v.T)
            zero = jnp.zeros((HD, quarter), BF16)
            q0 = turned[0] * BF16(0.125)
            q2 = turned[3] * BF16(0.125)
            QZ[3 * s, :HD, at] = q0[:HD]
            QZ[3 * s, HD:, at] = zero
            QZ[3 * s + 1, :HD, at] = zero
            QZ[3 * s + 1, HD:, at] = q0[HD:]
            QZ[3 * s + 2, :HD, at] = zero
            QZ[3 * s + 2, HD:, at] = q2[:HD]
            KT[3 * s, :, at] = turned[1][:HD]
            KT[3 * s + 1, :, at] = turned[1][HD:]
            KT[3 * s + 2, :, at] = turned[3][HD:]
            VT[3 * s, :, at] = turned[2][:HD]
            VT[3 * s + 1, :, at] = turned[2][HD:]
            VT[3 * s + 2, :, at] = turned[4][:HD]
            return 0

        lax.fori_loop(0, 4, step, 0)

    def spans():
        for qb in range(4):
            lo = max(0, qb * quarter - length // 2 + 1) // quarter * quarter
            hi = min(length, -(-(qb * quarter + quarter - 1 + length // 2) // quarter) * quarter)
            yield pl.ds(qb * quarter, quarter), pl.ds(lo, hi - lo)

    def scores_of(s, hh, h, at, keys):
        left = jnp.concatenate([PK[s, 1 + 2 * lax.div(hh, 2), keys, :], SEGK[keys, :]], axis=1)
        right = jnp.concatenate([QZ[h, :, at], SEGQ[:, at]], axis=0)
        return mm(left, right)

    def attend(first, heads):
        def step(n, _):
            h = first + n
            s, hh = lax.div(h, 3), lax.rem(h, 3)
            for at, keys in spans():
                st = scores_of(s, hh, h, at, keys)
                top = jnp.max(st, axis=0, keepdims=True)
                p = jnp.exp(st - top)
                total = jnp.sum(p, axis=0, keepdims=True)
                ot = mm(VT[h, :, keys], p.astype(BF16)) * (1.0 / total)
                LSE[pl.ds(h, 1), at] = top + jnp.log(total)
                ATTT[h, :, at] = ot.astype(BF16)
            return 0

        lax.fori_loop(0, heads, step, 0)

    def turn_heads(s):
        def turn(i, _):
            at = at_quarter(i)
            pair = jnp.concatenate([ATTT[3 * s, :, at], ATTT[3 * s + 1, :, at]], axis=0)
            lone = jnp.concatenate([jnp.zeros((HD, quarter), BF16), ATTT[3 * s + 2, :, at]], axis=0)
            ATT[s, at, :LANES] = lone.T
            ATT[s, at, LANES:] = pair.T
            return 0

        lax.fori_loop(0, 4, turn, 0)

    project(0)
    e2(2)
    e3(3, 1)
    e4(0)
    project(1)
    e2(1)
    attend(0, 2)
    e3(2, 2)
    attend(2, 2)
    e4(3)
    attend(4, 2)
    e3(1, 2)
    turn_heads(0)
    turn_heads(1)
    last_exchange = []

    def exchange(n, part):
        if last_exchange:
            sent(last_exchange.pop())

        def other(k, _):
            CXS[k] = part(1 - c + 2 * k).astype(BF16)
            return 0

        lax.fori_loop(0, 2, other, 0)
        copy = rc(CXS, CXR.at[n % 2], dev_c)
        last_exchange.append(copy)

        def own(k, _):
            ACC[k] = part(c + 2 * k)
            return 0

        lax.fori_loop(0, 2, own, 0)
        copy.wait_recv()

    def spread():
        return [rc(F4.at[c + 2 * k], F4.at[c + 2 * k], dev_c) for k in range(2)]

    def out_part(i):
        at = at_quarter(i)
        return mt(ATT[0, at, :], wmat(0, 0, 4 * LANES)) + mt(ATT[1, at, :], wmat(0, 1, 4 * LANES))

    exchange(0, out_part)
    ct_far = rc(cot.at[1 - xi], CT.at[xi], dev_x)
    tile = quarter // 2

    def over_tiles(fn):
        def step(n, _):
            k = lax.div(n, 2)
            fn(k, c + 2 * k, pl.ds(pl.multiple_of(lax.rem(n, 2) * tile, tile), tile))
            return 0

        lax.fori_loop(0, 4, step, 0)

    def kept_rows(k, at):
        return pl.ds(pl.multiple_of(k * quarter + at.start, tile), tile)

    def first_norm(k, i, at):
        z1 = X[i, at, :].astype(F32) + ACC[k, at, :] + CXR[0, k, at, :].astype(F32)
        n1, rstd = norm_of(z1)
        N1[k, at, :] = n1
        DKA[kept_rows(k, at), :] = jnp.broadcast_to(rstd, (tile, LANES))
        F4[i, at, :] = (n1 * g1_ref[...] + b1_ref[...]).astype(BF16)

    over_tiles(first_norm)
    h_copies = spread()
    for copy in h_copies:
        copy.wait_recv()
    turn_rows(F4, TT)

    def ff_up(s, i):
        at = at_quarter(i)
        g = mm(F4[i], wmat(1, s))
        u = mm(F4[i], wmat(2, s))
        GP[s, at, :] = g.astype(BF16)
        UP[s, at, :] = u.astype(BF16)
        RR[s, at, :] = (g * jax.nn.sigmoid(g) * u).astype(BF16)
        return 0

    lax.fori_loop(0, 4, lambda i, _: ff_up(0, i), 0)
    e4(2)
    e4(1)
    lax.fori_loop(0, 4, lambda i, _: ff_up(1, i), 0)
    f4(LAST)

    def down_part(i):
        at = at_quarter(i)
        return mt(RR[0, at, :], wmat(3, 0)) + mt(RR[1, at, :], wmat(3, 1))

    for copy in h_copies:
        sent(copy)
    exchange(1, down_part)
    ct_far.wait_recv()

    def second_norm(k, i, at):
        h = N1[k, at, :] * g1_ref[...] + b1_ref[...]
        z2 = h + ACC[k, at, :] + CXR[1, k, at, :].astype(F32)
        n2, rstd = norm_of(z2)
        OB[k, at, :] = (n2 * g2_ref[...] + b2_ref[...]).astype(BF16)
        dy = CT[k, at, :].astype(F32)
        NG[2:3, :] += colsum(dy * n2)
        NG[3:4, :] += colsum(dy)
        dz = grad_of_norm(dy * g2_ref[...], n2, rstd)
        DZ[k, at, :] = dz
        F4[i, at, :] = dz.astype(BF16)

    over_tiles(second_norm)
    d_copies = spread()
    o_far = rc(OB.at[1 - xi], out_h.at[xi], dev_x)
    o_own = lc(OB.at[xi], out_h.at[xi])

    slots = {3: G, 1: W.at[3], 2: W.at[1], 0: W.at[2]}
    rs = {}
    by_x = {1: 1, 2: 2, 3: 1, QKV: 2, REST: 2, OUT: 1}

    def g_at(p, s, zz, yy):
        return cut(slots[pieces[p][0]].at[s, zz, yy], p)

    def into(ref, p, *at):
        return cut(ref.at[(pieces[p][0],) + at], p)

    def plus(target, *others):
        total = target[...].astype(F32)
        for other in others:
            total = total + other[...].astype(F32)
        target[...] = total.astype(BF16)

    def early(p):
        return pl.ds(0, by_x[p]), pl.ds(by_x[p], nz - by_x[p])

    def r1_far(p):
        nx = by_x[p]
        near, far = early(p)
        rs[p, "dx"] = rc(g_at(p, 1, near, oy), into(S1X, p, pl.ds(0, nx)), dev_x)
        rs[p, "dy"] = rc(g_at(p, 1, far, oy), into(S1Y, p, pl.ds(0, nz - nx)), dev_y)
        rs[p, "x0"] = rc(g_at(p, 1, near, y), into(S2X, p, near), dev_x)

    def r1_near(p):
        _, far = early(p)
        rs[p, "y0"] = rc(g_at(p, 0, far, oy), into(S2Y, p, far), dev_y)

    def r2(p):
        nx = by_x[p]
        near, far = early(p)
        rs[p, "dx"].wait_recv()
        for j in range(nx):
            plus(g_at(p, 0, j, oy), into(S1X, p, j))
        rs[p, "y1"] = rc(g_at(p, 0, near, oy), into(S2Y, p, near), dev_y)
        rs[p, "dy"].wait_recv()
        for j in range(nx, nz):
            plus(g_at(p, 1, j, y), into(S1Y, p, j - nx))
        rs[p, "x1"] = rc(g_at(p, 1, far, y), into(S2X, p, far), dev_x)

    def r3(p):
        for name in ("x0", "y0", "y1", "x1"):
            rs[p, name].wait_recv()
        for j in range(nz):
            plus(g_at(p, 0, j, y), into(S2X, p, j), into(S2Y, p, j))
        rs[p, "z"] = [rc(g_at(p, 0, zs[j], y), into(ZR, p, z), dev_z[j]) for j in range(1, nz)]

    def place(p):
        k = pieces[p][0]
        return cut(N1.at[k // 2, pl.ds((k % 2) * rows, rows)], p)

    def r4(p):
        for copy in rs[p, "z"]:
            copy.wait_recv()
        total = g_at(p, 0, z, y)[...].astype(F32)
        for j in range(1, nz):
            total = total + into(ZR, p, zfrom[j])[...].astype(F32)
        target = place(p)
        target[...] = total
        rs[p, "out"] = lc(target, cut(gw_h.at[pieces[p][0]], p))

    def q1(p):
        rs[p, "z"] = [
            rc(cut(slots[3].at[:, zs[j]], p), ZB.at[z], dev_z[j]) for j in range(1, nz)
        ]

    def q2(p):
        for copy in rs[p, "z"]:
            copy.wait_recv()
        for s in range(2):
            for yy in range(NY):
                plus(g_at(p, s, z, yy), *(ZB.at[zfrom[j], s, yy] for j in range(1, nz)))
        rs[p, "dx"] = rc(g_at(p, 1, z, oy).at[top_rows], into(S1X, p, 0).at[top_rows], dev_x)
        rs[p, "dy"] = rc(g_at(p, 1, z, oy).at[low_rows], into(S1Y, p, 0).at[low_rows], dev_y)
        rs[p, "x0"] = rc(g_at(p, 1, z, y).at[top_rows], into(S2X, p, 0).at[top_rows], dev_x)
        rs[p, "y0"] = rc(g_at(p, 0, z, oy).at[low_rows], into(S2Y, p, 0).at[low_rows], dev_y)

    def q3(p):
        rs[p, "dx"].wait_recv()
        plus(g_at(p, 0, z, oy).at[top_rows], into(S1X, p, 0).at[top_rows])
        rs[p, "y1"] = rc(g_at(p, 0, z, oy).at[top_rows], into(S2Y, p, 0).at[top_rows], dev_y)
        rs[p, "dy"].wait_recv()
        plus(g_at(p, 1, z, y).at[low_rows], into(S1Y, p, 0).at[low_rows])
        rs[p, "x1"] = rc(g_at(p, 1, z, y).at[low_rows], into(S2X, p, 0).at[low_rows], dev_x)

    def q4(p):
        for name in ("x0", "y0", "y1", "x1"):
            rs[p, name].wait_recv()
        total = g_at(p, 0, z, y)[...].astype(F32)
        total = total + into(S2X, p, 0)[...].astype(F32) + into(S2Y, p, 0)[...].astype(F32)
        target = place(p)
        target[...] = total
        rs[p, "out"] = lc(target, cut(gw_h.at[3], p))

    def weight_grad(p, s, left, right):
        k, lo, n = pieces[p]
        block = NY * rows

        def step(j, _):
            at = pl.ds(pl.multiple_of(j * block, block), block)
            part = mm(left[at, :], right[s, :, lo : lo + n]).astype(BF16)
            slots[k][s, j, :, :, lo : lo + n] = part.reshape(NY, rows, n)
            return 0

        lax.fori_loop(0, nz, step, 0)


    def turn_half(first):
        def step(k, _):
            i = first + 2 * k
            DT[:, at_quarter(i)] = F4[i].T
            return 0

        lax.fori_loop(0, 2, step, 0)

    turn_half(c)
    for copy in d_copies:
        copy.wait_recv()
    turn_half(1 - c)
    weight_grad(LAST, 0, DT, RR)
    weight_grad(LAST, 1, DT, RR)
    q1(LAST)
    weight_grad(3, 1, DT, RR)
    weight_grad(3, 0, DT, RR)
    r1_far(3)
    r1_near(3)

    def ff_back(n, _):
        s = lax.div(n, 4)
        i = lax.rem(n, 4)
        at = at_quarter(i)
        dr = mm(F4[i], wmat(3, s))
        g = GP[s, at, :].astype(F32)
        u = UP[s, at, :].astype(F32)
        sg = jax.nn.sigmoid(g)
        GP[s, at, :] = (dr * u * sg * (1.0 + g * (1.0 - sg))).astype(BF16)
        UP[s, at, :] = (dr * g * sg).astype(BF16)
        return 0

    lax.fori_loop(0, 8, ff_back, 0)
    e_sent(3)
    e_sent(LAST)
    weight_grad(1, 1, TT, GP)
    r1_far(1)
    weight_grad(1, 0, TT, GP)
    r2(3)

    def hidden_part(i):
        at = at_quarter(i)
        return (
            mt(GP[0, at, :], wmat(1, 0))
            + mt(UP[0, at, :], wmat(2, 0))
            + mt(GP[1, at, :], wmat(1, 1))
            + mt(UP[1, at, :], wmat(2, 1))
        )

    for copy in d_copies:
        sent(copy)
    exchange(2, hidden_part)

    def first_norm_back(k, i, at):
        dh = DZ[k, at, :] + ACC[k, at, :] + CXR[0, k, at, :].astype(F32)
        n1 = N1[k, at, :]
        NG[0:1, :] += colsum(dh * n1)
        NG[1:2, :] += colsum(dh)
        dz = grad_of_norm(dh * g1_ref[...], n1, DKA[kept_rows(k, at), :1])
        DZ[k, at, :] = dz
        F4[i, at, :] = dz.astype(BF16)

    over_tiles(first_norm_back)
    b_copies = spread()
    n_core = rc(NG, NR.at[0], dev_c)
    e_sent(1)
    e_sent(2)
    r1_near(1)
    weight_grad(2, 1, TT, UP)
    r2(1)
    weight_grad(2, 0, TT, UP)
    for copy in b_copies:
        copy.wait_recv()
    n_core.wait_recv()
    NS[0] = NG[...] + NR[0]
    n_x = rc(NS.at[0], NR.at[1], dev_x)
    turn_rows(F4, DT)
    r1_far(2)
    def out_grad(n, _):
        s = lax.div(n, nz)
        j = lax.rem(n, nz)
        block = NY * rows
        at = pl.ds(pl.multiple_of(j * block, block), block)
        part = mm(DT[at, :], ATT[s]).astype(BF16)
        slots[0][s, j, :, :, 4 * LANES :] = part.reshape(NY, rows, 2 * LANES)
        return 0

    lax.fori_loop(0, 2 * nz, out_grad, 0)

    def head_lanes(h):
        return pl.ds(pl.multiple_of(h * LANES, LANES), LANES)

    def att_grad(i, _):
        at = at_quarter(i)
        for s in range(2):
            da = mm(F4[i], wmat(0, s, 4 * LANES))
            pair = da[:, LANES:]
            lone = pltpu.roll(da[:, :LANES], HD, 1)
            zero = jnp.zeros_like(pair)
            views = (
                jnp.where(low_half, pair, zero),
                jnp.where(low_half, zero, pair),
                jnp.where(low_half, lone, zero),
            )
            for hh in range(3):
                h = 3 * s + hh
                v = views[hh].astype(BF16)
                GP[0, at, h * LANES : (h + 1) * LANES] = v
                vt = v.T
                TT[h * LANES : (h + 1) * LANES, at] = vt
                part = vt[HD:] if hh == 1 else vt[:HD]
                DEL[h : h + 1, at] = colsum(part.astype(F32) * ATTT[h, :, at].astype(F32))
        return 0

    lax.fori_loop(0, 4, att_grad, 0)
    n_x.wait_recv()
    NS[1] = NS[0] + NR[1]
    n_y = rc(NS.at[1], NR.at[2], dev_y)
    def attend_back(s, first, heads):
        def head(hh, _):
            h = 3 * s + hh
            DKA[...] = jnp.zeros_like(DKA)
            DVA[...] = jnp.zeros_like(DVA)
            hl = head_lanes(h)

            for at, keys in spans():
                p = jnp.exp(scores_of(s, hh, h, at, keys) - LSE[pl.ds(h, 1), at])
                dpt = mm(PK[s, 2 + 2 * lax.div(hh, 2), keys, :], TT[hl, at])
                ds = (p * (dpt - DEL[pl.ds(h, 1), at])).astype(BF16)
                DVA[keys, :] += mm(p.astype(BF16), GP[0, at, hl])
                DKA[keys, :] += mm(ds, PK[s, 3 * lax.div(hh, 2), at, :])
                dq = mm(KT[h, :, keys], ds) * 0.125
                a, b = dq[: HD // 2], dq[HD // 2 :]
                cos, sin = COSF[:, at], SINF[:, at]
                VT[h, : HD // 2, at] = (a * cos + b * sin).astype(BF16)
                VT[h, HD // 2 :, at] = (b * cos - a * sin).astype(BF16)

            def finish(i, _):
                at = at_quarter(i)
                dk = DKA[at, :] * 0.125
                UP[0, at, hl] = (dk * COSL[at, :] - swap(dk) * SINL[at, :]).astype(BF16)
                GP[0, at, hl] = DVA[at, :].astype(BF16)
                return 0

            lax.fori_loop(0, 4, finish, 0)
            return 0

        lax.fori_loop(first, first + heads, head, 0)

    def join_heads(s):
        def gather(i, _):
            at = at_quarter(i)

            def part(ref, hh):
                h = 3 * s + hh
                return ref[0, at, h * LANES : (h + 1) * LANES].astype(F32)

            dq0 = jnp.concatenate([VT[3 * s, :, at], VT[3 * s + 1, :, at]], axis=0).T
            dq2 = jnp.concatenate([VT[3 * s + 2, :, at]] * 2, axis=0).T
            dk2 = pltpu.roll(part(UP, 2), HD, 1)
            dv2 = part(GP, 2)
            RR[s, at, 0:LANES] = dq0
            RR[s, at, LANES : 2 * LANES] = jnp.where(low_half, part(UP, 0), part(UP, 1)).astype(BF16)
            RR[s, at, 2 * LANES : 3 * LANES] = jnp.where(
                low_half, part(GP, 0), part(GP, 1)
            ).astype(BF16)
            RR[s, at, 3 * LANES : 4 * LANES] = jnp.where(low_half, dq2.astype(F32), dk2).astype(BF16)
            RR[s, at, 4 * LANES : 5 * LANES] = jnp.where(
                low_half, dv2, jnp.zeros_like(dv2)
            ).astype(BF16)
            return 0

        lax.fori_loop(0, 4, gather, 0)

    def in_grad(s, p):
        block = NY * rows
        _, lo, n = pieces[p]

        def step(j, _):
            at = pl.ds(pl.multiple_of(j * block, block), block)
            part = mm(XT[at, :], RR[s, :, lo : lo + n])
            if p == REST:
                mixed = slots[0][s, j, :, :, 4 * LANES : 5 * LANES].reshape(block, LANES)
                mixed = (part[:, LANES:] + mixed.astype(F32)).astype(BF16)
                part = part[:, :LANES]
                slots[0][s, j, :, :, 4 * LANES : 5 * LANES] = mixed.reshape(NY, rows, LANES)
                n_out = LANES
            else:
                n_out = n
            slots[0][s, j, :, :, lo : lo + n_out] = part.astype(BF16).reshape(NY, rows, n_out)
            return 0

        lax.fori_loop(0, nz, step, 0)

    attend_back(1, 0, 1)
    r1_near(2)
    r3(3)
    attend_back(1, 1, 1)
    r3(1)
    attend_back(1, 2, 1)
    r2(2)
    join_heads(1)
    r1_far(OUT)
    in_grad(1, QKV)
    r1_far(QKV)
    in_grad(1, REST)
    r1_near(OUT)
    n_y.wait_recv()
    NS[2] = NS[1] + NR[2]
    NZR[z] = NS[2]
    n_z = [rc(NS.at[2], NZR.at[z], dev_z[j]) for j in range(1, nz)]
    attend_back(0, 0, 2)
    r1_far(REST)
    r3(2)
    attend_back(0, 2, 1)
    r2(OUT)
    join_heads(0)
    in_grad(0, QKV)
    r1_near(QKV)
    r2(QKV)
    q2(LAST)
    r4(3)
    in_grad(0, REST)
    r1_near(REST)
    def input_part(i):
        at = at_quarter(i)
        return mt(RR[0, at, : 5 * LANES], wmat(0, 0, 0, 5 * LANES)) + mt(
            RR[1, at, : 5 * LANES], wmat(0, 1, 0, 5 * LANES)
        )

    exchange(3, input_part)

    def input_grad(k, i, at):
        g = DZ[k, at, :] + ACC[k, at, :] + CXR[1, k, at, :].astype(F32)
        CT[k, at, :] = g.astype(BF16)

    over_tiles(input_grad)
    r3(OUT)
    r2(REST)
    i_far = rc(CT.at[1 - xi], gin_h.at[xi], dev_x)
    i_own = lc(CT.at[xi], gin_h.at[xi])
    r4(1)
    r3(QKV)
    q3(LAST)
    for copy in n_z:
        copy.wait_recv()
    total = NZR[0]
    for j in range(1, nz):
        total = total + NZR[j]
    ng_out[...] = total
    r3(REST)
    r4(OUT)
    r4(2)
    r4(QKV)
    q4(LAST)
    r4(REST)
    o_far.wait_recv()
    i_far.wait_recv()
    o_own.wait()
    i_own.wait()
    for p in (1, 2, 3, LAST, QKV, REST, OUT):
        rs[p, "out"].wait()
    for copy in list(sends.values()):
        sent(copy)


def layer_per_device(
    dp_size,
    layer_input,
    cotangent,
    segment_ids,
    query_weight,
    key_weight,
    value_weight,
    output_weight,
    gate_weight,
    up_weight,
    down_weight,
    first_gain,
    first_bias,
    second_gain,
    second_bias,
):
    _, quarter, width = layer_input.shape
    length = 4 * quarter
    rows = query_weight.shape[0]
    nz = dp_size // NY
    tables = [jnp.asarray(t) for t in lane_tables(length)]
    anywhere = pl.BlockSpec(memory_space=pl.ANY)
    vmem = pl.BlockSpec(memory_space=pltpu.VMEM)
    half = HD // 2
    copies = 152
    part = query_weight.shape[1]
    scratch = [
        ((4, 2, nz, NY, rows, width), BF16),
        ((2, nz, NY, rows, width), BF16),
        ((4, nz // 2, rows, width), BF16),
        ((4, nz - 1, rows, width), BF16),
        ((4, nz, rows, width), BF16),
        ((4, nz, rows, width), BF16),
        ((4, nz, rows, width), BF16),
        ((4, quarter, width), BF16),
        ((width, length), BF16),
        ((width, length), BF16),
        ((width, length), BF16),
        ((2, quarter, width), BF16),
        ((LANES, length), BF16),
        ((length, LANES), BF16),
        ((length, LANES), F32),
        ((length, LANES), F32),
        ((half, length), F32),
        ((half, length), F32),
        ((2, 5, length, LANES), BF16),
        ((6, LANES, length), BF16),
        ((6, HD, length), BF16),
        ((6, HD, length), BF16),
        ((8, length), F32),
        ((8, length), F32),
        ((2, length, 2 * LANES), BF16),
        ((6, HD, length), BF16),
        ((2, quarter, width), F32),
        ((4, quarter, width), BF16),
        ((2, length, width), BF16),
        ((2, length, width), BF16),
        ((2, length, width), BF16),
        ((2, quarter, width), F32),
        ((2, quarter, width), BF16),
        ((2, 2, quarter, width), BF16),
        ((2, quarter, width), F32),
        ((2, quarter, width), BF16),
        ((length, LANES), F32),
        ((length, LANES), F32),
        ((2, length), jnp.int32),
        ((rows, part), BF16),
        ((rows, part), BF16),
        ((rows, part), BF16),
        ((part, rows), BF16),
        ((4, 1, width), F32),
        ((8, width), F32),
        ((3, 8, width), F32),
        ((3, 8, width), F32),
        ((nz, 8, width), F32),
        ((nz, 2, NY, rows, width - width // 3), BF16),
    ]
    outputs, grad_input, grads, norms = pl.pallas_call(
        functools.partial(layer_kernel, nz),
        out_shape=(
            jax.ShapeDtypeStruct(layer_input.shape, BF16),
            jax.ShapeDtypeStruct(layer_input.shape, BF16),
            jax.ShapeDtypeStruct((4, rows, width), F32),
            jax.ShapeDtypeStruct((8, width), F32),
        ),
        in_specs=[anywhere] * 18,
        out_specs=(anywhere, anywhere, anywhere, vmem),
        scratch_shapes=[pltpu.VMEM(shape, kind) for shape, kind in scratch]
        + [
            pltpu.SemaphoreType.DMA((27,)),
            pltpu.SemaphoreType.DMA((copies,)),
            pltpu.SemaphoreType.DMA((copies,)),
        ],
        compiler_params=pltpu.CompilerParams(
            collective_id=0, has_side_effects=True, vmem_limit_bytes=VMEM_BYTES
        ),
    )(
        layer_input,
        cotangent,
        segment_ids,
        query_weight,
        key_weight,
        value_weight,
        output_weight,
        gate_weight,
        up_weight,
        down_weight.T,
        first_gain,
        first_bias,
        second_gain,
        second_bias,
        *tables,
    )
    vector = jax.ShapeDtypeStruct((width,), F32)
    like = lambda a: jax.ShapeDtypeStruct(a.shape, F32)
    results = pl.pallas_call(
        place_kernel,
        out_shape=(
            jax.ShapeDtypeStruct(layer_input.shape, BF16),
            jax.ShapeDtypeStruct(layer_input.shape, BF16),
            like(query_weight),
            like(key_weight),
            like(value_weight),
            like(output_weight),
            like(gate_weight),
            like(up_weight),
            jax.ShapeDtypeStruct(down_weight.shape[::-1], F32),
            vector,
            vector,
            vector,
            vector,
        ),
        in_specs=[anywhere] * 4,
        out_specs=(anywhere, anywhere) + (vmem,) * 4 + (anywhere,) * 3 + (vmem,) * 4,
        scratch_shapes=[
            pltpu.VMEM(layer_input.shape, BF16),
            pltpu.VMEM(layer_input.shape, BF16),
            pltpu.VMEM((4, rows, width), F32),
            pltpu.VMEM((8, width), F32),
            pltpu.SemaphoreType.DMA((7,)),
            pltpu.SemaphoreType.DMA((5,)),
        ],
        compiler_params=pltpu.CompilerParams(vmem_limit_bytes=VMEM_BYTES),
    )(outputs, grad_input, grads, norms)
    return (*results[:8], results[8].T, *results[9:])


def place_kernel(
    out_i,
    gin_i,
    gw,
    ng,
    out_o,
    gin_o,
    gq,
    gk,
    gv,
    go,
    gg,
    gu,
    gd,
    n0,
    n1,
    n2,
    n3,
    OUT,
    GIN,
    GW,
    NB,
    sem,
    osem,
):
    loads = [
        pltpu.make_async_copy(src, dst, sem.at[i])
        for i, (src, dst) in enumerate(
            [
                (gw.at[0], GW.at[0]),
                (ng, NB),
                (gw.at[1], GW.at[1]),
                (gw.at[2], GW.at[2]),
                (gw.at[3], GW.at[3]),
                (out_i, OUT),
                (gin_i, GIN),
            ]
        )
    ]
    for copy in loads:
        copy.start()
    stores = [
        pltpu.make_async_copy(src, dst, osem.at[i])
        for i, (src, dst) in enumerate(
            [(GW.at[1], gg), (GW.at[2], gu), (GW.at[3], gd), (OUT, out_o), (GIN, gin_o)]
        )
    ]
    for load, store in zip(loads[2:], stores):
        load.wait()
        store.start()
    loads[0].wait()
    two = 2 * HD
    b = [GW[0, :, i * two : (i + 1) * two] for i in range(6)]
    gq[...] = jnp.concatenate([b[0], b[3][:, :HD]], axis=1)
    gk[...] = jnp.concatenate([b[1], b[3][:, HD:]], axis=1)
    gv[...] = jnp.concatenate([b[2], b[4][:, :HD]], axis=1)
    go[...] = jnp.concatenate([b[5], b[4][:, HD:]], axis=1).T
    loads[1].wait()
    for i, n in enumerate((n0, n1, n2, n3)):
        n[...] = NB[i, :]
    for store in stores:
        store.wait()


VMEM_BYTES = 64 << 20


def solution(mesh):
    in_specs = (
        P("dp", "tensor", None),
        P("dp", "tensor", None),
        P("dp", None),
        P("dp", "tensor"),
        P("dp", "tensor"),
        P("dp", "tensor"),
        P("tensor", "dp"),
        P("dp", "tensor"),
        P("dp", "tensor"),
        P("tensor", "dp"),
        P(),
        P(),
        P(),
        P(),
    )
    out_specs = (
        P("dp", "tensor", None),
        P("dp", "tensor", None),
        P("dp", "tensor"),
        P("dp", "tensor"),
        P("dp", "tensor"),
        P("tensor", "dp"),
        P("dp", "tensor"),
        P("dp", "tensor"),
        P("tensor", "dp"),
        P(),
        P(),
        P(),
        P(),
    )
    dp_size, tensor_size = mesh.shape["dp"], mesh.shape["tensor"]

    def whole(*arrays):
        layer_input, query_weight, gate_weight = arrays[0], arrays[3], arrays[7]
        batch, length, width = layer_input.shape
        fits = (
            tensor_size == 4
            and dp_size % (2 * NY) == 0
            and batch == 2 * dp_size
            and width % (16 * dp_size) == 0
            and query_weight.shape[1] == 12 * HD
            and query_weight.shape[1] == width
            and gate_weight.shape[1] == 4 * width
            and length % 1024 == 0
        )
        program = functools.partial(layer_per_device, dp_size) if fits else per_device
        return jax.shard_map(
            program, mesh=mesh, in_specs=in_specs, out_specs=out_specs, check_vma=False
        )(*arrays)

    return whole
```
